32 devices in a mesh: groups: 2 (over x), seq: 16 (over z, y, core).
Axes of the slice: x: 2, y: 2, z: 4, core: 2. Of those that a mesh axis runs over, the one named last changes fastest.
Arguments:
- span_keys: bfloat16 [32768, 512], P(('groups', 'seq')), parts along dimension 0, may hold values from -6 to 6
- span_values: bfloat16 [32768, 512], P(('groups', 'seq')), parts along dimension 0, may hold values from -6 to 6
- block_device: int32 [4096, 1], P(('groups', 'seq')), parts along dimension 0, may hold values from 0 to 15; in each aligned block of 128 rows (0 to 127, 128 to 255, ...) at most 16 rows name the same one
- block_row: int32 [4096], P(('groups', 'seq')), parts along dimension 0, may hold values from 0 to 7
- cache_len: int32 [256], P(('groups', 'seq')), parts along dimension 0, may hold values from 1 to 512, 16384 in all
- cache_keys: bfloat16 [256, 512, 512], P(('groups', 'seq')), parts along dimension 0, may hold values from -6 to 6
- cache_values: bfloat16 [256, 512, 512], P(('groups', 'seq')), parts along dimension 0, may hold values from -6 to 6
- queries: bfloat16 [256, 4, 8192], P(('groups', 'seq')), parts along dimension 0, may hold values from -250 to 250, as said below
- step_keys: bfloat16 [256, 4, 512], P(('groups', 'seq')), parts along dimension 0, may hold values from -6 to 6
- step_values: bfloat16 [256, 4, 512], P(('groups', 'seq')), parts along dimension 0, may hold values from -6 to 6
Outputs:
- attended: bfloat16 [256, 4, 8192], P(('groups', 'seq')), parts along dimension 0
The draws below stay inside these ranges and needn't reach their ends.
There are 2 independent parts, one for each index of `groups`. The reference program is written for one: setup_inputs(seed, part) draws one part's arguments, and reference() takes and returns one part's arrays. A program takes and returns all parts, laid end to end along the dimension named above; each array names one. Nothing has to cross between parts.
Inputs may be any that keep to these rules, and one draw needn't show every extreme that they name: Float queries of order one; a few heads may be much larger. `cache_len`: the lengths of each part along groups sum to 16384.
All inputs are finite; a program needn't handle non-finite values.
Results may differ from the reference program's by a relative error of at most 0.012.
The reference program's roundings to bfloat16 on the way (of `turned` and `weights`) count: a program that leaves them out, or rounds other values in their place, can miss the bound.
Values may be sent and summed in bfloat16 or wider, within the bound.
No kernel may reach another device: no remote copies, remote signals or barrier semaphores. Data moves between devices by JAX's collectives and lax.ppermute only.
A program may use at most 128 MiB of HBM per device.

```python
import math
import jax
import jax.numpy as jnp
import numpy as np
from jax import lax

KVH = 4
QH = 64
HD = 128
STEPS = 4
BLK = 8
ROWS_DEV = 8
CACHE = 512
BPD = 128
CAP = 16
ROWS = 128
NBLK = 2048
N_SEQ = 16


def draw_queries(key, part):
    out_shape = (ROWS, STEPS, QH * HD)
    first_key = jax.random.fold_in(key, 0)
    return jnp.clip(jax.random.normal(first_key, out_shape, jnp.float32), -6.0, 6.0).astype(jnp.bfloat16)


def with_ends(values, key, low, largest):
    longest = values.shape.index(max(values.shape))
    spots = []
    for shift in (0, 1):
        where = [jax.random.randint(jax.random.fold_in(key, axis), (), 0, length) for axis, length in enumerate(values.shape)]
        where[longest] = (where[longest] + shift) % values.shape[longest]
        spots.append(tuple(where))
    return values.at[spots[0]].set(low).at[spots[1]].set(largest)


def block_scale(stream_key, extent, pieces, least, top_value):
    level = 1.0
    for dim, shards_of in pieces:
        steps = jax.random.uniform(jax.random.fold_in(jax.random.fold_in(stream_key, 6), dim), (shards_of,), jnp.float32, least / len(pieces), top_value / len(pieces))
        level = level * jnp.repeat(jnp.exp(steps), extent[dim] // shards_of).reshape((-1,) + (1,) * (len(extent) - 1 - dim))
    return level


def profile(count, total, reach, slope):
    portions = [(1 << 20) // math.isqrt(grade ** slope) + 1 for grade in range(2, count + 1)]
    rest, given = total - reach - (count - 1), [1] * (count - 1)
    while rest > 0:
        candidates = [i for i in range(count - 1) if given[i] < reach]
        mass, budget = sum([portions[i] for i in candidates]), rest
        for i in candidates:
            addition = min(reach - given[i], max(1, budget * portions[i] // mass), rest)
            given[i] = given[i] + addition
            rest = rest - addition
    return np.array([reach] + given)


def uneven(stream_key, amount, total, most, lean):
    if amount == 2:
        one = jax.random.randint(stream_key, (), max(1, total - most), min(most, total - 1) + 1)
        return jnp.stack([one, total - one])
    lengths = jnp.asarray(profile(amount, total, most, lean), jnp.int32)
    pairs = (amount - 1) // 2
    giver, receiver = lengths[1:1 + 2 * pairs:2], lengths[2:2 + 2 * pairs:2]
    slack = jnp.minimum(giver - 1, most - receiver)
    passed = jax.random.randint(jax.random.fold_in(stream_key, 1), (pairs,), 0, 1 << 20) % (slack + 1)
    lengths = lengths.at[1:1 + 2 * pairs:2].set(giver - passed).at[2:2 + 2 * pairs:2].set(receiver + passed)
    return lengths[jax.random.permutation(jax.random.fold_in(stream_key, 2), amount)]


def deal_out(rng, own, number, rows, count, top, most, lean):
    order = jax.random.permutation(rng, count)
    heavy_load, ordinary = portions_of(count, rows * top, most, lean, True), portions_of(count, rows * top, most, lean, False)
    places = jnp.arange(count)

    def named(lengths, rotation):
        used = int((lengths > 0).sum())
        fixed = max(1, used // 4)
        moved = fixed + (places - fixed + rotation * (used - fixed)) % max(1, count - fixed)
        return jnp.zeros((count,), jnp.int32).at[order[jnp.where(places < fixed, places, moved)]].set(jnp.asarray(lengths, jnp.int32))

    lengths = jnp.where(number % 4 == 0, named(heavy_load, number // 4), named(ordinary, number - number // 4 - 1))
    mixed = jax.random.permutation(jax.random.fold_in(own, 3), count)
    source_of, taker = mixed[0:count // 2 * 2:2], mixed[1:count // 2 * 2:2]
    slack = jnp.minimum(lengths[source_of] - 1, most - lengths[taker]) // 2
    slack = jnp.where((source_of == order[0]) | (taker == order[0]) | (lengths[taker] == 0), 0, jnp.maximum(slack, 0))
    moved = jax.random.randint(jax.random.fold_in(own, 4), (count // 2,), 0, 1 << 20) % (slack + 1)
    lengths = lengths.at[source_of].add(-moved).at[taker].add(moved)
    labels = jnp.searchsorted(jnp.cumsum(lengths), jnp.arange(rows * top), side="right").astype(jnp.int32)
    listing = labels.reshape(top, rows).T
    listing = listing[jax.random.permutation(jax.random.fold_in(own, 1), rows)]
    rotation = jax.random.randint(jax.random.fold_in(own, 2), (rows, 1), 0, top)
    return jnp.take_along_axis(listing, (jnp.arange(top)[None, :] + rotation) % top, axis=1)


def portions_of(count, total, reach, skew, full):
    loads = [(1 << 20) // math.isqrt(rank ** skew) + 1 for rank in range(1, count + 1)]
    largest = reach if full else min(reach, max(-(-total // count), total * loads[0] // sum(loads)))
    least = 1 if total - largest >= count - 1 else 0
    holding, surplus = [largest] + [least] * (count - 1), total - largest - least * (count - 1)
    while surplus > 0:
        free = [i for i in range(1, count) if holding[i] < largest] or [i for i in range(1, count) if holding[i] < reach]
        pool, budget = sum([loads[i] for i in free]), surplus
        for i in free:
            addition = min(reach - holding[i], max(1, budget * loads[i] // pool), surplus)
            holding[i] = holding[i] + addition
            surplus = surplus - addition
    return np.array(holding)


def scatter_about(stream_key, extent, deviation, bound, cuts=(), kind=jnp.bfloat16):
    result = deviation * jax.random.normal(stream_key, extent, jnp.float32)
    if cuts:
        result = result * block_scale(stream_key, extent, cuts, -0.22, 0.18)
    return jnp.clip(result, -bound, bound).astype(kind)


def setup_inputs(seed: int = 0, part: int = 0) -> dict:
    key_of = jax.random.split(jax.random.key(seed), 11)
    part_splits = jax.random.split(jax.random.fold_in(key_of[10], part), 11)
    span_keys = scatter_about(part_splits[0], (NBLK * BLK, KVH * HD), 1.0, 6.0, ((0, 16),))
    span_values = scatter_about(part_splits[1], (NBLK * BLK, KVH * HD), 1.0, 6.0, ((0, 16),))
    block_device_keys = jax.random.split(jax.random.fold_in(part_splits[2], 1), NBLK // BPD)
    block_device_turns = jax.random.permutation(jax.random.fold_in(part_splits[2], 3), NBLK // BPD)
    block_device = jax.vmap(lambda own, number: deal_out(jax.random.fold_in(part_splits[2], 2), own, number, BPD, N_SEQ, 1, CAP, 2))(block_device_keys, block_device_turns).reshape((NBLK, 1))
    block_row = with_ends(jax.random.randint(part_splits[3], (NBLK,), 0, ROWS_DEV), jax.random.fold_in(part_splits[3], 1), 0, ROWS_DEV - 1).astype(jnp.int32)
    cache_len = uneven(part_splits[4], ROWS, ROWS * CACHE // 4, CACHE, 2).astype(jnp.int32)
    cache_keys = scatter_about(part_splits[5], (ROWS, CACHE, KVH * HD), 1.0, 6.0, ((0, 16),))
    cache_values = scatter_about(part_splits[6], (ROWS, CACHE, KVH * HD), 1.0, 6.0, ((0, 16),))
    queries = draw_queries(jax.random.fold_in(jax.random.fold_in(key_of[10], part), 71), part)
    step_keys = scatter_about(part_splits[8], (ROWS, STEPS, KVH * HD), 1.0, 6.0, ((0, 16),))
    step_values = scatter_about(part_splits[9], (ROWS, STEPS, KVH * HD), 1.0, 6.0, ((0, 16),))
    return dict(span_keys=span_keys, span_values=span_values, block_device=block_device, block_row=block_row, cache_len=cache_len, cache_keys=cache_keys, cache_values=cache_values, queries=queries, step_keys=step_keys, step_values=step_values)


def frequencies(half_width):
    freq_index = jnp.arange(half_width, dtype=jnp.float32)
    base_freq = 1.0 / (500000.0 ** (freq_index / half_width))
    wavelen = 2.0 * jnp.pi / base_freq
    smooth = (8192.0 / wavelen - 1.0) / 3.0
    blended = (1.0 - smooth) * base_freq / 8.0 + smooth * base_freq
    scaled = jnp.where(wavelen > 8192.0, base_freq / 8.0, blended)
    return jnp.where(wavelen < 2048.0, base_freq, scaled)


def rotate(key_rows, positions, head_count):
    token_count = key_rows.shape[0]
    head_width = key_rows.shape[1] // head_count
    half_width = head_width // 2
    angles = positions.astype(jnp.float32)[:, None] * frequencies(half_width)[None, :]
    cosine = jnp.cos(angles)[:, None, :]
    sine_table = jnp.sin(angles)[:, None, :]
    split_keys = key_rows.astype(jnp.float32).reshape(token_count, head_count, head_width)
    first_half = split_keys[..., :half_width]
    second_half = split_keys[..., half_width:]
    turned = jnp.concatenate([first_half * cosine - second_half * sine_table, second_half * cosine + first_half * sine_table], axis=-1)
    return turned.reshape(token_count, head_count * head_width).astype(jnp.bfloat16)


def reference(span_keys, span_values, block_device, block_row, cache_len, cache_keys, cache_values, queries, step_keys, step_values):
    feature_width = KVH * HD
    group_size = QH // KVH
    window = N_SEQ * CAP
    score_scale = HD ** -0.5
    dest_device = block_device[:, 0]
    target_row = dest_device * ROWS_DEV + block_row
    row_hits = (target_row[:, None] == jnp.arange(ROWS, dtype=jnp.int32)[None, :]).astype(jnp.int32)
    block_rank = jnp.sum((jnp.cumsum(row_hits, axis=0) - row_hits) * row_hits, axis=1)
    cache_base = cache_len[target_row]
    positions = ((cache_base + block_rank * BLK)[:, None] + jnp.arange(BLK, dtype=jnp.int32)[None, :]).reshape(-1)
    turned = rotate(span_keys, positions, KVH).reshape(NBLK, BLK, feature_width)
    shaped_values = span_values.reshape(NBLK, BLK, feature_width)
    sort_order = jnp.argsort(dest_device, stable=True)
    per_device = jnp.sum((dest_device[:, None] == jnp.arange(N_SEQ, dtype=jnp.int32)[None, :]).astype(jnp.int32), axis=0)
    starts = (jnp.cumsum(per_device) - per_device).astype(jnp.int32)
    padded_keys = jnp.concatenate([turned[sort_order], jnp.zeros((window, BLK, feature_width), jnp.bfloat16)], axis=0)
    padded_values = jnp.concatenate([shaped_values[sort_order], jnp.zeros((window, BLK, feature_width), jnp.bfloat16)], axis=0)
    padded_dest = jnp.concatenate([dest_device[sort_order], jnp.full((window,), -1, jnp.int32)], axis=0)
    padded_row = jnp.concatenate([block_row[sort_order], jnp.full((window,), -1, jnp.int32)], axis=0)

    def one_device(device_index):
        first_row = (device_index * ROWS_DEV).astype(jnp.int32)
        row_queries = lax.dynamic_slice_in_dim(queries, first_row, ROWS_DEV, 0).astype(jnp.float32).reshape(ROWS_DEV, STEPS, KVH, group_size, HD)
        cached_keys = lax.dynamic_slice_in_dim(cache_keys, first_row, ROWS_DEV, 0).astype(jnp.float32).reshape(ROWS_DEV, CACHE, KVH, HD)
        cached_values = lax.dynamic_slice_in_dim(cache_values, first_row, ROWS_DEV, 0).astype(jnp.float32).reshape(ROWS_DEV, CACHE, KVH, HD)
        own_keys = lax.dynamic_slice_in_dim(step_keys, first_row, ROWS_DEV, 0).astype(jnp.float32).reshape(ROWS_DEV, STEPS, KVH, HD)
        own_values = lax.dynamic_slice_in_dim(step_values, first_row, ROWS_DEV, 0).astype(jnp.float32).reshape(ROWS_DEV, STEPS, KVH, HD)
        live_len = lax.dynamic_slice_in_dim(cache_len, first_row, ROWS_DEV, 0)
        window_start = starts[device_index]
        window_keys = lax.dynamic_slice_in_dim(padded_keys, window_start, window, 0).astype(jnp.float32).reshape(window * BLK, KVH, HD)
        window_values = lax.dynamic_slice_in_dim(padded_values, window_start, window, 0).astype(jnp.float32).reshape(window * BLK, KVH, HD)
        window_dest = lax.dynamic_slice_in_dim(padded_dest, window_start, window, 0)
        window_row = jnp.where(window_dest == device_index, lax.dynamic_slice_in_dim(padded_row, window_start, window, 0), -1)
        token_row = jnp.repeat(window_row, BLK)
        cache_scores = jnp.einsum("rsngd,rlnd->rsngl", row_queries, cached_keys) * score_scale
        span_scores = jnp.einsum("rsngd,tnd->rsngt", row_queries, window_keys) * score_scale
        step_scores = jnp.einsum("rsngd,rund->rsngu", row_queries, own_keys) * score_scale
        cache_mask = jnp.broadcast_to((jnp.arange(CACHE, dtype=jnp.int32)[None, :] < live_len[:, None])[:, None, None, None, :], cache_scores.shape)
        span_mask = jnp.broadcast_to((token_row[None, :] == jnp.arange(ROWS_DEV, dtype=jnp.int32)[:, None])[:, None, None, None, :], span_scores.shape)
        step_mask = jnp.broadcast_to((jnp.arange(STEPS)[None, :] <= jnp.arange(STEPS)[:, None])[None, :, None, None, :], step_scores.shape)
        scores = jnp.concatenate([cache_scores, span_scores, step_scores], axis=-1)
        allowed = jnp.concatenate([cache_mask, span_mask, step_mask], axis=-1)
        row_max = jnp.max(jnp.where(allowed, scores, -1e30), axis=-1, keepdims=True)
        raw_weights = jnp.where(allowed, jnp.exp(scores - row_max), 0.0)
        denominator = jnp.sum(raw_weights, axis=-1)
        weights = lax.optimization_barrier(raw_weights.astype(jnp.bfloat16)).astype(jnp.float32)
        split_at = CACHE + window * BLK
        numerator = jnp.einsum("rsngl,rlnd->rsngd", weights[..., :CACHE], cached_values)
        numerator = numerator + jnp.einsum("rsngt,tnd->rsngd", weights[..., CACHE:split_at], window_values)
        numerator = numerator + jnp.einsum("rsngu,rund->rsngd", weights[..., split_at:], own_values)
        attended_rows = numerator / denominator[..., None]
        return attended_rows.astype(jnp.bfloat16).reshape(ROWS_DEV, STEPS, QH * HD)

    stacked = lax.map(one_device, jnp.arange(N_SEQ, dtype=jnp.int32))
    return stacked.reshape(ROWS, STEPS, QH * HD)
```

```python
import functools

import jax
import jax.numpy as jnp
from jax import lax
from jax.experimental import pallas as pl
from jax.experimental.pallas import tpu as pltpu
from jax.sharding import PartitionSpec as P

KVH = 4
QH = 64
HD = 128
BLK = 8
PLANES = 4
CHUNK = 256
NEG = -1e30


def frequencies(half_width):
    freq_index = jnp.arange(half_width, dtype=jnp.float32)
    base_freq = 1.0 / 500000.0 ** (freq_index / half_width)
    wavelen = 2.0 * jnp.pi / base_freq
    smooth = (8192.0 / wavelen - 1.0) / 3.0
    blended = (1.0 - smooth) * base_freq / 8.0 + smooth * base_freq
    scaled = jnp.where(wavelen > 8192.0, base_freq / 8.0, blended)
    return jnp.where(wavelen < 2048.0, base_freq, scaled)


def turn_tables(positions):
    freq = frequencies(HD // 2)
    angles = positions.astype(jnp.float32)[..., None] * jnp.concatenate([freq, freq])
    sign = jnp.where(jnp.arange(HD) < HD // 2, -1.0, 1.0).astype(jnp.float32)
    return jnp.cos(angles), jnp.sin(angles) * sign


def pack_kernel(n, cap, target, rows, rel, keys, values, *refs):
    meta = refs[0]
    outs = refs[1 : 1 + n]
    slots, fill, sems = refs[1 + n :]
    blocks = keys.shape[0]

    def clear(i, _):
        fill[i] = 0
        for k in range(cap):
            meta[i * cap + k] = -1
        return 0

    lax.fori_loop(0, n, clear, 0)

    def put(b, _):
        dest = target[b]
        slot = fill[dest]
        fill[dest] = slot + 1
        meta[dest * cap + slot] = rows[b]
        message = rel[dest]
        slots[message, 0, slot] = keys[b]
        slots[message, 1, slot] = values[b]
        return 0

    lax.fori_loop(0, blocks, put, 0, unroll=2)
    copies = [pltpu.make_async_copy(slots.at[i], outs[i], sems.at[i]) for i in range(n)]
    for copy in copies:
        copy.start()
    for copy in copies:
        copy.wait()


def pack(n, cap, target, rows, rel, keys, values):
    width = keys.shape[-1]
    message = jax.ShapeDtypeStruct((2, cap, BLK, width), jnp.bfloat16)
    smem = pl.BlockSpec(memory_space=pltpu.SMEM)
    vmem = pl.BlockSpec(memory_space=pltpu.VMEM)
    return pl.pallas_call(
        functools.partial(pack_kernel, n, cap),
        out_shape=(jax.ShapeDtypeStruct((n * cap,), jnp.int32),) + (message,) * n,
        in_specs=[smem, smem, smem, vmem, vmem],
        out_specs=(smem,) + (pl.BlockSpec(memory_space=pl.ANY),) * n,
        scratch_shapes=[
            pltpu.VMEM((n, 2, cap, BLK, width), jnp.bfloat16),
            pltpu.SMEM((n,), jnp.int32),
            pltpu.SemaphoreType.DMA((n,)),
        ],
        name="pack",
    )(target, rows, rel, keys, values)


def absorb(row, q_ref, keys_at, values_at, allowed, acc, top, total):
    scale = HD ** (-0.5)
    for head in range(KVH):
        scores = (
            lax.dot_general(
                q_ref[row, head],
                keys_at(head),
                (((1,), (1,)), ((), ())),
                preferred_element_type=jnp.float32,
            )
            * scale
        )
        ok = allowed(scores.shape)
        scores = jnp.where(ok, scores, NEG)
        old_top = top[row, head]
        new_top = jnp.maximum(old_top, jnp.max(scores, axis=-1, keepdims=True))
        raw = jnp.where(ok, jnp.exp(scores - new_top[:, :1]), 0.0)
        factor = jnp.exp(old_top - new_top)
        total[row, head] = total[row, head] * factor + jnp.sum(raw, axis=-1, keepdims=True)
        acc[row, head] = acc[row, head] * factor + jnp.dot(
            raw.astype(jnp.bfloat16), values_at(head), preferred_element_type=jnp.float32
        )
        top[row, head] = new_top


def resident_kernel(
    lens, q_ref, step_k, step_v, keys, values, acc, top, total, kbuf, vbuf, sems
):
    rows, slot_count = kbuf.shape[0], kbuf.shape[1]
    piece = min(CHUNK, slot_count)
    pieces = slot_count // piece
    steps = step_k.shape[1]

    def copies(r, i):
        span = pl.ds(i * piece, piece)
        return (
            pltpu.make_async_copy(keys.at[r, span], kbuf.at[r, span], sems.at[0, r, i]),
            pltpu.make_async_copy(values.at[r, span], vbuf.at[r, span], sems.at[1, r, i]),
        )

    def fetch(r, _):
        for i in range(pieces):

            @pl.when(i * piece < lens[r])
            def _():
                for copy in copies(r, i):
                    copy.start()

        return 0

    lax.fori_loop(0, rows, fetch, 0)
    group = q_ref.shape[2] // steps

    def one_row(r, _):
        acc[r] = jnp.zeros_like(acc[r])
        top[r] = jnp.full_like(top[r], NEG)
        total[r] = jnp.zeros_like(total[r])

        def columns(head):
            return pl.ds(head * HD, HD)

        def causal(shape):
            step = lax.broadcasted_iota(jnp.int32, shape, 0) // group
            return lax.broadcasted_iota(jnp.int32, shape, 1) <= step

        absorb(
            r,
            q_ref,
            lambda head: step_k[r, :, columns(head)],
            lambda head: step_v[r, :, columns(head)],
            causal,
            acc,
            top,
            total,
        )
        for i in range(pieces):

            @pl.when(i * piece < lens[r])
            def _():
                for copy in copies(r, i):
                    copy.wait()
                span = pl.ds(i * piece, piece)
                absorb(
                    r,
                    q_ref,
                    lambda head: kbuf[r, span, columns(head)],
                    lambda head: vbuf[r, span, columns(head)],
                    lambda shape: lax.broadcasted_iota(jnp.int32, shape, 1) + i * piece < lens[r],
                    acc,
                    top,
                    total,
                )

        return 0

    lax.fori_loop(0, rows, one_row, 0)


def state_shapes(rows, width):
    shape = jax.ShapeDtypeStruct((rows, KVH, width, HD), jnp.float32)
    return (shape,) * 3


def resident(lens, grouped, step_k, step_v, keys, values):
    rows, slot_count, feature = keys.shape
    pieces = slot_count // min(CHUNK, slot_count)
    vmem = pl.BlockSpec(memory_space=pltpu.VMEM)
    hbm = pl.BlockSpec(memory_space=pl.ANY)
    return pl.pallas_call(
        resident_kernel,
        out_shape=state_shapes(rows, grouped.shape[2]),
        in_specs=[pl.BlockSpec(memory_space=pltpu.SMEM), vmem, vmem, vmem, hbm, hbm],
        out_specs=(vmem,) * 3,
        scratch_shapes=[
            pltpu.VMEM((rows, slot_count, feature), jnp.bfloat16),
            pltpu.VMEM((rows, slot_count, feature), jnp.bfloat16),
            pltpu.SemaphoreType.DMA((2, rows, pieces)),
        ],
        cost_estimate=pl.CostEstimate(
            flops=2 * 10**9, bytes_accessed=16 * 2**20, transcendentals=10**6
        ),
        name="resident",
    )(lens, grouped, step_k, step_v, keys, values)


def span_kernel(kind, count, cap, base, counts, rows_of, ranks, q_ref, ca, sa, cb, sb, *refs):
    messages = refs[:count]
    refs = refs[count:]
    if kind == "partial":
        out, stats, acc, top, total, kbuf, vbuf, fill, start = refs
    elif kind == "state":
        acc0, top0, total0, acc, top, total, kbuf, vbuf, fill, start = refs
    else:
        acc0, top0, total0, part, stats, out, acc, top, total, scr, kbuf, vbuf, fill, start = refs
    rows = q_ref.shape[0]
    feature = kbuf.shape[1]
    if kind == "partial":
        acc[...] = jnp.zeros_like(acc)
        top[...] = jnp.full_like(top, NEG)
        total[...] = jnp.zeros_like(total)
    else:
        acc[...] = acc0[...]
        top[...] = top0[...]
        total[...] = total0[...]
    for r in range(rows):
        fill[r] = 0
    for j in range(count):
        first = base[j]

        def tally(k, _):
            r = rows_of[first + k]
            fill[r] = fill[r] + 1
            return 0

        lax.fori_loop(0, counts[j], tally, 0)
    at = 0
    for r in range(rows):
        start[r] = at
        at = at + fill[r]
        fill[r] = start[r]
    tail = pl.ds(pl.multiple_of(at * BLK, BLK), CHUNK)
    vbuf[tail, :] = jnp.zeros((CHUNK, feature), jnp.float32)
    for j in range(count):
        first = base[j]
        message = messages[j]

        def place(k, _):
            r = rows_of[first + k]
            slot = fill[r]
            fill[r] = slot + 1
            rank = ranks[first + k]
            c_a, s_a = ca[r], sa[r]
            c_b, s_b = cb[pl.ds(rank, 1), :], sb[pl.ds(rank, 1), :]
            cosine = c_a * c_b - s_a * s_b
            sine = s_a * c_b + c_a * s_b
            where = pl.ds(pl.multiple_of(slot * BLK, BLK), BLK)
            vbuf[where, :] = message[1, k].astype(jnp.float32)
            for head in range(KVH):
                part_k = message[0, k, :, head * HD : (head + 1) * HD].astype(jnp.float32)
                kbuf[where, head * HD : (head + 1) * HD] = (
                    part_k * cosine + pltpu.roll(part_k, HD // 2, 1) * sine
                )
            return 0

        lax.fori_loop(0, counts[j], place, 0)

    def one_row(r, _):
        tokens = (fill[r] - start[r]) * BLK
        origin = start[r] * BLK

        def piece(i, _):
            where = pl.ds(pl.multiple_of(origin + i * CHUNK, BLK), CHUNK)
            absorb(
                r,
                q_ref,
                lambda head: kbuf[where, head * HD : (head + 1) * HD].astype(jnp.bfloat16),
                lambda head: vbuf[where, head * HD : (head + 1) * HD].astype(jnp.bfloat16),
                lambda shape: lax.broadcasted_iota(jnp.int32, shape, 1) + i * CHUNK < tokens,
                acc,
                top,
                total,
            )
            return 0

        lax.fori_loop(0, (tokens + CHUNK - 1) // CHUNK, piece, 0)
        width = q_ref.shape[2]
        eye = lax.broadcasted_iota(jnp.int32, (width, width), 0) == lax.broadcasted_iota(
            jnp.int32, (width, width), 1
        )
        if kind == "partial":
            for head in range(KVH):
                held = total[r, head]
                safe = jnp.where(held > 0.0, held, 1.0)
                out[r, head] = (acc[r, head] / safe).astype(jnp.bfloat16)
                for i, column in enumerate((top, total)):
                    line = jnp.where(eye, column[r, head][:, :width], 0.0)
                    stats[r, head, pl.ds(i, 1), :] = jnp.sum(line, axis=0, keepdims=True)
        if kind == "final":
            steps = out.shape[1]
            group = width // steps
            for head in range(KVH):
                lines = []
                for i in range(2):
                    line = jnp.broadcast_to(stats[r, head, pl.ds(i, 1), :], (width, width))
                    lines.append(jnp.sum(jnp.where(eye, line, 0.0), axis=1, keepdims=True))
                other_top, other_total = lines
                other_top = jnp.where(other_total > 0.0, other_top, NEG)
                old_top = top[r, head]
                new_top = jnp.maximum(old_top, other_top)
                mine = jnp.exp(old_top - new_top)
                theirs = jnp.exp(other_top - new_top) * other_total
                whole = total[r, head] * mine + theirs
                merged = acc[r, head] * mine + part[r, head].astype(jnp.float32) * theirs
                scr[head] = merged / whole
            for head in range(KVH):
                for g in range(group):
                    column = (head * group + g) * HD
                    out[r, :, column : column + HD] = scr[
                        head, pl.ds(g, steps, stride=group), :
                    ].astype(jnp.bfloat16)
        return 0

    lax.fori_loop(0, rows, one_row, 0)


def span(kind, cap, base, counts, rows_of, ranks, grouped, tables, messages, extra, steps):
    rows, _, width, _ = grouped.shape
    feature = messages[0].shape[-1]
    count = len(messages)
    room = (count * cap) * BLK + CHUNK
    smem = pl.BlockSpec(memory_space=pltpu.SMEM)
    vmem = pl.BlockSpec(memory_space=pltpu.VMEM)
    state = [pltpu.VMEM((rows, KVH, width, HD), jnp.float32)] * 3
    scratch = []
    if kind == "partial":
        out_shape = (
            jax.ShapeDtypeStruct((rows, KVH, width, HD), jnp.bfloat16),
            jax.ShapeDtypeStruct((rows, KVH, 2, width), jnp.float32),
        )
        scratch += state
    elif kind == "state":
        out_shape = state_shapes(rows, width)
    else:
        out_shape = jax.ShapeDtypeStruct((rows, steps, QH * HD), jnp.bfloat16)
        scratch += state + [pltpu.VMEM((KVH, width, HD), jnp.float32)]
    scratch += [
        pltpu.VMEM((room, feature), jnp.float32),
        pltpu.VMEM((room, feature), jnp.float32),
        pltpu.SMEM((rows,), jnp.int32),
        pltpu.SMEM((rows,), jnp.int32),
    ]
    return pl.pallas_call(
        functools.partial(span_kernel, kind, count, cap),
        out_shape=out_shape,
        in_specs=[smem] * 4 + [vmem] * (5 + count + len(extra)),
        out_specs=jax.tree.map(lambda _: vmem, out_shape),
        scratch_shapes=scratch,
        cost_estimate=pl.CostEstimate(
            flops=10**9, bytes_accessed=12 * 2**20, transcendentals=10**6
        ),
        name="span_" + kind,
    )(base, counts, rows_of, ranks, grouped, *tables, *messages, *extra)


def site_plane(plane, flip):
    dest = plane ^ flip
    half = PLANES // 2
    inner = (half - 1, half)
    if (plane < half) != (dest < half) and dest in inner:
        return PLANES - 1 - dest
    return dest


def route(n, flip, offset):
    in_plane = n // PLANES
    return [
        (
            plane * in_plane + place,
            site_plane(plane, flip) * in_plane + (place + offset) % in_plane,
        )
        for plane in range(PLANES)
        for place in range(in_plane)
    ]


def body(
    span_keys,
    span_values,
    block_device,
    block_row,
    cache_len,
    cache_keys,
    cache_values,
    queries,
    step_keys,
    step_values,
):
    n = lax.axis_size("seq")
    in_plane = n // PLANES
    me = lax.axis_index("seq").astype(jnp.int32)
    plane, place = me // in_plane, me % in_plane
    rows = cache_len.shape[0]
    feature = span_keys.shape[1]
    blocks = span_keys.shape[0] // BLK
    cap = max(2, (2 * blocks + n - 1) // n)
    steps = queries.shape[1]
    group = QH // KVH
    seq = jnp.arange(n, dtype=jnp.int32)

    rel = ((seq // in_plane) ^ plane) * in_plane + (seq % in_plane - place) % in_plane
    meta, *messages = pack(
        n,
        cap,
        block_device[:, 0],
        block_row,
        rel,
        span_keys.reshape(blocks, BLK, feature),
        span_values.reshape(blocks, BLK, feature),
    )

    grouped = (
        queries.reshape(rows, steps, KVH, group, HD)
        .transpose(0, 2, 1, 3, 4)
        .reshape(rows, KVH, steps * group, HD)
    )
    half = PLANES // 2
    swap = [
        (a * in_plane + i, b * in_plane + i)
        for a, b in ((half - 1, half), (half, half - 1))
        for i in range(in_plane)
    ]
    mirrored = lax.ppermute(grouped, "seq", swap)

    def send(flip, offset, value):
        pairs = route(n, flip, offset)
        if all(a == b for a, b in pairs):
            return value
        return lax.ppermute(value, "seq", pairs)

    def sent(flip, values):
        return [send(flip, o, values[o]) for o in range(in_plane)]

    packed = [messages[f * in_plane : (f + 1) * in_plane] for f in range(PLANES)]
    got = [None] * PLANES
    got[2] = sent(2, packed[2])
    got[3] = sent(3, packed[3])
    got[0] = sent(0, packed[0])

    table = meta.reshape(PLANES, in_plane, cap)
    table_mirror = jnp.concatenate(
        [table[p if p in (0, PLANES - 1) else PLANES - 1 - p][None] for p in range(PLANES)]
    )
    notes = jnp.concatenate(
        [
            table.reshape(n, cap),
            table_mirror.reshape(n, cap),
            jnp.broadcast_to(cache_len[None], (n, rows)),
        ],
        axis=1,
    )
    notes = lax.all_to_all(notes, "seq", split_axis=0, concat_axis=0, tiled=True)
    own_rows = notes[:, :cap].reshape(-1)
    mirror_rows = notes[:, cap : 2 * cap].reshape(-1)
    mirror_me = (PLANES - 1 - plane) * in_plane + place
    mirror_len = jnp.sum(jnp.where((seq == mirror_me)[:, None], notes[:, 2 * cap :], 0), axis=0)
    row_ids = jnp.arange(rows, dtype=jnp.int32)
    hits = jnp.concatenate(
        [own_rows[:, None] == row_ids[None], mirror_rows[:, None] == row_ids[None]], axis=1
    )
    order = jnp.arange(n * cap, dtype=jnp.int32)
    earlier = jnp.dot(
        (order[:, None] > order[None, :]).astype(jnp.bfloat16),
        hits.astype(jnp.bfloat16),
        preferred_element_type=jnp.float32,
    )
    earlier = jnp.where(hits, earlier, 0.0).astype(jnp.int32)
    ranks = jnp.concatenate(
        [jnp.sum(earlier[:, :rows], axis=1), jnp.sum(earlier[:, rows:], axis=1)]
    )
    rows_of = jnp.concatenate([own_rows, mirror_rows])
    filled = jnp.concatenate(
        [
            jnp.sum((notes[:, :cap] >= 0).astype(jnp.int32), axis=1),
            jnp.sum((notes[:, cap : 2 * cap] >= 0).astype(jnp.int32), axis=1),
        ]
    )
    own_tables = turn_tables(cache_len[:, None] + jnp.arange(BLK, dtype=jnp.int32)[None])
    mirror_tables = turn_tables(mirror_len[:, None] + jnp.arange(BLK, dtype=jnp.int32)[None])
    rank_tables = turn_tables(order * BLK)

    from_plane = jnp.array(
        [
            [
                next(s for s in range(PLANES) if site_plane(s, f) == p)
                for p in range(PLANES)
            ]
            for f in range(PLANES)
        ],
        jnp.int32,
    )
    for_mirror = jnp.array(
        [
            [
                int(next(s for s in range(PLANES) if site_plane(s, f) == p) ^ f != p)
                for p in range(PLANES)
            ]
            for f in range(PLANES)
        ],
        jnp.int32,
    )
    at_plane = (jnp.arange(PLANES, dtype=jnp.int32) == plane).astype(jnp.int32)
    came = jnp.sum(from_plane * at_plane[None], axis=1)
    other = jnp.sum(for_mirror * at_plane[None], axis=1)
    offsets = jnp.arange(in_plane, dtype=jnp.int32)
    source = came[:, None] * in_plane + (place - offsets[None]) % in_plane
    entry = (other[:, None] * n + source).reshape(-1)
    base = entry * cap
    number = jnp.sum(
        jnp.where(entry[:, None] == jnp.arange(2 * n, dtype=jnp.int32)[None], filled[None], 0),
        axis=1,
    )
    is_mirror = jnp.repeat(other, in_plane)

    def part(flips, value):
        return jnp.concatenate([value[f * in_plane : (f + 1) * in_plane] for f in flips])

    state = resident(cache_len, grouped, step_keys, step_values, cache_keys, cache_values)

    gathered = lax.optimization_barrier((got[2], got[3], packed[1]))
    got[2], got[3], packed[1] = gathered
    got[1] = sent(1, packed[1])

    partial, stats = span(
        "partial",
        cap,
        part((2, 3), base),
        part((2, 3), number * is_mirror),
        rows_of,
        ranks,
        mirrored,
        mirror_tables + rank_tables,
        got[2] + got[3],
        (),
        steps,
    )
    partial = lax.ppermute(partial, "seq", swap)
    stats = lax.ppermute(stats, "seq", swap)
    state = span(
        "state",
        cap,
        part((2, 3, 0), base),
        part((2, 3, 0), number * (1 - is_mirror)),
        rows_of,
        ranks,
        grouped,
        own_tables + rank_tables,
        got[2] + got[3] + got[0],
        tuple(state),
        steps,
    )
    return span(
        "final",
        cap,
        part((1,), base),
        part((1,), number),
        rows_of,
        ranks,
        grouped,
        own_tables + rank_tables,
        got[1],
        tuple(state) + (partial, stats),
        steps,
    )


def solution(mesh):
    placed = (
        P(("groups", "seq"), None),
        P(("groups", "seq"), None),
        P(("groups", "seq"), None),
        P(("groups", "seq")),
        P(("groups", "seq")),
        P(("groups", "seq"), None, None),
        P(("groups", "seq"), None, None),
        P(("groups", "seq"), None, None),
        P(("groups", "seq"), None, None),
        P(("groups", "seq"), None, None),
    )
    return jax.shard_map(
        body,
        mesh=mesh,
        in_specs=placed,
        out_specs=P(("groups", "seq"), None, None),
        check_vma=False,
    )
```

```python
import functools

import jax
import jax.numpy as jnp
from jax import lax
from jax.experimental import pallas as pl
from jax.experimental.pallas import tpu as pltpu
from jax.sharding import PartitionSpec as P


KVH = 4
QH = 64
HD = 128
BLK = 8
PLANES = 4
CHUNK = 256
SPAN = 128
UNROLL = 4
NEG = -1e30


def frequencies(half_width):
    freq_index = jnp.arange(half_width, dtype=jnp.float32)
    base_freq = 1.0 / 500000.0 ** (freq_index / half_width)
    wavelen = 2.0 * jnp.pi / base_freq
    smooth = (8192.0 / wavelen - 1.0) / 3.0
    blended = (1.0 - smooth) * base_freq / 8.0 + smooth * base_freq
    scaled = jnp.where(wavelen > 8192.0, base_freq / 8.0, blended)
    return jnp.where(wavelen < 2048.0, base_freq, scaled)


def turn_tables(positions):
    freq = frequencies(HD // 2)
    angles = positions.astype(jnp.float32)[..., None] * jnp.concatenate([freq, freq])
    sign = jnp.where(jnp.arange(HD) < HD // 2, -1.0, 1.0).astype(jnp.float32)
    return jnp.cos(angles), jnp.sin(angles) * sign


def pack_kernel(n, cap, target, rows, rel, keys, values, *refs):
    meta = refs[0]
    outs = refs[1 : 1 + n]
    slots, fill, sems = refs[1 + n :]
    blocks = keys.shape[0]

    def clear(i, _):
        fill[i] = 0
        for k in range(cap):
            meta[i * cap + k] = -1
        return 0

    lax.fori_loop(0, n, clear, 0)

    def put(b, _):
        dest = target[b]
        slot = fill[dest]
        fill[dest] = slot + 1
        meta[dest * cap + slot] = rows[b]
        message = rel[dest]
        slots[message, 0, slot] = keys[b]
        slots[message, 1, slot] = values[b]
        return 0

    lax.fori_loop(0, blocks, put, 0, unroll=2)
    copies = [pltpu.make_async_copy(slots.at[i], outs[i], sems.at[i]) for i in range(n)]
    for copy in copies:
        copy.start()
    for copy in copies:
        copy.wait()


def pack(n, cap, target, rows, rel, keys, values):
    width = keys.shape[-1]
    message = jax.ShapeDtypeStruct((2, cap, BLK, width), jnp.bfloat16)
    smem = pl.BlockSpec(memory_space=pltpu.SMEM)
    vmem = pl.BlockSpec(memory_space=pltpu.VMEM)
    return pl.pallas_call(
        functools.partial(pack_kernel, n, cap),
        out_shape=(jax.ShapeDtypeStruct((n * cap,), jnp.int32),) + (message,) * n,
        in_specs=[smem, smem, smem, vmem, vmem],
        out_specs=(smem,) + (pl.BlockSpec(memory_space=pl.ANY),) * n,
        scratch_shapes=[
            pltpu.VMEM((n, 2, cap, BLK, width), jnp.bfloat16),
            pltpu.SMEM((n,), jnp.int32),
            pltpu.SemaphoreType.DMA((n,)),
        ],
        name="pack",
    )(target, rows, rel, keys, values)


def absorb(row, q_ref, pieces, state, fresh):
    acc, top, total = state
    scale = HD ** (-0.5)
    heads = range(KVH)
    queries = [q_ref[row, head] for head in heads]
    keys = [[piece[0](head) for piece in pieces] for head in heads]
    values = [[piece[1](head) for piece in pieces] for head in heads]
    if not fresh:
        old_acc = [acc[row, head] for head in heads]
        old_top = [top[row, head] for head in heads]
        old_total = [total[row, head] for head in heads]
    scores = [
        [
            jnp.where(
                piece[2],
                lax.dot_general(
                    queries[head], key, (((1,), (1,)), ((), ())), preferred_element_type=jnp.float32
                )
                * scale,
                NEG,
            )
            for piece, key in zip(pieces, keys[head])
        ]
        for head in heads
    ]
    new = []
    for head in heads:
        peak = functools.reduce(
            jnp.maximum, [jnp.max(one, axis=-1, keepdims=True) for one in scores[head]]
        )
        new_top = jnp.broadcast_to(peak, (peak.shape[0], HD)) if fresh else jnp.maximum(
            old_top[head], peak
        )
        raw = [jnp.exp(one - new_top[:, :1]) for one in scores[head]]
        added = sum(jnp.sum(one, axis=-1, keepdims=True) for one in raw)
        mixed = sum(
            jnp.dot(one.astype(jnp.bfloat16), value, preferred_element_type=jnp.float32)
            for one, value in zip(raw, values[head])
        )
        if fresh:
            new.append((mixed, new_top, jnp.broadcast_to(added, new_top.shape)))
        else:
            factor = jnp.exp(old_top[head] - new_top)
            new.append(
                (old_acc[head] * factor + mixed, new_top, old_total[head] * factor + added)
            )
    for head in heads:
        acc[row, head], top[row, head], total[row, head] = new[head]


def resident_kernel(
    lens, q_ref, step_k, step_v, keys, values, acc, top, total, kbuf, vbuf, sems
):
    rows, slot_count = kbuf.shape[0], kbuf.shape[1]
    piece = min(CHUNK, slot_count)
    pieces = slot_count // piece
    steps = step_k.shape[1]
    width = q_ref.shape[2]
    group = width // steps

    def copies(r, i):
        part = pl.ds(i * piece, piece)
        return (
            pltpu.make_async_copy(keys.at[r, part], kbuf.at[r, part], sems.at[0, r, i]),
            pltpu.make_async_copy(values.at[r, part], vbuf.at[r, part], sems.at[1, r, i]),
        )

    def fetch(r, _):
        for i in range(pieces):

            @pl.when((i == 0) | (i * piece < lens[r]))
            def _():
                for copy in copies(r, i):
                    copy.start()

        return 0

    lax.fori_loop(0, rows, fetch, 0)
    lane = lax.broadcasted_iota(jnp.int32, (width, piece), 1)
    causal = (
        lax.broadcasted_iota(jnp.int32, (width, steps), 1)
        <= lax.broadcasted_iota(jnp.int32, (width, steps), 0) // group
    )

    def one_row(r, _):
        def part(i):
            span = pl.ds(i * piece, piece)
            return (
                lambda head: kbuf[r, span, head * HD : (head + 1) * HD],
                lambda head: vbuf[r, span, head * HD : (head + 1) * HD],
                lane + i * piece < lens[r],
            )

        own = (
            lambda head: step_k[r, :, head * HD : (head + 1) * HD],
            lambda head: step_v[r, :, head * HD : (head + 1) * HD],
            causal,
        )
        for copy in copies(r, 0):
            copy.wait()
        absorb(r, q_ref, [own, part(0)], (acc, top, total), True)
        for i in range(1, pieces):

            @pl.when(i * piece < lens[r])
            def _():
                for copy in copies(r, i):
                    copy.wait()
                absorb(r, q_ref, [part(i)], (acc, top, total), False)

        return 0

    lax.fori_loop(0, rows, one_row, 0)


def state_shapes(rows, width):
    shape = jax.ShapeDtypeStruct((rows, KVH, width, HD), jnp.float32)
    return (shape,) * 3


def resident(lens, grouped, step_k, step_v, keys, values):
    rows, slot_count, feature = keys.shape
    pieces = slot_count // min(CHUNK, slot_count)
    vmem = pl.BlockSpec(memory_space=pltpu.VMEM)
    hbm = pl.BlockSpec(memory_space=pl.ANY)
    return pl.pallas_call(
        resident_kernel,
        out_shape=state_shapes(rows, grouped.shape[2]),
        in_specs=[pl.BlockSpec(memory_space=pltpu.SMEM), vmem, vmem, vmem, hbm, hbm],
        out_specs=(vmem,) * 3,
        scratch_shapes=[
            pltpu.VMEM((rows, slot_count, feature), jnp.bfloat16),
            pltpu.VMEM((rows, slot_count, feature), jnp.bfloat16),
            pltpu.SemaphoreType.DMA((2, rows, pieces)),
        ],
        cost_estimate=pl.CostEstimate(
            flops=2 * 10**9, bytes_accessed=16 * 2**20, transcendentals=10**6
        ),
        name="resident",
    )(lens, grouped, step_k, step_v, keys, values)


def span_kernel(
    kind, count, cap, base, used, slot_of, row_of, rank_of, start, tokens_of,
    q_ref, ca, sa, cb, sb, *refs,
):
    messages = refs[:count]
    refs = refs[count:]
    if kind == "partial":
        out, stats, acc, top, total, got, kbuf, vbuf, sems = refs
        loads = []
    elif kind == "state":
        *before, acc, top, total, got, kbuf, vbuf, sems = refs
        loads = list(zip(before, (acc, top, total)))
    else:
        *before, part, stats, out, acc, top, total, scr, got, kbuf, vbuf, sems = refs
        loads = list(zip(before, (acc, top, total)))
    state = (acc, top, total)
    rows = q_ref.shape[0]
    width = q_ref.shape[2]
    feature = kbuf.shape[1]
    fetches = [pltpu.make_async_copy(messages[j], got.at[j], sems.at[j]) for j in range(count)]
    for fetch in fetches:
        fetch.start()
    loads = [
        pltpu.make_async_copy(a, b, sems.at[count + i]) for i, (a, b) in enumerate(loads)
    ]
    for load in loads:
        load.start()
    last = start[rows - 1] * BLK + tokens_of[rows - 1]
    tail = pl.ds(pl.multiple_of(last, BLK), SPAN)
    vbuf[tail, :] = jnp.zeros((SPAN, feature), jnp.float32)
    unroll = min(UNROLL, cap)
    for j in range(count):
        first = base[j]
        fetches[j].wait()

        def place(step, _):
            ready = []
            for u in range(unroll):
                k = step * unroll + u
                slot = slot_of[first + k]
                r = row_of[first + k]
                rank = rank_of[first + k]
                c_a, s_a = ca[r], sa[r]
                c_b, s_b = cb[pl.ds(rank, 1), :], sb[pl.ds(rank, 1), :]
                cosine = c_a * c_b - s_a * s_b
                sine = s_a * c_b + c_a * s_b
                where = pl.ds(pl.multiple_of(slot * BLK, BLK), BLK)
                value = got[j, 1, k].astype(jnp.float32)
                key = got[j, 0, k].astype(jnp.float32)
                turned = []
                for head in range(KVH):
                    piece = key[:, head * HD : (head + 1) * HD]
                    turned.append(piece * cosine + pltpu.roll(piece, HD // 2, 1) * sine)
                ready.append((where, turned, value))
            for where, turned, value in ready:
                vbuf[where, :] = value
                for head in range(KVH):
                    kbuf[where, head * HD : (head + 1) * HD] = turned[head]
            return 0

        lax.fori_loop(0, (used[j] + unroll - 1) // unroll, place, 0)
    for load in loads:
        load.wait()
    lane = lax.broadcasted_iota(jnp.int32, (width, SPAN), 1)
    eye = lax.broadcasted_iota(jnp.int32, (width, width), 0) == lax.broadcasted_iota(
        jnp.int32, (width, width), 1
    )

    def one_row(r, _):
        tokens = tokens_of[r]
        origin = start[r] * BLK
        if kind == "partial":
            acc[r] = jnp.zeros_like(acc[r])
            top[r] = jnp.full_like(top[r], NEG)
            total[r] = jnp.zeros_like(total[r])

        def piece(i, _):
            where = pl.ds(pl.multiple_of(origin + i * SPAN, BLK), SPAN)
            block = (
                lambda head: kbuf[where, head * HD : (head + 1) * HD].astype(jnp.bfloat16),
                lambda head: vbuf[where, head * HD : (head + 1) * HD].astype(jnp.bfloat16),
                lane + i * SPAN < tokens,
            )
            absorb(r, q_ref, [block], state, False)
            return 0

        lax.fori_loop(0, (tokens + SPAN - 1) // SPAN, piece, 0)
        if kind == "partial":
            done = []
            for head in range(KVH):
                held = total[r, head]
                safe = jnp.where(held > 0.0, held, 1.0)
                lines = [
                    jnp.sum(jnp.where(eye, one[:, :width], 0.0), axis=0, keepdims=True)
                    for one in (top[r, head], held)
                ]
                done.append(((acc[r, head] / safe).astype(jnp.bfloat16), lines))
            for head in range(KVH):
                out[r, head] = done[head][0]
                for i in range(2):
                    stats[r, head, pl.ds(i, 1), :] = done[head][1][i]
        if kind == "final":
            steps = out.shape[1]
            group = width // steps
            done = []
            for head in range(KVH):
                lines = []
                for i in range(2):
                    line = jnp.broadcast_to(stats[r, head, pl.ds(i, 1), :], (width, width))
                    lines.append(jnp.sum(jnp.where(eye, line, 0.0), axis=1, keepdims=True))
                other_top, other_total = lines
                other_top = jnp.where(other_total > 0.0, other_top, NEG)
                old_top = top[r, head]
                new_top = jnp.maximum(old_top, other_top)
                mine = jnp.exp(old_top - new_top)
                theirs = jnp.exp(other_top - new_top) * other_total
                whole = total[r, head] * mine + theirs
                merged = acc[r, head] * mine + part[r, head].astype(jnp.float32) * theirs
                done.append(merged / whole)
            for head in range(KVH):
                scr[head] = done[head]
            for head in range(KVH):
                for g in range(group):
                    column = (head * group + g) * HD
                    out[r, :, column : column + HD] = scr[
                        head, pl.ds(g, steps, stride=group), :
                    ].astype(jnp.bfloat16)
        return 0

    lax.fori_loop(0, rows, one_row, 0)


def span(kind, cap, scalars, grouped, tables, messages, state, extra, steps):
    rows, _, width, _ = grouped.shape
    feature = messages[0].shape[-1]
    count = len(messages)
    room = (count * cap + 1) * BLK + SPAN
    smem = pl.BlockSpec(memory_space=pltpu.SMEM)
    vmem = pl.BlockSpec(memory_space=pltpu.VMEM)
    hbm = pl.BlockSpec(memory_space=pl.ANY)
    hold = [pltpu.VMEM((rows, KVH, width, HD), jnp.float32)] * 3
    scratch = []
    if kind == "partial":
        out_shape = (
            jax.ShapeDtypeStruct((rows, KVH, width, HD), jnp.bfloat16),
            jax.ShapeDtypeStruct((rows, KVH, 2, width), jnp.float32),
        )
        scratch += hold
    elif kind == "state":
        out_shape = state_shapes(rows, width)
    else:
        out_shape = jax.ShapeDtypeStruct((rows, steps, QH * HD), jnp.bfloat16)
        scratch += hold + [pltpu.VMEM((KVH, width, HD), jnp.float32)]
    scratch += [
        pltpu.VMEM((count, 2, cap, BLK, feature), jnp.bfloat16),
        pltpu.VMEM((room, feature), jnp.float32),
        pltpu.VMEM((room, feature), jnp.float32),
        pltpu.SemaphoreType.DMA((count + 3,)),
    ]
    return pl.pallas_call(
        functools.partial(span_kernel, kind, count, cap),
        out_shape=out_shape,
        in_specs=[smem] * 7 + [vmem] * 5 + [hbm] * (count + len(state)) + [vmem] * len(extra),
        out_specs=jax.tree.map(lambda _: vmem, out_shape),
        scratch_shapes=scratch,
        cost_estimate=pl.CostEstimate(
            flops=10**9, bytes_accessed=12 * 2**20, transcendentals=10**6
        ),
    )(*scalars, grouped, *tables, *messages, *state, *extra)


PHASES = {"d": (2, 2, 2, 2), "f": (0, 3, 3, 0), "g": (3, 0, 0, 3), "b": (1, 1, 1, 1)}


def site_plane(plane, flip):
    dest = plane ^ flip
    half = PLANES // 2
    if (plane < half) != (dest < half) and dest in (half - 1, half):
        return PLANES - 1 - dest
    return dest


def came_from(phase, plane):
    flips = PHASES[phase]
    return next(s for s in range(PLANES) if site_plane(s, flips[s]) == plane)


def for_mirror(phase, plane):
    source = came_from(phase, plane)
    return int(source ^ PHASES[phase][source] != plane)


def route(n, phase, offset):
    in_plane = n // PLANES
    return [
        (
            plane * in_plane + place,
            site_plane(plane, flip) * in_plane + (place + offset) % in_plane,
        )
        for plane, flip in enumerate(PHASES[phase])
        for place in range(in_plane)
    ]


def by_plane(table, plane):
    table = jnp.array(table, jnp.int32)
    chosen = jnp.arange(PLANES, dtype=jnp.int32) == plane
    return jnp.sum(jnp.where(chosen.reshape((-1,) + (1,) * (table.ndim - 1)), table, 0), axis=0)


def body(
    span_keys,
    span_values,
    block_device,
    block_row,
    cache_len,
    cache_keys,
    cache_values,
    queries,
    step_keys,
    step_values,
):
    n = lax.axis_size("seq")
    in_plane = n // PLANES
    me = lax.axis_index("seq").astype(jnp.int32)
    plane, place = me // in_plane, me % in_plane
    rows = cache_len.shape[0]
    feature = span_keys.shape[1]
    blocks = span_keys.shape[0] // BLK
    cap = max(2, (2 * blocks + n - 1) // n)
    steps = queries.shape[1]
    group = QH // KVH
    seq = jnp.arange(n, dtype=jnp.int32)
    names = list(PHASES)

    phase_of_flip = [
        [next(i for i, p in enumerate(names) if PHASES[p][z] == z ^ d) for d in range(PLANES)]
        for z in range(PLANES)
    ]
    rel = (
        jnp.repeat(by_plane(phase_of_flip, plane), in_plane) * in_plane
        + (seq % in_plane - place) % in_plane
    )
    grouped = (
        queries.reshape(rows, steps, KVH, group, HD)
        .transpose(0, 2, 1, 3, 4)
        .reshape(rows, KVH, steps * group, HD)
    )
    half = PLANES // 2
    swap = [
        (a * in_plane + i, b * in_plane + i)
        for a, b in ((half - 1, half), (half, half - 1))
        for i in range(in_plane)
    ]
    mirrored = lax.ppermute(grouped, "seq", swap)

    meta, *messages = pack(
        n,
        cap,
        block_device[:, 0],
        block_row,
        rel,
        span_keys.reshape(blocks, BLK, feature),
        span_values.reshape(blocks, BLK, feature),
    )
    packed = {p: messages[i * in_plane : (i + 1) * in_plane] for i, p in enumerate(names)}

    def send(phase, after=None):
        out = []
        for offset in range(in_plane):
            value = packed[phase][offset]
            if after is not None:
                value, after[offset] = lax.optimization_barrier((value, after[offset]))
            pairs = route(n, phase, offset)
            if any(a != b for a, b in pairs):
                value = lax.ppermute(value, "seq", pairs)
            out.append(value)
        return out

    got = {}
    got["d"] = send("d")
    got["f"] = send("f")
    got["g"] = send("g", got["d"])
    got["b"] = send("b", got["g"])

    table = meta.reshape(PLANES, in_plane, cap)
    mirror_plane = [p if p in (0, PLANES - 1) else PLANES - 1 - p for p in range(PLANES)]
    table_mirror = jnp.concatenate([table[p][None] for p in mirror_plane])
    notes = jnp.concatenate(
        [
            table.reshape(n, cap),
            table_mirror.reshape(n, cap),
            jnp.broadcast_to(cache_len[None], (n, rows)),
        ],
        axis=1,
    )
    notes = lax.all_to_all(notes, "seq", split_axis=0, concat_axis=0, tiled=True)
    mirror_me = by_plane(mirror_plane, plane) * in_plane + place
    mirror_len = jnp.sum(jnp.where((seq == mirror_me)[:, None], notes[:, 2 * cap :], 0), axis=0)
    rows_of = jnp.stack([notes[:, :cap], notes[:, cap : 2 * cap]])

    came = by_plane([[came_from(p, z) for p in names] for z in range(PLANES)], plane)
    other = by_plane([[for_mirror(p, z) for p in names] for z in range(PLANES)], plane)
    offsets = jnp.arange(in_plane, dtype=jnp.int32)
    source = came[:, None] * in_plane + (place - offsets[None]) % in_plane
    entry = (other[:, None] * n + source).reshape(-1)
    kernel_of_phase = {"d": 1, "f": 1, "g": 2, "b": 3}
    stage = jnp.array([[kernel_of_phase[p]] for p in names], jnp.int32)
    stage = jnp.where(other[:, None] == 1, 0, stage)
    stage = jnp.broadcast_to(stage, (len(names), in_plane)).reshape(-1)
    same = entry[:, None] == jnp.arange(2 * n, dtype=jnp.int32)[None]
    stage_of = jnp.max(jnp.where(same, stage[:, None], -1), axis=0).reshape(2, n)

    row_ids = jnp.arange(rows, dtype=jnp.int32)
    hits = rows_of[..., None] == row_ids
    kinds = [(0, None), (1, None), (1, 0), (0, 1), (0, 2), (0, 3)]
    columns = [
        hits[s] if k is None else hits[s] & (stage_of[s] == k)[:, None, None] for s, k in kinds
    ]
    columns = jnp.concatenate([c.reshape(n * cap, rows) for c in columns], axis=1)
    order = jnp.arange(n * cap, dtype=jnp.int32)
    earlier = jnp.dot(
        (order[:, None] > order[None, :]).astype(jnp.bfloat16),
        columns.astype(jnp.bfloat16),
        preferred_element_type=jnp.float32,
    ).astype(jnp.int32)
    number = jnp.sum(columns.astype(jnp.int32), axis=0).reshape(len(kinds), rows)
    below = row_ids[:, None] > row_ids[None, :]
    begin = jnp.sum(jnp.where(below[None], number[:, None, :], 0), axis=2)
    begin_flat = jnp.where(
        jnp.arange(len(kinds))[:, None] < 2, 0, begin
    ).reshape(-1)
    where = jnp.where(columns, earlier + begin_flat[None], 0)
    where = jnp.sum(where.reshape(n * cap, len(kinds), rows), axis=2)
    member = jnp.any(columns.reshape(n * cap, len(kinds), rows), axis=2)
    rank_of = jnp.concatenate([where[:, 0], where[:, 1]])
    spare = SPAN // BLK
    trash = {0: 2 * in_plane * cap + spare, 1: 2 * in_plane * cap + spare, 2: in_plane * cap + spare}
    own_slot = jnp.where(
        member[:, 3], where[:, 3], jnp.where(member[:, 4], where[:, 4], where[:, 5])
    )
    own_trash = jnp.where(stage_of[0] == 1, trash[1], trash[2])
    own_slot = jnp.where(
        rows_of[0].reshape(-1) < 0, jnp.repeat(own_trash, cap), own_slot
    )
    mirror_slot = jnp.where(rows_of[1].reshape(-1) < 0, trash[0], where[:, 2])
    slot_of = jnp.concatenate([own_slot, mirror_slot])
    row_of = jnp.maximum(rows_of.reshape(-1), 0)
    filled = jnp.sum((rows_of >= 0).astype(jnp.int32), axis=2).reshape(-1)
    used = jnp.sum(jnp.where(same, filled[None], 0), axis=1)
    base = entry * cap

    own_tables = turn_tables(cache_len[:, None] + jnp.arange(BLK, dtype=jnp.int32)[None])
    mirror_tables = turn_tables(mirror_len[:, None] + jnp.arange(BLK, dtype=jnp.int32)[None])
    rank_tables = turn_tables(order * BLK)

    def scalars(phases, kernel):
        def part(value):
            return jnp.concatenate(
                [
                    value[names.index(p) * in_plane : (names.index(p) + 1) * in_plane]
                    for p in phases
                ]
            )

        column = kernel + 2
        return (
            part(base),
            jnp.where(part(stage) == kernel, part(used), 0),
            slot_of,
            row_of,
            rank_of,
            begin[column],
            number[column] * BLK,
        )

    state = resident(cache_len, grouped, step_keys, step_values, cache_keys, cache_values)
    partial, stats = span(
        "partial", cap, scalars("df", 0), mirrored,
        mirror_tables + rank_tables, got["d"] + got["f"], (), (), steps,
    )
    partial = lax.ppermute(partial, "seq", swap)
    stats = lax.ppermute(stats, "seq", swap)
    state = span(
        "state", cap, scalars("df", 1), grouped,
        own_tables + rank_tables, got["d"] + got["f"], tuple(state), (), steps,
    )
    state = span(
        "state", cap, scalars("g", 2), grouped,
        own_tables + rank_tables, got["g"], tuple(state), (), steps,
    )
    return span(
        "final", cap, scalars("b", 3), grouped,
        own_tables + rank_tables, got["b"], tuple(state), (partial, stats), steps,
    )


def solution(mesh):
    placed = (
        P(("groups", "seq"), None),
        P(("groups", "seq"), None),
        P(("groups", "seq"), None),
        P(("groups", "seq")),
        P(("groups", "seq")),
        P(("groups", "seq"), None, None),
        P(("groups", "seq"), None, None),
        P(("groups", "seq"), None, None),
        P(("groups", "seq"), None, None),
        P(("groups", "seq"), None, None),
    )

    return jax.shard_map(
        body,
        mesh=mesh,
        in_specs=placed,
        out_specs=P(("groups", "seq"), None, None),
        check_vma=False,
    )
```

```python
import functools

import jax
import jax.numpy as jnp
import numpy as np
from jax import lax
from jax.experimental import pallas as pl
from jax.experimental.pallas import tpu as pltpu
from jax.sharding import PartitionSpec as P


KVH = 4
QH = 64
HD = 128
BLK = 8
PLANES = 4
CHUNK = 256
SPAN = 128
LANES = 128
GRANT = 20 * 2**20
UNROLL = 4
NEG = -1e30


def frequencies(half_width):
    freq_index = jnp.arange(half_width, dtype=jnp.float32)
    base_freq = 1.0 / 500000.0 ** (freq_index / half_width)
    wavelen = 2.0 * jnp.pi / base_freq
    smooth = (8192.0 / wavelen - 1.0) / 3.0
    blended = (1.0 - smooth) * base_freq / 8.0 + smooth * base_freq
    scaled = jnp.where(wavelen > 8192.0, base_freq / 8.0, blended)
    return jnp.where(wavelen < 2048.0, base_freq, scaled)


def turn_tables(positions):
    freq = frequencies(HD // 2)
    angles = positions.astype(jnp.float32)[..., None] * jnp.concatenate([freq, freq])
    sign = jnp.where(jnp.arange(HD) < HD // 2, -1.0, 1.0).astype(jnp.float32)
    return jnp.cos(angles), jnp.sin(angles) * sign


def pack_kernel(n, cap, phase_table, target, rows, lens, keys, values, *refs):
    notes = refs[0]
    outs = refs[1 : 1 + n]
    slots, fill, rel, sems = refs[1 + n :]
    blocks = keys.shape[0]
    in_plane = n // PLANES
    me = lax.axis_index("seq")
    plane, place = me // in_plane, me % in_plane

    def clear(i, _):
        fill[i] = 0
        offset = (i % in_plane - place + in_plane) % in_plane
        rel[i] = phase_table[plane, i // in_plane] * in_plane + offset
        for k in range(cap):
            notes[i, k] = -1
            notes[i, LANES + k] = -1
        for k in range(lens.shape[0]):
            notes[i, 2 * LANES + k] = lens[k]
        return 0

    lax.fori_loop(0, n, clear, 0)

    def put(b, _):
        dest = target[b]
        slot = fill[dest]
        fill[dest] = slot + 1
        row = rows[b]
        dest_plane = dest // in_plane
        inner = (dest_plane > 0) & (dest_plane < PLANES - 1)
        twin = jnp.where(inner, (PLANES - 1 - 2 * dest_plane) * in_plane + dest, dest)
        notes[dest, slot] = row
        notes[twin, LANES + slot] = row
        message = rel[dest]
        slots[message, 0, slot] = keys[b]
        slots[message, 1, slot] = values[b]
        return 0

    lax.fori_loop(0, blocks, put, 0, unroll=4)
    copies = [pltpu.make_async_copy(slots.at[i], outs[i], sems.at[i]) for i in range(n)]
    for copy in copies:
        copy.start()
    for copy in copies:
        copy.wait()


def pack(n, cap, phase_table, target, rows, lens, keys, values):
    width = keys.shape[-1]
    message = jax.ShapeDtypeStruct((2, cap, BLK, width), jnp.bfloat16)
    smem = pl.BlockSpec(memory_space=pltpu.SMEM)
    vmem = pl.BlockSpec(memory_space=pltpu.VMEM)
    return pl.pallas_call(
        functools.partial(pack_kernel, n, cap),
        out_shape=(jax.ShapeDtypeStruct((n, 3 * LANES), jnp.int32),) + (message,) * n,
        in_specs=[smem] * 4 + [vmem] * 2,
        out_specs=(smem,) + (pl.BlockSpec(memory_space=pl.ANY),) * n,
        scratch_shapes=[
            pltpu.VMEM((n, 2, cap, BLK, width), jnp.bfloat16),
            pltpu.SMEM((n,), jnp.int32),
            pltpu.SMEM((n,), jnp.int32),
            pltpu.SemaphoreType.DMA((n,)),
        ],
        compiler_params=pltpu.CompilerParams(vmem_limit_bytes=GRANT),
        name="pack",
    )(phase_table, target, rows, lens, keys, values)


def index_kernel(n, cap, rows, notes, stages, place, row_of, rank_of, used, tally):
    f32 = jnp.float32

    def iotas(shape):
        return [lax.broadcasted_iota(jnp.int32, shape, d) for d in (0, 1)]

    a, b = iotas((cap, cap))
    before = (a < b).astype(f32)
    a, b = iotas((n, n))
    sooner = (b < a).astype(f32)
    lines = [jnp.broadcast_to(stages[i : i + 1, :n], (n, n)) for i in range(2)]
    posts = [
        jnp.sum(jnp.where(a == b, line, 0), axis=1, keepdims=True) for line in lines
    ]
    mates = [jnp.where(line == post, sooner, 0.0) for line, post in zip(lines, posts)]
    kernel, lane = iotas((8, LANES))
    counts = jnp.zeros((8, LANES), f32)
    for side in range(2):
        rows_here = notes[:, side * LANES : side * LANES + cap]
        rank = jnp.zeros((n, cap), f32)
        local = jnp.zeros((n, cap), f32)
        for r in range(rows):
            hit = (rows_here == r).astype(f32)
            inside = jnp.dot(hit, before, preferred_element_type=f32)
            ahead = jnp.dot(sooner, hit, preferred_element_type=f32)
            near = jnp.dot(mates[side], hit, preferred_element_type=f32)
            rank += hit * (inside + jnp.sum(ahead, axis=1, keepdims=True))
            local += hit * (inside + jnp.sum(near, axis=1, keepdims=True))
            per_source = jnp.sum(hit, axis=1, keepdims=True)
            for stage in range(3):
                if (stage == 0) == (side == 1):
                    number = jnp.sum(
                        jnp.where(posts[side] == stage, per_source, 0.0), axis=0, keepdims=True
                    )
                    counts += jnp.where((kernel == stage) & (lane == r), number, 0.0)
        span = slice(side * n, side * n + n)
        valid = rows_here >= 0
        place[span, :] = jnp.where(valid, local, -1.0).astype(jnp.int32)
        row_of[span, :] = jnp.maximum(rows_here, 0)
        rank_of[span, :] = rank.astype(jnp.int32)
        filled = jnp.sum(valid.astype(f32), axis=1, keepdims=True)
        used[span, :] = jnp.broadcast_to(filled, (n, cap)).astype(jnp.int32)
    a, b = iotas((LANES, LANES))
    begin = jnp.dot(counts, (a < b).astype(f32), preferred_element_type=f32)
    tally[0:8, :] = begin.astype(jnp.int32)
    tally[8:16, :] = (counts * BLK).astype(jnp.int32)


def index(n, cap, rows, notes, stages):
    vmem = pl.BlockSpec(memory_space=pltpu.VMEM)
    slots = jax.ShapeDtypeStruct((2 * n, cap), jnp.int32)
    return pl.pallas_call(
        functools.partial(index_kernel, n, cap, rows),
        out_shape=(slots,) * 4 + (jax.ShapeDtypeStruct((16, LANES), jnp.int32),),
        in_specs=[vmem] * 2,
        out_specs=(vmem,) * 5,
        compiler_params=pltpu.CompilerParams(vmem_limit_bytes=GRANT),
        name="index",
    )(notes, stages)


def blend(queries, pieces, old, guard=False):
    scale = HD ** (-0.5)
    heads = range(KVH)
    scores = [
        [
            jnp.where(
                piece[2],
                lax.dot_general(
                    queries[head],
                    piece[0][head],
                    (((1,), (1,)), ((), ())),
                    preferred_element_type=jnp.float32,
                )
                * scale,
                NEG,
            )
            for piece in pieces
        ]
        for head in heads
    ]
    new = []
    for head in heads:
        peak = functools.reduce(
            jnp.maximum, [jnp.max(one, axis=-1, keepdims=True) for one in scores[head]]
        )
        if old is None:
            new_top = jnp.broadcast_to(peak, (peak.shape[0], HD))
        else:
            old_acc, old_top, old_total = old[head]
            new_top = jnp.maximum(old_top, peak)
        raw = [jnp.exp(one - new_top[:, :1]) for one in scores[head]]
        if guard:
            raw = [jnp.where(piece[2], one, 0.0) for piece, one in zip(pieces, raw)]
        added = sum(jnp.sum(one, axis=-1, keepdims=True) for one in raw)
        mixed = sum(
            jnp.dot(one.astype(jnp.bfloat16), piece[1][head], preferred_element_type=jnp.float32)
            for one, piece in zip(raw, pieces)
        )
        if old is None:
            new.append((mixed, new_top, jnp.broadcast_to(added, new_top.shape)))
        else:
            factor = jnp.exp(old_top - new_top)
            new.append((old_acc * factor + mixed, new_top, old_total * factor + added))
    return new


def held(row, state):
    return [tuple(one[row, head] for one in state) for head in range(KVH)]


def hold(row, state, new):
    for head in range(KVH):
        for one, value in zip(state, new[head]):
            one[row, head] = value


def row_queries(row, q_ref):
    return [q_ref[row, head] for head in range(KVH)]


def resident_kernel(
    lens, q_ref, step_k, step_v, keys, values, acc, top, total, kbuf, vbuf, sems
):
    rows, slot_count = kbuf.shape[0], kbuf.shape[1]
    piece = min(CHUNK, slot_count)
    pieces = slot_count // piece
    steps = step_k.shape[1]
    width = q_ref.shape[2]
    group = width // steps

    def copies(r, i):
        part = pl.ds(i * piece, piece)
        return (
            pltpu.make_async_copy(keys.at[r, part], kbuf.at[r, part], sems.at[0, r, i]),
            pltpu.make_async_copy(values.at[r, part], vbuf.at[r, part], sems.at[1, r, i]),
        )

    def fetch(r, _):
        for i in range(pieces):

            @pl.when((i == 0) | (i * piece < lens[r]))
            def _():
                for copy in copies(r, i):
                    copy.start()

        return 0

    lax.fori_loop(0, rows, fetch, 0)
    lane = lax.broadcasted_iota(jnp.int32, (width, piece), 1)
    causal = (
        lax.broadcasted_iota(jnp.int32, (width, steps), 1)
        <= lax.broadcasted_iota(jnp.int32, (width, steps), 0) // group
    )

    def one_row(r, _):
        def part(i):
            span = pl.ds(i * piece, piece)
            return (
                [kbuf[r, span, head * HD : (head + 1) * HD] for head in range(KVH)],
                [vbuf[r, span, head * HD : (head + 1) * HD] for head in range(KVH)],
                lane + i * piece < lens[r],
            )

        own = (
            [step_k[r, :, head * HD : (head + 1) * HD] for head in range(KVH)],
            [step_v[r, :, head * HD : (head + 1) * HD] for head in range(KVH)],
            causal,
        )
        state = (acc, top, total)
        for copy in copies(r, 0):
            copy.wait()
        hold(r, state, blend(row_queries(r, q_ref), [own, part(0)], None))
        for i in range(1, pieces):

            @pl.when(i * piece < lens[r])
            def _():
                for copy in copies(r, i):
                    copy.wait()
                hold(r, state, blend(row_queries(r, q_ref), [part(i)], held(r, state)))

        return 0

    lax.fori_loop(0, rows, one_row, 0)


def state_shapes(rows, width):
    shape = jax.ShapeDtypeStruct((rows, KVH, width, HD), jnp.float32)
    return (shape,) * 3


def resident(lens, grouped, step_k, step_v, keys, values):
    rows, slot_count, feature = keys.shape
    pieces = slot_count // min(CHUNK, slot_count)
    vmem = pl.BlockSpec(memory_space=pltpu.VMEM)
    hbm = pl.BlockSpec(memory_space=pl.ANY)
    return pl.pallas_call(
        resident_kernel,
        out_shape=state_shapes(rows, grouped.shape[2]),
        in_specs=[pl.BlockSpec(memory_space=pltpu.SMEM), vmem, vmem, vmem, hbm, hbm],
        out_specs=(vmem,) * 3,
        scratch_shapes=[
            pltpu.VMEM((rows, slot_count, feature), jnp.bfloat16),
            pltpu.VMEM((rows, slot_count, feature), jnp.bfloat16),
            pltpu.SemaphoreType.DMA((2, rows, pieces)),
        ],
        compiler_params=pltpu.CompilerParams(vmem_limit_bytes=GRANT),
        cost_estimate=pl.CostEstimate(
            flops=2 * 10**9, bytes_accessed=16 * 2**20, transcendentals=10**6
        ),
        name="resident",
    )(lens, grouped, step_k, step_v, keys, values)


def span_kernel(
    kind, kernel, count, cap, entry, stage, place_of, row_of, rank_of, used, tally,
    q_ref, ca, sa, cb, sb, *refs,
):
    messages = refs[:count]
    refs = refs[count:]
    if kind == "partial":
        out, stats, acc, top, total, got, kbuf, vbuf, sems = refs
        loads = []
    elif kind == "state":
        *before, acc, top, total, got, kbuf, vbuf, sems = refs
        loads = list(zip(before, (acc, top, total)))
    else:
        *before, part, stats, out, acc, top, total, scr, got, kbuf, vbuf, sems = refs
        loads = list(zip(before, (acc, top, total)))
    state = (acc, top, total)
    rows = q_ref.shape[0]
    width = q_ref.shape[2]
    feature = kbuf.shape[1]
    fetches = [pltpu.make_async_copy(messages[j], got.at[j], sems.at[j]) for j in range(count)]
    for j in range(count):

        @pl.when(stage[j] == kernel)
        def _():
            fetches[j].start()

    loads = [
        pltpu.make_async_copy(a, b, sems.at[count + i]) for i, (a, b) in enumerate(loads)
    ]
    for load in loads:
        load.start()
    last = tally[kernel, rows - 1] * BLK + tally[8 + kernel, rows - 1]
    tail = pl.ds(pl.multiple_of(last, BLK), SPAN)
    vbuf[tail, :] = jnp.zeros((SPAN, feature), jnp.float32)
    unroll = min(UNROLL, cap)
    trash = count * cap + SPAN // BLK
    for j in range(count):

        @pl.when(stage[j] == kernel)
        def _():
            source = entry[j]
            fetches[j].wait()

            def place(step, _):
                ready = []
                for u in range(unroll):
                    k = step * unroll + u
                    r = row_of[source, k]
                    rank = rank_of[source, k]
                    local = place_of[source, k]
                    slot = jnp.where(local < 0, trash, tally[kernel, r] + local)
                    c_a, s_a = ca[r], sa[r]
                    c_b, s_b = cb[pl.ds(rank, 1), :], sb[pl.ds(rank, 1), :]
                    cosine = c_a * c_b - s_a * s_b
                    sine = s_a * c_b + c_a * s_b
                    where = pl.ds(pl.multiple_of(slot * BLK, BLK), BLK)
                    value = got[j, 1, k].astype(jnp.float32)
                    key = got[j, 0, k].astype(jnp.float32)
                    turned = []
                    for head in range(KVH):
                        piece = key[:, head * HD : (head + 1) * HD]
                        turned.append(piece * cosine + pltpu.roll(piece, HD // 2, 1) * sine)
                    ready.append((where, turned, value))
                for where, turned, value in ready:
                    vbuf[where, :] = value
                    for head in range(KVH):
                        kbuf[where, head * HD : (head + 1) * HD] = turned[head]
                return 0

            lax.fori_loop(0, (used[source, 0] + unroll - 1) // unroll, place, 0)

    for load in loads:
        load.wait()
    lane = lax.broadcasted_iota(jnp.int32, (width, SPAN), 1)
    eye = lax.broadcasted_iota(jnp.int32, (width, width), 0) == lax.broadcasted_iota(
        jnp.int32, (width, width), 1
    )

    def block(r, i):
        where = pl.ds(pl.multiple_of(tally[kernel, r] * BLK + i * SPAN, BLK), SPAN)
        return (
            [kbuf[where, h * HD : (h + 1) * HD].astype(jnp.bfloat16) for h in range(KVH)],
            [vbuf[where, h * HD : (h + 1) * HD].astype(jnp.bfloat16) for h in range(KVH)],
            lane + i * SPAN < tally[8 + kernel, r],
        )

    def beyond(r):
        def piece(i, _):
            hold(r, state, blend(row_queries(r, q_ref), [block(r, i)], held(r, state)))
            return 0

        lax.fori_loop(1, (tally[8 + kernel, r] + SPAN - 1) // SPAN, piece, 0)

    def partial_rows(pair):
        new = [blend(row_queries(r, q_ref), [block(r, 0)], None, guard=True) for r in pair]
        for r, one in zip(pair, new):
            hold(r, state, one)
        for r in pair:
            beyond(r)
        done = []
        for r in pair:
            for head in range(KVH):
                amount = total[r, head]
                safe = jnp.where(amount > 0.0, amount, 1.0)
                lines = [
                    jnp.sum(jnp.where(eye, one[:, :width], 0.0), axis=0, keepdims=True)
                    for one in (top[r, head], amount)
                ]
                done.append((r, head, (acc[r, head] / safe).astype(jnp.bfloat16), lines))
        for r, head, value, lines in done:
            out[r, head] = value
            for i in range(2):
                stats[r, head, pl.ds(i, 1), :] = lines[i]

    def state_rows(pair):
        for r in pair:
            beyond(r)
        new = [blend(row_queries(r, q_ref), [block(r, 0)], held(r, state)) for r in pair]
        for r, one in zip(pair, new):
            hold(r, state, one)

    def final_rows(pair):
        for r in pair:
            beyond(r)
        done = []
        for r in pair:
            new = blend(row_queries(r, q_ref), [block(r, 0)], held(r, state))
            for head in range(KVH):
                lines = []
                for i in range(2):
                    line = jnp.broadcast_to(stats[r, head, pl.ds(i, 1), :], (width, width))
                    lines.append(jnp.sum(jnp.where(eye, line, 0.0), axis=1, keepdims=True))
                other_top, other_total = lines
                other_top = jnp.where(other_total > 0.0, other_top, NEG)
                value, old_top, amount = new[head]
                new_top = jnp.maximum(old_top, other_top)
                mine = jnp.exp(old_top - new_top)
                theirs = jnp.exp(other_top - new_top) * other_total
                whole = amount * mine + theirs
                merged = value * mine + part[r, head].astype(jnp.float32) * theirs
                done.append(merged / whole)
        for i, value in enumerate(done):
            scr[i] = value
        steps = out.shape[1]
        group = width // steps
        for i, r in enumerate(pair):
            for head in range(KVH):
                for g in range(group):
                    column = (head * group + g) * HD
                    out[r, :, column : column + HD] = scr[
                        i * KVH + head, pl.ds(g, steps, stride=group), :
                    ].astype(jnp.bfloat16)

    run = {"partial": partial_rows, "state": state_rows, "final": final_rows}[kind]
    together = 2 if rows % 2 == 0 else 1

    def some_rows(i, _):
        run([i * together + u for u in range(together)])
        return 0

    lax.fori_loop(0, rows // together, some_rows, 0)


def span(kind, kernel, cap, scalars, grouped, tables, messages, state, extra, steps):
    rows, _, width, _ = grouped.shape
    feature = messages[0].shape[-1]
    count = len(messages)
    room = (count * cap + 1) * BLK + SPAN
    smem = pl.BlockSpec(memory_space=pltpu.SMEM)
    vmem = pl.BlockSpec(memory_space=pltpu.VMEM)
    hbm = pl.BlockSpec(memory_space=pl.ANY)
    running = [pltpu.VMEM((rows, KVH, width, HD), jnp.float32)] * 3
    scratch = []
    if kind == "partial":
        out_shape = (
            jax.ShapeDtypeStruct((rows, KVH, width, HD), jnp.bfloat16),
            jax.ShapeDtypeStruct((rows, KVH, 2, width), jnp.float32),
        )
        scratch += running
    elif kind == "state":
        out_shape = state_shapes(rows, width)
    else:
        out_shape = jax.ShapeDtypeStruct((rows, steps, QH * HD), jnp.bfloat16)
        scratch += running + [pltpu.VMEM((2 * KVH, width, HD), jnp.float32)]
    scratch += [
        pltpu.VMEM((count, 2, cap, BLK, feature), jnp.bfloat16),
        pltpu.VMEM((room, feature), jnp.float32),
        pltpu.VMEM((room, feature), jnp.float32),
        pltpu.SemaphoreType.DMA((count + 3,)),
    ]
    return pl.pallas_call(
        functools.partial(span_kernel, kind, kernel, count, cap),
        out_shape=out_shape,
        in_specs=[smem] * 7 + [vmem] * 5 + [hbm] * (count + len(state)) + [vmem] * len(extra),
        out_specs=jax.tree.map(lambda _: vmem, out_shape),
        scratch_shapes=scratch,
        compiler_params=pltpu.CompilerParams(vmem_limit_bytes=GRANT),
        cost_estimate=pl.CostEstimate(
            flops=10**9, bytes_accessed=12 * 2**20, transcendentals=10**6
        ),
    )(*scalars, grouped, *tables, *messages, *state, *extra)


PHASES = {"d": (2, 2, 2, 2), "f": (0, 3, 3, 0), "g": (3, 0, 0, 3), "b": (1, 1, 1, 1)}


def site_plane(plane, flip):
    dest = plane ^ flip
    half = PLANES // 2
    if (plane < half) != (dest < half) and dest in (half - 1, half):
        return PLANES - 1 - dest
    return dest


def came_from(phase, plane):
    flips = PHASES[phase]
    return next(s for s in range(PLANES) if site_plane(s, flips[s]) == plane)


def for_mirror(phase, plane):
    source = came_from(phase, plane)
    return int(source ^ PHASES[phase][source] != plane)


def route(n, phase, offset):
    in_plane = n // PLANES
    return [
        (
            plane * in_plane + place,
            site_plane(plane, flip) * in_plane + (place + offset) % in_plane,
        )
        for plane, flip in enumerate(PHASES[phase])
        for place in range(in_plane)
    ]


STAGE = {"d": 1, "f": 1, "g": 1, "b": 2}


def device_tables(n):
    in_plane = n // PLANES
    lines = []
    for me in range(n):
        plane, place = me // in_plane, me % in_plane
        entry, stage = [], []
        post = [[-1] * n, [-1] * n]
        for phase in PHASES:
            mirror = for_mirror(phase, plane)
            for offset in range(in_plane):
                source = came_from(phase, plane) * in_plane + (place - offset) % in_plane
                entry.append(mirror * n + source)
                stage.append(0 if mirror else STAGE[phase])
                post[mirror][source] = stage[-1]
        lines.append((entry, stage, post[0], post[1]))
    return np.array(lines, np.int32)


def body(
    span_keys,
    span_values,
    block_device,
    block_row,
    cache_len,
    cache_keys,
    cache_values,
    queries,
    step_keys,
    step_values,
):
    n = lax.axis_size("seq")
    in_plane = n // PLANES
    me = lax.axis_index("seq").astype(jnp.int32)
    rows = cache_len.shape[0]
    feature = span_keys.shape[1]
    blocks = span_keys.shape[0] // BLK
    cap = max(2, (2 * blocks + n - 1) // n)
    steps = queries.shape[1]
    group = QH // KVH
    names = list(PHASES)

    phase_table = jnp.array(
        [
            [next(i for i, p in enumerate(names) if PHASES[p][z] == z ^ d) for d in range(PLANES)]
            for z in range(PLANES)
        ],
        jnp.int32,
    )
    notes, *messages = pack(
        n,
        cap,
        phase_table,
        block_device[:, 0],
        block_row,
        cache_len,
        span_keys.reshape(blocks, BLK, feature),
        span_values.reshape(blocks, BLK, feature),
    )
    packed = {p: messages[i * in_plane : (i + 1) * in_plane] for i, p in enumerate(names)}

    grouped = (
        queries.reshape(rows, steps, KVH, group, HD)
        .transpose(0, 2, 1, 3, 4)
        .reshape(rows, KVH, steps * group, HD)
    )
    half = PLANES // 2
    swap = [
        (a * in_plane + i, b * in_plane + i)
        for a, b in ((half - 1, half), (half, half - 1))
        for i in range(in_plane)
    ]
    mirrored = lax.ppermute(grouped, "seq", swap)

    def send(phase, after=None):
        out = []
        for offset in range(in_plane):
            value = packed[phase][offset]
            if after is not None:
                value, after[offset] = lax.optimization_barrier((value, after[offset]))
            pairs = route(n, phase, offset)
            if any(a != b for a, b in pairs):
                value = lax.ppermute(value, "seq", pairs)
            out.append(value)
        return out

    got = {}
    got["d"] = send("d")
    got["f"] = send("f")
    got["g"] = send("g")
    got["b"] = send("b", got["d"])

    notes = lax.all_to_all(notes, "seq", split_axis=0, concat_axis=0, tiled=True)
    mine = lax.dynamic_index_in_dim(jnp.array(device_tables(n)), me, 0, keepdims=False)
    *slots, tally = index(n, cap, rows, notes, mine[2:])
    twin = [m if m // in_plane in (0, PLANES - 1) else (PLANES - 1 - m // in_plane) * in_plane
            + m % in_plane for m in range(n)]
    twin = jnp.sum(jnp.where(jnp.arange(n) == me, jnp.array(twin, jnp.int32), 0))
    mirror_len = lax.dynamic_index_in_dim(notes, twin, 0, keepdims=False)
    mirror_len = mirror_len[2 * LANES : 2 * LANES + rows]

    own_tables = turn_tables(cache_len[:, None] + jnp.arange(BLK, dtype=jnp.int32)[None])
    mirror_tables = turn_tables(mirror_len[:, None] + jnp.arange(BLK, dtype=jnp.int32)[None])
    rank_tables = turn_tables(jnp.arange(n * cap, dtype=jnp.int32) * BLK)

    def scalars(phases):
        first = names.index(phases[0]) * in_plane
        picked = mine[:2, first : first + len(phases) * in_plane]
        return (picked[0], picked[1], *slots, tally)

    state = resident(cache_len, grouped, step_keys, step_values, cache_keys, cache_values)
    partial, stats = span(
        "partial", 0, cap, scalars("df"), mirrored,
        mirror_tables + rank_tables, got["d"] + got["f"], (), (), steps,
    )
    partial = lax.ppermute(partial, "seq", swap)
    stats = lax.ppermute(stats, "seq", swap)
    state = span(
        "state", 1, cap, scalars("dfg"), grouped,
        own_tables + rank_tables, got["d"] + got["f"] + got["g"], tuple(state), (), steps,
    )
    return span(
        "final", 2, cap, scalars("b"), grouped,
        own_tables + rank_tables, got["b"], tuple(state), (partial, stats), steps,
    )


def solution(mesh):
    placed = (
        P(("groups", "seq"), None),
        P(("groups", "seq"), None),
        P(("groups", "seq"), None),
        P(("groups", "seq")),
        P(("groups", "seq")),
        P(("groups", "seq"), None, None),
        P(("groups", "seq"), None, None),
        P(("groups", "seq"), None, None),
        P(("groups", "seq"), None, None),
        P(("groups", "seq"), None, None),
    )

    return jax.shard_map(
        body,
        mesh=mesh,
        in_specs=placed,
        out_specs=P(("groups", "seq"), None, None),
        check_vma=False,
    )
```

```python
import functools

import jax
import jax.numpy as jnp
import numpy as np
from jax import lax
from jax.experimental import pallas as pl
from jax.experimental.pallas import tpu as pltpu
from jax.sharding import PartitionSpec as P


KVH = 4
QH = 64
HD = 128
BLK = 8
PLANES = 4
CHUNK = 256
SPAN = 128
LANES = 128
GRANT = 20 * 2**20
UNROLL = 4
NEG = -1e30


def frequencies(half_width):
    freq_index = jnp.arange(half_width, dtype=jnp.float32)
    base_freq = 1.0 / 500000.0 ** (freq_index / half_width)
    wavelen = 2.0 * jnp.pi / base_freq
    smooth = (8192.0 / wavelen - 1.0) / 3.0
    blended = (1.0 - smooth) * base_freq / 8.0 + smooth * base_freq
    scaled = jnp.where(wavelen > 8192.0, base_freq / 8.0, blended)
    return jnp.where(wavelen < 2048.0, base_freq, scaled)


def turn_tables(positions):
    freq = frequencies(HD // 2)
    angles = positions.astype(jnp.float32)[..., None] * jnp.concatenate([freq, freq])
    sign = jnp.where(jnp.arange(HD) < HD // 2, -1.0, 1.0).astype(jnp.float32)
    return jnp.cos(angles), jnp.sin(angles) * sign


def pack_kernel(n, cap, phase_table, target, rows, lens, keys, values, *refs):
    notes = refs[0]
    outs = refs[1 : 1 + n]
    slots, fill, rel, sems = refs[1 + n :]
    blocks = keys.shape[0]
    in_plane = n // PLANES
    me = lax.axis_index("seq")
    plane, place = me // in_plane, me % in_plane

    def clear(i, _):
        fill[i] = 0
        offset = (i % in_plane - place + in_plane) % in_plane
        rel[i] = phase_table[plane, i // in_plane] * in_plane + offset
        for k in range(cap):
            notes[i, k] = -1
            notes[i, LANES + k] = -1
        for k in range(lens.shape[0]):
            notes[i, 2 * LANES + k] = lens[k]
        return 0

    lax.fori_loop(0, n, clear, 0)

    def put(b, _):
        dest = target[b]
        slot = fill[dest]
        fill[dest] = slot + 1
        row = rows[b]
        dest_plane = dest // in_plane
        inner = (dest_plane > 0) & (dest_plane < PLANES - 1)
        twin = jnp.where(inner, (PLANES - 1 - 2 * dest_plane) * in_plane + dest, dest)
        notes[dest, slot] = row
        notes[twin, LANES + slot] = row
        message = rel[dest]
        slots[message, 0, slot] = keys[b]
        slots[message, 1, slot] = values[b]
        return 0

    lax.fori_loop(0, blocks, put, 0, unroll=4)
    copies = [pltpu.make_async_copy(slots.at[i], outs[i], sems.at[i]) for i in range(n)]
    for copy in copies:
        copy.start()
    for copy in copies:
        copy.wait()


def pack(n, cap, phase_table, target, rows, lens, keys, values):
    width = keys.shape[-1]
    message = jax.ShapeDtypeStruct((2, cap, BLK, width), jnp.bfloat16)
    smem = pl.BlockSpec(memory_space=pltpu.SMEM)
    vmem = pl.BlockSpec(memory_space=pltpu.VMEM)
    return pl.pallas_call(
        functools.partial(pack_kernel, n, cap),
        out_shape=(jax.ShapeDtypeStruct((n, 3 * LANES), jnp.int32),) + (message,) * n,
        in_specs=[smem] * 4 + [vmem] * 2,
        out_specs=(smem,) + (pl.BlockSpec(memory_space=pl.ANY),) * n,
        scratch_shapes=[
            pltpu.VMEM((n, 2, cap, BLK, width), jnp.bfloat16),
            pltpu.SMEM((n,), jnp.int32),
            pltpu.SMEM((n,), jnp.int32),
            pltpu.SemaphoreType.DMA((n,)),
        ],
        name="pack",
    )(phase_table, target, rows, lens, keys, values)


def index_kernel(n, cap, rows, notes, stages, place, row_of, rank_of, used, tally):
    f32 = jnp.float32

    def iotas(shape):
        return [lax.broadcasted_iota(jnp.int32, shape, d) for d in (0, 1)]

    a, b = iotas((cap, cap))
    before = (a < b).astype(f32)
    a, b = iotas((n, n))
    sooner = (b < a).astype(f32)
    lines = [jnp.broadcast_to(stages[i : i + 1, :n], (n, n)) for i in range(2)]
    posts = [
        jnp.sum(jnp.where(a == b, line, 0), axis=1, keepdims=True) for line in lines
    ]
    mates = [jnp.where(line == post, sooner, 0.0) for line, post in zip(lines, posts)]
    kernel, lane = iotas((8, LANES))
    counts = jnp.zeros((8, LANES), f32)
    for side in range(2):
        rows_here = notes[:, side * LANES : side * LANES + cap]
        rank = jnp.zeros((n, cap), f32)
        local = jnp.zeros((n, cap), f32)
        for r in range(rows):
            hit = (rows_here == r).astype(f32)
            inside = jnp.dot(hit, before, preferred_element_type=f32)
            ahead = jnp.dot(sooner, hit, preferred_element_type=f32)
            near = jnp.dot(mates[side], hit, preferred_element_type=f32)
            rank += hit * (inside + jnp.sum(ahead, axis=1, keepdims=True))
            local += hit * (inside + jnp.sum(near, axis=1, keepdims=True))
            per_source = jnp.sum(hit, axis=1, keepdims=True)
            for stage in range(3):
                if (stage == 0) == (side == 1):
                    number = jnp.sum(
                        jnp.where(posts[side] == stage, per_source, 0.0), axis=0, keepdims=True
                    )
                    counts += jnp.where((kernel == stage) & (lane == r), number, 0.0)
        span = slice(side * n, side * n + n)
        valid = rows_here >= 0
        place[span, :] = jnp.where(valid, local, -1.0).astype(jnp.int32)
        row_of[span, :] = jnp.maximum(rows_here, 0)
        rank_of[span, :] = rank.astype(jnp.int32)
        filled = jnp.sum(valid.astype(f32), axis=1, keepdims=True)
        used[span, :] = jnp.broadcast_to(filled, (n, cap)).astype(jnp.int32)
    a, b = iotas((LANES, LANES))
    begin = jnp.dot(counts, (a < b).astype(f32), preferred_element_type=f32)
    tally[0:8, :] = begin.astype(jnp.int32)
    tally[8:16, :] = (counts * BLK).astype(jnp.int32)


def index(n, cap, rows, notes, stages):
    vmem = pl.BlockSpec(memory_space=pltpu.VMEM)
    slots = jax.ShapeDtypeStruct((2 * n, cap), jnp.int32)
    return pl.pallas_call(
        functools.partial(index_kernel, n, cap, rows),
        out_shape=(slots,) * 4 + (jax.ShapeDtypeStruct((16, LANES), jnp.int32),),
        in_specs=[vmem] * 2,
        out_specs=(vmem,) * 5,
        compiler_params=pltpu.CompilerParams(vmem_limit_bytes=GRANT),
        name="index",
    )(notes, stages)


def blend(queries, pieces, old, guard=False):
    scale = HD ** (-0.5)
    heads = range(KVH)
    scores = [
        [
            jnp.where(
                piece[2],
                lax.dot_general(
                    queries[head],
                    piece[0][head],
                    (((1,), (1,)), ((), ())),
                    preferred_element_type=jnp.float32,
                )
                * scale,
                NEG,
            )
            for piece in pieces
        ]
        for head in heads
    ]
    new = []
    for head in heads:
        peak = functools.reduce(
            jnp.maximum, [jnp.max(one, axis=-1, keepdims=True) for one in scores[head]]
        )
        if old is None:
            new_top = jnp.broadcast_to(peak, (peak.shape[0], HD))
        else:
            old_acc, old_top, old_total = old[head]
            new_top = jnp.maximum(old_top, peak)
        raw = [jnp.exp(one - new_top[:, :1]) for one in scores[head]]
        if guard:
            raw = [jnp.where(piece[2], one, 0.0) for piece, one in zip(pieces, raw)]
        added = sum(jnp.sum(one, axis=-1, keepdims=True) for one in raw)
        mixed = sum(
            jnp.dot(one.astype(jnp.bfloat16), piece[1][head], preferred_element_type=jnp.float32)
            for one, piece in zip(raw, pieces)
        )
        if old is None:
            new.append((mixed, new_top, jnp.broadcast_to(added, new_top.shape)))
        else:
            factor = jnp.exp(old_top - new_top)
            new.append((old_acc * factor + mixed, new_top, old_total * factor + added))
    return new


def held(row, state):
    return [tuple(one[row, head] for one in state) for head in range(KVH)]


def hold(row, state, new):
    for head in range(KVH):
        for one, value in zip(state, new[head]):
            one[row, head] = value


def row_queries(row, q_ref):
    return [q_ref[row, head] for head in range(KVH)]


def resident_kernel(
    lens, q_ref, step_k, step_v, keys, values, acc, top, total, kbuf, vbuf, sems
):
    rows, slot_count = kbuf.shape[0], kbuf.shape[1]
    piece = min(CHUNK, slot_count)
    pieces = slot_count // piece
    steps = step_k.shape[1]
    width = q_ref.shape[2]
    group = width // steps

    def copies(r, i):
        part = pl.ds(i * piece, piece)
        return (
            pltpu.make_async_copy(keys.at[r, part], kbuf.at[r, part], sems.at[0, r, i]),
            pltpu.make_async_copy(values.at[r, part], vbuf.at[r, part], sems.at[1, r, i]),
        )

    def fetch(r, _):
        for i in range(pieces):

            @pl.when((i == 0) | (i * piece < lens[r]))
            def _():
                for copy in copies(r, i):
                    copy.start()

        return 0

    lax.fori_loop(0, rows, fetch, 0)
    lane = lax.broadcasted_iota(jnp.int32, (width, piece), 1)
    causal = (
        lax.broadcasted_iota(jnp.int32, (width, steps), 1)
        <= lax.broadcasted_iota(jnp.int32, (width, steps), 0) // group
    )

    def one_row(r, _):
        def part(i):
            span = pl.ds(i * piece, piece)
            return (
                [kbuf[r, span, head * HD : (head + 1) * HD] for head in range(KVH)],
                [vbuf[r, span, head * HD : (head + 1) * HD] for head in range(KVH)],
                lane + i * piece < lens[r],
            )

        own = (
            [step_k[r, :, head * HD : (head + 1) * HD] for head in range(KVH)],
            [step_v[r, :, head * HD : (head + 1) * HD] for head in range(KVH)],
            causal,
        )
        state = (acc, top, total)
        for copy in copies(r, 0):
            copy.wait()
        hold(r, state, blend(row_queries(r, q_ref), [own, part(0)], None))
        for i in range(1, pieces):

            @pl.when(i * piece < lens[r])
            def _():
                for copy in copies(r, i):
                    copy.wait()
                hold(r, state, blend(row_queries(r, q_ref), [part(i)], held(r, state)))

        return 0

    lax.fori_loop(0, rows, one_row, 0)


def state_shapes(rows, width):
    shape = jax.ShapeDtypeStruct((rows, KVH, width, HD), jnp.float32)
    return (shape,) * 3


def resident(lens, grouped, step_k, step_v, keys, values):
    rows, slot_count, feature = keys.shape
    pieces = slot_count // min(CHUNK, slot_count)
    vmem = pl.BlockSpec(memory_space=pltpu.VMEM)
    hbm = pl.BlockSpec(memory_space=pl.ANY)
    return pl.pallas_call(
        resident_kernel,
        out_shape=state_shapes(rows, grouped.shape[2]),
        in_specs=[pl.BlockSpec(memory_space=pltpu.SMEM), vmem, vmem, vmem, hbm, hbm],
        out_specs=(vmem,) * 3,
        scratch_shapes=[
            pltpu.VMEM((rows, slot_count, feature), jnp.bfloat16),
            pltpu.VMEM((rows, slot_count, feature), jnp.bfloat16),
            pltpu.SemaphoreType.DMA((2, rows, pieces)),
        ],
        compiler_params=pltpu.CompilerParams(vmem_limit_bytes=GRANT),
        cost_estimate=pl.CostEstimate(
            flops=2 * 10**9, bytes_accessed=16 * 2**20, transcendentals=10**6
        ),
        name="resident",
    )(lens, grouped, step_k, step_v, keys, values)


def span_kernel(
    kind, kernel, count, cap, entry, stage, place_of, row_of, rank_of, used, tally,
    q_ref, ca, sa, cb, sb, *refs,
):
    messages = refs[:count]
    refs = refs[count:]
    before = refs[:3]
    if kind == "partial":
        out, stats, acc, top, total, kbuf, vbuf = refs
    elif kind == "state":
        part, stats, acc, top, total, kbuf, vbuf = refs[3:]
    else:
        out, acc, top, total, scr, kbuf, vbuf = refs[3:]
    state = (acc, top, total)
    rows = q_ref.shape[0]
    width = q_ref.shape[2]
    feature = kbuf.shape[1]
    last = tally[kernel, rows - 1] * BLK + tally[8 + kernel, rows - 1]
    tail = pl.ds(pl.multiple_of(last, BLK), SPAN)
    vbuf[tail, :] = jnp.zeros((SPAN, feature), jnp.float32)
    unroll = min(UNROLL, cap)
    trash = count * cap + SPAN // BLK
    for j in range(count):

        @pl.when(stage[j] == kernel)
        def _():
            source = entry[j]
            message = messages[j]

            def place(step, _):
                ready = []
                for u in range(unroll):
                    k = step * unroll + u
                    r = row_of[source, k]
                    rank = rank_of[source, k]
                    local = place_of[source, k]
                    slot = jnp.where(local < 0, trash, tally[kernel, r] + local)
                    c_a, s_a = ca[r], sa[r]
                    c_b, s_b = cb[pl.ds(rank, 1), :], sb[pl.ds(rank, 1), :]
                    cosine = c_a * c_b - s_a * s_b
                    sine = s_a * c_b + c_a * s_b
                    where = pl.ds(pl.multiple_of(slot * BLK, BLK), BLK)
                    value = message[1, k].astype(jnp.float32)
                    key = message[0, k].astype(jnp.float32)
                    turned = []
                    for head in range(KVH):
                        piece = key[:, head * HD : (head + 1) * HD]
                        turned.append(piece * cosine + pltpu.roll(piece, HD // 2, 1) * sine)
                    ready.append((where, turned, value))
                for where, turned, value in ready:
                    vbuf[where, :] = value
                    for head in range(KVH):
                        kbuf[where, head * HD : (head + 1) * HD] = turned[head]
                return 0

            lax.fori_loop(0, (used[source, 0] + unroll - 1) // unroll, place, 0)

    lane = lax.broadcasted_iota(jnp.int32, (width, SPAN), 1)
    eye = lax.broadcasted_iota(jnp.int32, (width, width), 0) == lax.broadcasted_iota(
        jnp.int32, (width, width), 1
    )

    def block(r, i):
        where = pl.ds(pl.multiple_of(tally[kernel, r] * BLK + i * SPAN, BLK), SPAN)
        return (
            [kbuf[where, h * HD : (h + 1) * HD].astype(jnp.bfloat16) for h in range(KVH)],
            [vbuf[where, h * HD : (h + 1) * HD].astype(jnp.bfloat16) for h in range(KVH)],
            lane + i * SPAN < tally[8 + kernel, r],
        )

    def beyond(r):
        def piece(i, _):
            hold(r, state, blend(row_queries(r, q_ref), [block(r, i)], held(r, state)))
            return 0

        lax.fori_loop(1, (tally[8 + kernel, r] + SPAN - 1) // SPAN, piece, 0)

    def partial_rows(pair):
        new = [blend(row_queries(r, q_ref), [block(r, 0)], None, guard=True) for r in pair]
        for r, one in zip(pair, new):
            hold(r, state, one)
        for r in pair:
            beyond(r)
        done = []
        for r in pair:
            for head in range(KVH):
                amount = total[r, head]
                safe = jnp.where(amount > 0.0, amount, 1.0)
                lines = [
                    jnp.sum(jnp.where(eye, one[:, :width], 0.0), axis=0, keepdims=True)
                    for one in (top[r, head], amount)
                ]
                done.append((r, head, (acc[r, head] / safe).astype(jnp.bfloat16), lines))
        for r, head, value, lines in done:
            out[r, head] = value
            for i in range(2):
                stats[r, head, pl.ds(i, 1), :] = lines[i]

    def with_part(r, new):
        merged = []
        for head in range(KVH):
            lines = []
            for i in range(2):
                line = jnp.broadcast_to(stats[r, head, pl.ds(i, 1), :], (width, width))
                lines.append(jnp.sum(jnp.where(eye, line, 0.0), axis=1, keepdims=True))
            other_top, other_total = lines
            other_top = jnp.where(other_total > 0.0, other_top, NEG)
            value, old_top, amount = new[head]
            new_top = jnp.maximum(old_top, other_top)
            mine = jnp.exp(old_top - new_top)
            theirs = jnp.exp(other_top - new_top) * other_total
            merged.append(
                (
                    value * mine + part[r, head].astype(jnp.float32) * theirs,
                    new_top,
                    amount * mine + theirs,
                )
            )
        return merged

    def state_rows(pair):
        new = [blend(row_queries(r, q_ref), [block(r, 0)], held(r, before)) for r in pair]
        new = [with_part(r, one) for r, one in zip(pair, new)]
        for r, one in zip(pair, new):
            hold(r, state, one)
        for r in pair:
            beyond(r)

    def put_out(pair, new):
        done = [value / amount for one in new for value, _, amount in one]
        for i, value in enumerate(done):
            scr[i] = value
        steps = out.shape[1]
        group = width // steps
        for i, r in enumerate(pair):
            for head in range(KVH):
                for g in range(group):
                    column = (head * group + g) * HD
                    out[r, :, column : column + HD] = scr[
                        i * KVH + head, pl.ds(g, steps, stride=group), :
                    ].astype(jnp.bfloat16)

    def final_rows(pair):
        new = [blend(row_queries(r, q_ref), [block(r, 0)], held(r, before)) for r in pair]
        put_out(pair, new)
        longest = functools.reduce(jnp.maximum, [tally[8 + kernel, r] for r in pair])

        @pl.when(longest > SPAN)
        def _():
            for r, one in zip(pair, new):
                hold(r, state, one)
            for r in pair:
                beyond(r)
            put_out(pair, [held(r, state) for r in pair])

    run = {"partial": partial_rows, "state": state_rows, "final": final_rows}[kind]
    together = 2 if rows % 2 == 0 else 1

    def some_rows(i, _):
        run([i * together + u for u in range(together)])
        return 0

    lax.fori_loop(0, rows // together, some_rows, 0)


def span(kind, kernel, cap, scalars, grouped, tables, messages, state, extra, steps):
    rows, _, width, _ = grouped.shape
    feature = messages[0].shape[-1]
    count = len(messages)
    room = (count * cap + 1) * BLK + SPAN
    smem = pl.BlockSpec(memory_space=pltpu.SMEM)
    vmem = pl.BlockSpec(memory_space=pltpu.VMEM)
    running = [pltpu.VMEM((rows, KVH, width, HD), jnp.float32)] * 3
    scratch = []
    if kind == "partial":
        out_shape = (
            jax.ShapeDtypeStruct((rows, KVH, width, HD), jnp.bfloat16),
            jax.ShapeDtypeStruct((rows, KVH, 2, width), jnp.float32),
        )
        scratch += running
    elif kind == "state":
        out_shape = state_shapes(rows, width)
    else:
        out_shape = jax.ShapeDtypeStruct((rows, steps, QH * HD), jnp.bfloat16)
        scratch += running + [pltpu.VMEM((2 * KVH, width, HD), jnp.float32)]
    scratch += [pltpu.VMEM((room, feature), jnp.float32)] * 2
    return pl.pallas_call(
        functools.partial(span_kernel, kind, kernel, count, cap),
        out_shape=out_shape,
        in_specs=[smem] * 7 + [vmem] * (5 + count + len(state) + len(extra)),
        out_specs=jax.tree.map(lambda _: vmem, out_shape),
        scratch_shapes=scratch,
        compiler_params=pltpu.CompilerParams(vmem_limit_bytes=GRANT),
        cost_estimate=pl.CostEstimate(
            flops=10**9, bytes_accessed=12 * 2**20, transcendentals=10**6
        ),
    )(*scalars, grouped, *tables, *messages, *state, *extra)


PHASES = {"d": (2, 2, 2, 2), "f": (0, 3, 3, 0), "g": (3, 0, 0, 3), "b": (1, 1, 1, 1)}


def site_plane(plane, flip):
    dest = plane ^ flip
    half = PLANES // 2
    if (plane < half) != (dest < half) and dest in (half - 1, half):
        return PLANES - 1 - dest
    return dest


def came_from(phase, plane):
    flips = PHASES[phase]
    return next(s for s in range(PLANES) if site_plane(s, flips[s]) == plane)


def for_mirror(phase, plane):
    source = came_from(phase, plane)
    return int(source ^ PHASES[phase][source] != plane)


def route(n, phase, offset):
    in_plane = n // PLANES
    return [
        (
            plane * in_plane + place,
            site_plane(plane, flip) * in_plane + (place + offset) % in_plane,
        )
        for plane, flip in enumerate(PHASES[phase])
        for place in range(in_plane)
    ]


STAGE = {"d": 1, "f": 1, "g": 1, "b": 2}


def device_tables(n):
    in_plane = n // PLANES
    lines = []
    for me in range(n):
        plane, place = me // in_plane, me % in_plane
        entry, stage = [], []
        post = [[-1] * n, [-1] * n]
        for phase in PHASES:
            mirror = for_mirror(phase, plane)
            for offset in range(in_plane):
                source = came_from(phase, plane) * in_plane + (place - offset) % in_plane
                entry.append(mirror * n + source)
                stage.append(0 if mirror else STAGE[phase])
                post[mirror][source] = stage[-1]
        lines.append((entry, stage, post[0], post[1]))
    return np.array(lines, np.int32)


def body(
    span_keys,
    span_values,
    block_device,
    block_row,
    cache_len,
    cache_keys,
    cache_values,
    queries,
    step_keys,
    step_values,
):
    n = lax.axis_size("seq")
    in_plane = n // PLANES
    me = lax.axis_index("seq").astype(jnp.int32)
    rows = cache_len.shape[0]
    feature = span_keys.shape[1]
    blocks = span_keys.shape[0] // BLK
    cap = max(2, (2 * blocks + n - 1) // n)
    steps = queries.shape[1]
    group = QH // KVH
    names = list(PHASES)

    phase_table = jnp.array(
        [
            [next(i for i, p in enumerate(names) if PHASES[p][z] == z ^ d) for d in range(PLANES)]
            for z in range(PLANES)
        ],
        jnp.int32,
    )
    notes, *messages = pack(
        n,
        cap,
        phase_table,
        block_device[:, 0],
        block_row,
        cache_len,
        span_keys.reshape(blocks, BLK, feature),
        span_values.reshape(blocks, BLK, feature),
    )
    packed = {p: messages[i * in_plane : (i + 1) * in_plane] for i, p in enumerate(names)}

    grouped = (
        queries.reshape(rows, steps, KVH, group, HD)
        .transpose(0, 2, 1, 3, 4)
        .reshape(rows, KVH, steps * group, HD)
    )
    half = PLANES // 2
    swap = [
        (a * in_plane + i, b * in_plane + i)
        for a, b in ((half - 1, half), (half, half - 1))
        for i in range(in_plane)
    ]
    mirrored = lax.ppermute(grouped, "seq", swap)

    def send(phase, after=None):
        out = []
        for offset in range(in_plane):
            value = packed[phase][offset]
            if after is not None:
                value, after[offset] = lax.optimization_barrier((value, after[offset]))
            pairs = route(n, phase, offset)
            if any(a != b for a, b in pairs):
                value = lax.ppermute(value, "seq", pairs)
            out.append(value)
        return out

    got = {}
    got["d"] = send("d")
    got["f"] = send("f")
    got["g"] = send("g")
    got["b"] = send("b", got["d"])

    notes = lax.all_to_all(notes, "seq", split_axis=0, concat_axis=0, tiled=True)
    mine = lax.dynamic_index_in_dim(jnp.array(device_tables(n)), me, 0, keepdims=False)
    *slots, tally = index(n, cap, rows, notes, mine[2:])
    twin = [m if m // in_plane in (0, PLANES - 1) else (PLANES - 1 - m // in_plane) * in_plane
            + m % in_plane for m in range(n)]
    twin = jnp.sum(jnp.where(jnp.arange(n) == me, jnp.array(twin, jnp.int32), 0))
    mirror_len = lax.dynamic_index_in_dim(notes, twin, 0, keepdims=False)
    mirror_len = mirror_len[2 * LANES : 2 * LANES + rows]

    own_tables = turn_tables(cache_len[:, None] + jnp.arange(BLK, dtype=jnp.int32)[None])
    mirror_tables = turn_tables(mirror_len[:, None] + jnp.arange(BLK, dtype=jnp.int32)[None])
    rank_tables = turn_tables(jnp.arange(n * cap, dtype=jnp.int32) * BLK)

    def scalars(phases):
        first = names.index(phases[0]) * in_plane
        picked = mine[:2, first : first + len(phases) * in_plane]
        return (picked[0], picked[1], *slots, tally)

    state = resident(cache_len, grouped, step_keys, step_values, cache_keys, cache_values)
    partial, stats = span(
        "partial", 0, cap, scalars("df"), mirrored,
        mirror_tables + rank_tables, got["d"] + got["f"], (), (), steps,
    )
    partial = lax.ppermute(partial, "seq", swap)
    stats = lax.ppermute(stats, "seq", swap)
    state = span(
        "state", 1, cap, scalars("dfg"), grouped,
        own_tables + rank_tables, got["d"] + got["f"] + got["g"], tuple(state),
        (partial, stats), steps,
    )
    return span(
        "final", 2, cap, scalars("b"), grouped,
        own_tables + rank_tables, got["b"], tuple(state), (), steps,
    )


def solution(mesh):
    placed = (
        P(("groups", "seq"), None),
        P(("groups", "seq"), None),
        P(("groups", "seq"), None),
        P(("groups", "seq")),
        P(("groups", "seq")),
        P(("groups", "seq"), None, None),
        P(("groups", "seq"), None, None),
        P(("groups", "seq"), None, None),
        P(("groups", "seq"), None, None),
        P(("groups", "seq"), None, None),
    )

    return jax.shard_map(
        body,
        mesh=mesh,
        in_specs=placed,
        out_specs=P(("groups", "seq"), None, None),
        check_vma=False,
    )
```

```python
import functools

import jax
import jax.numpy as jnp
import numpy as np
from jax import lax
from jax.experimental import pallas as pl
from jax.experimental.pallas import tpu as pltpu
from jax.sharding import PartitionSpec as P


KVH = 4
QH = 64
HD = 128
BLK = 8
PLANES = 4
CHUNK = 256
SPAN = 128
LANES = 128
GRANT = 20 * 2**20
UNROLL = 4
PACKED = 4
NEG = -1e30


def frequencies(half_width):
    freq_index = jnp.arange(half_width, dtype=jnp.float32)
    base_freq = 1.0 / 500000.0 ** (freq_index / half_width)
    wavelen = 2.0 * jnp.pi / base_freq
    smooth = (8192.0 / wavelen - 1.0) / 3.0
    blended = (1.0 - smooth) * base_freq / 8.0 + smooth * base_freq
    scaled = jnp.where(wavelen > 8192.0, base_freq / 8.0, blended)
    return jnp.where(wavelen < 2048.0, base_freq, scaled)


def turn_tables(positions):
    freq = frequencies(HD // 2)
    angles = positions.astype(jnp.float32)[..., None] * jnp.concatenate([freq, freq])
    sign = jnp.where(jnp.arange(HD) < HD // 2, -1.0, 1.0).astype(jnp.float32)
    return jnp.cos(angles), jnp.sin(angles) * sign


def pack_kernel(n, phase_table, target, keys, values, *refs):
    outs = refs[:n]
    slots, fill, rel, sems = refs[n:]
    blocks = keys.shape[0]
    in_plane = n // PLANES
    me = lax.axis_index("seq")
    plane, place = me // in_plane, me % in_plane

    def clear(p, _):
        for i in range(in_plane):
            fill[p * in_plane + i] = 0
            offset = i - place
            offset = jnp.where(offset < 0, offset + in_plane, offset)
            rel[p * in_plane + i] = phase_table[plane, p] * in_plane + offset
        return 0

    lax.fori_loop(0, PLANES, clear, 0)

    def put(step, _):
        ready = []
        for u in range(PACKED):
            b = step * PACKED + u
            dest = target[b]
            slot = fill[dest]
            fill[dest] = slot + 1
            ready.append((b, rel[dest], slot))
        for b, message, slot in ready:
            slots[message, 0, slot] = keys[b]
            slots[message, 1, slot] = values[b]
        return 0

    lax.fori_loop(0, blocks // PACKED, put, 0)
    copies = [pltpu.make_async_copy(slots.at[i], outs[i], sems.at[i]) for i in range(n)]
    for copy in copies:
        copy.start()
    for copy in copies:
        copy.wait()


def pack(n, cap, phase_table, target, keys, values):
    width = keys.shape[-1]
    message = jax.ShapeDtypeStruct((2, cap, BLK, width), jnp.bfloat16)
    smem = pl.BlockSpec(memory_space=pltpu.SMEM)
    vmem = pl.BlockSpec(memory_space=pltpu.VMEM)
    return pl.pallas_call(
        functools.partial(pack_kernel, n),
        out_shape=(message,) * n,
        in_specs=[smem] * 2 + [vmem] * 2,
        out_specs=(pl.BlockSpec(memory_space=pl.ANY),) * n,
        scratch_shapes=[
            pltpu.VMEM((n, 2, cap, BLK, width), jnp.bfloat16),
            pltpu.SMEM((n,), jnp.int32),
            pltpu.SMEM((n,), jnp.int32),
            pltpu.SemaphoreType.DMA((n,)),
        ],
        name="pack",
    )(phase_table, target, keys, values)


def note_kernel(n, cap, target, rows, lens, notes, fill):
    in_plane = n // PLANES

    def clear(i, _):
        fill[i] = 0
        for k in range(cap):
            notes[i, k] = -1
            notes[i, LANES + k] = -1
        for k in range(lens.shape[0]):
            notes[i, 2 * LANES + k] = lens[k]
        return 0

    lax.fori_loop(0, n, clear, 0)

    def put(b, _):
        dest = target[b]
        slot = fill[dest]
        fill[dest] = slot + 1
        row = rows[b]
        dest_plane = dest // in_plane
        inner = (dest_plane > 0) & (dest_plane < PLANES - 1)
        twin = jnp.where(inner, (PLANES - 1 - 2 * dest_plane) * in_plane + dest, dest)
        notes[dest, slot] = row
        notes[twin, LANES + slot] = row
        return 0

    lax.fori_loop(0, rows.shape[0], put, 0, unroll=4)


def note(n, cap, target, rows, lens):
    smem = pl.BlockSpec(memory_space=pltpu.SMEM)
    return pl.pallas_call(
        functools.partial(note_kernel, n, cap),
        out_shape=jax.ShapeDtypeStruct((n, 3 * LANES), jnp.int32),
        in_specs=[smem] * 3,
        out_specs=smem,
        scratch_shapes=[pltpu.SMEM((n,), jnp.int32)],
        compiler_params=pltpu.CompilerParams(vmem_limit_bytes=GRANT),
        name="note",
    )(target, rows, lens)


def index_kernel(n, cap, rows, notes, stages, place, row_of, rank_of, used, tally):
    f32 = jnp.float32

    def iotas(shape):
        return [lax.broadcasted_iota(jnp.int32, shape, d) for d in (0, 1)]

    a, b = iotas((cap, cap))
    before = (a < b).astype(f32)
    a, b = iotas((n, n))
    sooner = (b < a).astype(f32)
    lines = [jnp.broadcast_to(stages[i : i + 1, :n], (n, n)) for i in range(2)]
    posts = [
        jnp.sum(jnp.where(a == b, line, 0), axis=1, keepdims=True) for line in lines
    ]
    mates = [jnp.where(line == post, sooner, 0.0) for line, post in zip(lines, posts)]
    kernel, lane = iotas((8, LANES))
    counts = jnp.zeros((8, LANES), f32)
    for side in range(2):
        rows_here = notes[:, side * LANES : side * LANES + cap]
        rank = jnp.zeros((n, cap), f32)
        local = jnp.zeros((n, cap), f32)
        for r in range(rows):
            hit = (rows_here == r).astype(f32)
            inside = jnp.dot(hit, before, preferred_element_type=f32)
            ahead = jnp.dot(sooner, hit, preferred_element_type=f32)
            near = jnp.dot(mates[side], hit, preferred_element_type=f32)
            rank += hit * (inside + jnp.sum(ahead, axis=1, keepdims=True))
            local += hit * (inside + jnp.sum(near, axis=1, keepdims=True))
            per_source = jnp.sum(hit, axis=1, keepdims=True)
            for stage in range(3):
                if (stage == 0) == (side == 1):
                    number = jnp.sum(
                        jnp.where(posts[side] == stage, per_source, 0.0), axis=0, keepdims=True
                    )
                    counts += jnp.where((kernel == stage) & (lane == r), number, 0.0)
        span = slice(side * n, side * n + n)
        valid = rows_here >= 0
        place[span, :] = jnp.where(valid, local, -1.0).astype(jnp.int32)
        row_of[span, :] = jnp.maximum(rows_here, 0)
        rank_of[span, :] = rank.astype(jnp.int32)
        filled = jnp.sum(valid.astype(f32), axis=1, keepdims=True)
        used[span, :] = jnp.broadcast_to(filled, (n, cap)).astype(jnp.int32)
    a, b = iotas((LANES, LANES))
    begin = jnp.dot(counts, (a < b).astype(f32), preferred_element_type=f32)
    tally[0:8, :] = begin.astype(jnp.int32)
    tally[8:16, :] = (counts * BLK).astype(jnp.int32)


def index(n, cap, rows, notes, stages):
    vmem = pl.BlockSpec(memory_space=pltpu.VMEM)
    slots = jax.ShapeDtypeStruct((2 * n, cap), jnp.int32)
    return pl.pallas_call(
        functools.partial(index_kernel, n, cap, rows),
        out_shape=(slots,) * 4 + (jax.ShapeDtypeStruct((16, LANES), jnp.int32),),
        in_specs=[vmem] * 2,
        out_specs=(vmem,) * 5,
        compiler_params=pltpu.CompilerParams(vmem_limit_bytes=GRANT),
        name="index",
    )(notes, stages)


def as_wide(line, width):
    if width % HD == 0:
        return jnp.concatenate([line] * (width // HD), axis=1)
    return line[:, :width]


def blend(queries, pieces, old, guard=False):
    scale = HD ** (-0.5)
    heads = range(KVH)
    scores = [
        [
            jnp.where(
                piece[2],
                lax.dot_general(
                    queries[head],
                    piece[0][head],
                    (((1,), (1,)), ((), ())),
                    preferred_element_type=jnp.float32,
                )
                * scale,
                NEG,
            )
            for piece in pieces
        ]
        for head in heads
    ]
    new = []
    for head in heads:
        peak = functools.reduce(
            jnp.maximum, [jnp.max(one, axis=-1, keepdims=True) for one in scores[head]]
        )
        if old is None:
            new_top = jnp.broadcast_to(peak, (peak.shape[0], HD))
        else:
            old_acc, old_top, old_total = old[head]
            new_top = jnp.maximum(old_top, peak)
        raw = [jnp.exp(one - as_wide(new_top, one.shape[1])) for one in scores[head]]
        if guard:
            raw = [jnp.where(piece[2], one, 0.0) for piece, one in zip(pieces, raw)]
        added = sum(jnp.sum(one, axis=-1, keepdims=True) for one in raw)
        mixed = sum(
            jnp.dot(one.astype(jnp.bfloat16), piece[1][head], preferred_element_type=jnp.float32)
            for one, piece in zip(raw, pieces)
        )
        if old is None:
            new.append((mixed, new_top, jnp.broadcast_to(added, new_top.shape)))
        else:
            factor = jnp.exp(old_top - new_top)
            new.append((old_acc * factor + mixed, new_top, old_total * factor + added))
    return new


def held(row, state):
    return [tuple(one[row, head] for one in state) for head in range(KVH)]


def hold(row, state, new):
    for head in range(KVH):
        for one, value in zip(state, new[head]):
            one[row, head] = value


def row_queries(row, q_ref):
    return [q_ref[row, head] for head in range(KVH)]


def resident_kernel(
    lens, q_ref, step_k, step_v, keys, values, acc, top, total, kbuf, vbuf, sems
):
    rows, slot_count = kbuf.shape[0], kbuf.shape[1]
    piece = min(CHUNK, slot_count)
    pieces = slot_count // piece
    steps = step_k.shape[1]
    width = q_ref.shape[2]
    group = width // steps

    def copies(r, i):
        part = pl.ds(i * piece, piece)
        return (
            pltpu.make_async_copy(keys.at[r, part], kbuf.at[r, part], sems.at[0, r, i]),
            pltpu.make_async_copy(values.at[r, part], vbuf.at[r, part], sems.at[1, r, i]),
        )

    def fetch(r, _):
        for i in range(pieces):

            @pl.when((i == 0) | (i * piece < lens[r]))
            def _():
                for copy in copies(r, i):
                    copy.start()

        return 0

    lax.fori_loop(0, rows, fetch, 0)
    lane = lax.broadcasted_iota(jnp.int32, (width, piece), 1)
    causal = (
        lax.broadcasted_iota(jnp.int32, (width, steps), 1)
        <= lax.broadcasted_iota(jnp.int32, (width, steps), 0) // group
    )

    def one_row(r, _):
        def part(i):
            span = pl.ds(i * piece, piece)
            return (
                [kbuf[r, span, head * HD : (head + 1) * HD] for head in range(KVH)],
                [vbuf[r, span, head * HD : (head + 1) * HD] for head in range(KVH)],
                lane + i * piece < lens[r],
            )

        own = (
            [step_k[r, :, head * HD : (head + 1) * HD] for head in range(KVH)],
            [step_v[r, :, head * HD : (head + 1) * HD] for head in range(KVH)],
            causal,
        )
        state = (acc, top, total)
        for copy in copies(r, 0):
            copy.wait()
        hold(r, state, blend(row_queries(r, q_ref), [own, part(0)], None))
        for i in range(1, pieces):

            @pl.when(i * piece < lens[r])
            def _():
                for copy in copies(r, i):
                    copy.wait()
                hold(r, state, blend(row_queries(r, q_ref), [part(i)], held(r, state)))

        return 0

    lax.fori_loop(0, rows, one_row, 0)


def state_shapes(rows, width):
    shape = jax.ShapeDtypeStruct((rows, KVH, width, HD), jnp.float32)
    return (shape,) * 3


def resident(lens, grouped, step_k, step_v, keys, values):
    rows, slot_count, feature = keys.shape
    pieces = slot_count // min(CHUNK, slot_count)
    vmem = pl.BlockSpec(memory_space=pltpu.VMEM)
    hbm = pl.BlockSpec(memory_space=pl.ANY)
    return pl.pallas_call(
        resident_kernel,
        out_shape=state_shapes(rows, grouped.shape[2]),
        in_specs=[pl.BlockSpec(memory_space=pltpu.SMEM), vmem, vmem, vmem, hbm, hbm],
        out_specs=(vmem,) * 3,
        scratch_shapes=[
            pltpu.VMEM((rows, slot_count, feature), jnp.bfloat16),
            pltpu.VMEM((rows, slot_count, feature), jnp.bfloat16),
            pltpu.SemaphoreType.DMA((2, rows, pieces)),
        ],
        compiler_params=pltpu.CompilerParams(vmem_limit_bytes=GRANT),
        cost_estimate=pl.CostEstimate(
            flops=2 * 10**9, bytes_accessed=16 * 2**20, transcendentals=10**6
        ),
        name="resident",
    )(lens, grouped, step_k, step_v, keys, values)


def span_kernel(
    kind, kernel, count, cap, entry, stage, place_of, row_of, rank_of, used, tally,
    q_ref, ca, sa, cb, sb, *refs,
):
    messages = refs[:count]
    refs = refs[count:]
    before = refs[:3]
    if kind == "partial":
        out, stats, acc, top, total, kbuf, vbuf = refs
    elif kind == "state":
        part, stats, acc, top, total, kbuf, vbuf = refs[3:]
    else:
        out, acc, top, total, scr, kbuf, vbuf = refs[3:]
    state = (acc, top, total)
    rows = q_ref.shape[0]
    width = q_ref.shape[2]
    feature = kbuf.shape[1]
    last = tally[kernel, rows - 1] * BLK + tally[8 + kernel, rows - 1]
    tail = pl.ds(pl.multiple_of(last, BLK), SPAN)
    vbuf[tail, :] = jnp.zeros((SPAN, feature), jnp.float32)
    unroll = min(UNROLL, cap)
    trash = count * cap + SPAN // BLK
    for j in range(count):

        @pl.when(stage[j] == kernel)
        def _():
            source = entry[j]
            message = messages[j]

            def place(step, _):
                ready = []
                for u in range(unroll):
                    k = step * unroll + u
                    r = row_of[source, k]
                    rank = rank_of[source, k]
                    local = place_of[source, k]
                    slot = jnp.where(local < 0, trash, tally[kernel, r] + local)
                    c_a, s_a = ca[r], sa[r]
                    c_b, s_b = cb[pl.ds(rank, 1), :], sb[pl.ds(rank, 1), :]
                    cosine = c_a * c_b - s_a * s_b
                    sine = s_a * c_b + c_a * s_b
                    where = pl.ds(pl.multiple_of(slot * BLK, BLK), BLK)
                    value = message[1, k].astype(jnp.float32)
                    key = message[0, k].astype(jnp.float32)
                    turned = []
                    for head in range(KVH):
                        piece = key[:, head * HD : (head + 1) * HD]
                        turned.append(piece * cosine + pltpu.roll(piece, HD // 2, 1) * sine)
                    ready.append((where, turned, value))
                for where, turned, value in ready:
                    vbuf[where, :] = value
                    for head in range(KVH):
                        kbuf[where, head * HD : (head + 1) * HD] = turned[head]
                return 0

            lax.fori_loop(0, (used[source, 0] + unroll - 1) // unroll, place, 0)

    lane = lax.broadcasted_iota(jnp.int32, (width, SPAN), 1)
    eye = lax.broadcasted_iota(jnp.int32, (width, width), 0) == lax.broadcasted_iota(
        jnp.int32, (width, width), 1
    )

    def block(r, i):
        where = pl.ds(pl.multiple_of(tally[kernel, r] * BLK + i * SPAN, BLK), SPAN)
        return (
            [kbuf[where, h * HD : (h + 1) * HD].astype(jnp.bfloat16) for h in range(KVH)],
            [vbuf[where, h * HD : (h + 1) * HD].astype(jnp.bfloat16) for h in range(KVH)],
            lane + i * SPAN < tally[8 + kernel, r],
        )

    def beyond(r):
        def piece(i, _):
            hold(r, state, blend(row_queries(r, q_ref), [block(r, i)], held(r, state)))
            return 0

        lax.fori_loop(1, (tally[8 + kernel, r] + SPAN - 1) // SPAN, piece, 0)

    def partial_rows(pair):
        new = [blend(row_queries(r, q_ref), [block(r, 0)], None, guard=True) for r in pair]
        for r, one in zip(pair, new):
            hold(r, state, one)
        for r in pair:
            beyond(r)
        done = []
        for r in pair:
            for head in range(KVH):
                amount = total[r, head]
                safe = jnp.where(amount > 0.0, amount, 1.0)
                lines = [
                    jnp.sum(jnp.where(eye, one[:, :width], 0.0), axis=0, keepdims=True)
                    for one in (top[r, head], amount)
                ]
                done.append((r, head, (acc[r, head] / safe).astype(jnp.bfloat16), lines))
        for r, head, value, lines in done:
            out[r, head] = value
            for i in range(2):
                stats[r, head, pl.ds(i, 1), :] = lines[i]

    def with_part(r, new):
        merged = []
        for head in range(KVH):
            lines = []
            for i in range(2):
                line = jnp.broadcast_to(stats[r, head, pl.ds(i, 1), :], (width, width))
                lines.append(jnp.sum(jnp.where(eye, line, 0.0), axis=1, keepdims=True))
            other_top, other_total = lines
            other_top = jnp.where(other_total > 0.0, other_top, NEG)
            value, old_top, amount = new[head]
            new_top = jnp.maximum(old_top, other_top)
            mine = jnp.exp(old_top - new_top)
            theirs = jnp.exp(other_top - new_top) * other_total
            merged.append(
                (
                    value * mine + part[r, head].astype(jnp.float32) * theirs,
                    new_top,
                    amount * mine + theirs,
                )
            )
        return merged

    def state_rows(pair):
        new = [blend(row_queries(r, q_ref), [block(r, 0)], held(r, before)) for r in pair]
        new = [with_part(r, one) for r, one in zip(pair, new)]
        for r, one in zip(pair, new):
            hold(r, state, one)
        for r in pair:
            beyond(r)

    def put_out(pair, new):
        done = [value / amount for one in new for value, _, amount in one]
        for i, value in enumerate(done):
            scr[i] = value
        steps = out.shape[1]
        group = width // steps
        for i, r in enumerate(pair):
            for head in range(KVH):
                for g in range(group):
                    column = (head * group + g) * HD
                    out[r, :, column : column + HD] = scr[
                        i * KVH + head, pl.ds(g, steps, stride=group), :
                    ].astype(jnp.bfloat16)

    def final_rows(pair):
        new = [blend(row_queries(r, q_ref), [block(r, 0)], held(r, before)) for r in pair]
        put_out(pair, new)
        longest = functools.reduce(jnp.maximum, [tally[8 + kernel, r] for r in pair])

        @pl.when(longest > SPAN)
        def _():
            for r, one in zip(pair, new):
                hold(r, state, one)
            for r in pair:
                beyond(r)
            put_out(pair, [held(r, state) for r in pair])

    run = {"partial": partial_rows, "state": state_rows, "final": final_rows}[kind]
    together = 2 if rows % 2 == 0 else 1

    def some_rows(i, _):
        run([i * together + u for u in range(together)])
        return 0

    lax.fori_loop(0, rows // together, some_rows, 0)


def span(kind, kernel, cap, scalars, grouped, tables, messages, state, extra, steps):
    rows, _, width, _ = grouped.shape
    feature = messages[0].shape[-1]
    count = len(messages)
    room = (count * cap + 1) * BLK + SPAN
    smem = pl.BlockSpec(memory_space=pltpu.SMEM)
    vmem = pl.BlockSpec(memory_space=pltpu.VMEM)
    running = [pltpu.VMEM((rows, KVH, width, HD), jnp.float32)] * 3
    scratch = []
    if kind == "partial":
        out_shape = (
            jax.ShapeDtypeStruct((rows, KVH, width, HD), jnp.bfloat16),
            jax.ShapeDtypeStruct((rows, KVH, 2, width), jnp.float32),
        )
        scratch += running
    elif kind == "state":
        out_shape = state_shapes(rows, width)
    else:
        out_shape = jax.ShapeDtypeStruct((rows, steps, QH * HD), jnp.bfloat16)
        scratch += running + [pltpu.VMEM((2 * KVH, width, HD), jnp.float32)]
    scratch += [pltpu.VMEM((room, feature), jnp.float32)] * 2
    return pl.pallas_call(
        functools.partial(span_kernel, kind, kernel, count, cap),
        out_shape=out_shape,
        in_specs=[smem] * 7 + [vmem] * (5 + count + len(state) + len(extra)),
        out_specs=jax.tree.map(lambda _: vmem, out_shape),
        scratch_shapes=scratch,
        compiler_params=pltpu.CompilerParams(vmem_limit_bytes=GRANT),
        cost_estimate=pl.CostEstimate(
            flops=10**9, bytes_accessed=12 * 2**20, transcendentals=10**6
        ),
    )(*scalars, grouped, *tables, *messages, *state, *extra)


PHASES = {"d": (2, 2, 2, 2), "f": (0, 3, 3, 0), "g": (3, 0, 0, 3), "b": (1, 1, 1, 1)}


def site_plane(plane, flip):
    dest = plane ^ flip
    half = PLANES // 2
    if (plane < half) != (dest < half) and dest in (half - 1, half):
        return PLANES - 1 - dest
    return dest


def came_from(phase, plane):
    flips = PHASES[phase]
    return next(s for s in range(PLANES) if site_plane(s, flips[s]) == plane)


def for_mirror(phase, plane):
    source = came_from(phase, plane)
    return int(source ^ PHASES[phase][source] != plane)


def route(n, phase, offset):
    in_plane = n // PLANES
    return [
        (
            plane * in_plane + place,
            site_plane(plane, flip) * in_plane + (place + offset) % in_plane,
        )
        for plane, flip in enumerate(PHASES[phase])
        for place in range(in_plane)
    ]


STAGE = {"d": 1, "f": 1, "g": 1, "b": 2}


def device_tables(n):
    in_plane = n // PLANES
    lines = []
    for me in range(n):
        plane, place = me // in_plane, me % in_plane
        entry, stage = [], []
        post = [[-1] * n, [-1] * n]
        for phase in PHASES:
            mirror = for_mirror(phase, plane)
            for offset in range(in_plane):
                source = came_from(phase, plane) * in_plane + (place - offset) % in_plane
                entry.append(mirror * n + source)
                stage.append(0 if mirror else STAGE[phase])
                post[mirror][source] = stage[-1]
        lines.append((entry, stage, post[0], post[1]))
    return np.array(lines, np.int32)


def body(
    span_keys,
    span_values,
    block_device,
    block_row,
    cache_len,
    cache_keys,
    cache_values,
    queries,
    step_keys,
    step_values,
):
    n = lax.axis_size("seq")
    in_plane = n // PLANES
    me = lax.axis_index("seq").astype(jnp.int32)
    rows = cache_len.shape[0]
    feature = span_keys.shape[1]
    blocks = span_keys.shape[0] // BLK
    cap = max(2, (2 * blocks + n - 1) // n)
    steps = queries.shape[1]
    group = QH // KVH
    names = list(PHASES)

    phase_table = jnp.array(
        [
            [next(i for i, p in enumerate(names) if PHASES[p][z] == z ^ d) for d in range(PLANES)]
            for z in range(PLANES)
        ],
        jnp.int32,
    )
    half = PLANES // 2
    swap = [
        (a * in_plane + i, b * in_plane + i)
        for a, b in ((half - 1, half), (half, half - 1))
        for i in range(in_plane)
    ]
    mirrored = lax.ppermute(queries, "seq", swap)
    messages = pack(
        n,
        cap,
        phase_table,
        block_device[:, 0],
        span_keys.reshape(blocks, BLK, feature),
        span_values.reshape(blocks, BLK, feature),
    )
    packed = {p: messages[i * in_plane : (i + 1) * in_plane] for i, p in enumerate(names)}

    def send(phase):
        out = []
        for offset in range(in_plane):
            value = packed[phase][offset]
            pairs = route(n, phase, offset)
            if any(a != b for a, b in pairs):
                value = lax.ppermute(value, "seq", pairs)
            out.append(value)
        return out

    got = {phase: send(phase) for phase in names}

    def regroup(value):
        value = value.reshape(rows, steps, KVH, group, HD).transpose(0, 2, 1, 3, 4)
        return value.reshape(rows, KVH, steps * group, HD)

    queries, mirrored = lax.optimization_barrier((queries, mirrored))
    grouped, mirrored = regroup(queries), regroup(mirrored)

    notes = note(n, cap, block_device[:, 0], block_row, cache_len)
    notes = lax.all_to_all(notes, "seq", split_axis=0, concat_axis=0, tiled=True)
    mine = lax.dynamic_index_in_dim(jnp.array(device_tables(n)), me, 0, keepdims=False)
    *slots, tally = index(n, cap, rows, notes, mine[2:])
    twin = [m if m // in_plane in (0, PLANES - 1) else (PLANES - 1 - m // in_plane) * in_plane
            + m % in_plane for m in range(n)]
    twin = jnp.sum(jnp.where(jnp.arange(n) == me, jnp.array(twin, jnp.int32), 0))
    mirror_len = lax.dynamic_index_in_dim(notes, twin, 0, keepdims=False)
    mirror_len = mirror_len[2 * LANES : 2 * LANES + rows]

    own_tables = turn_tables(cache_len[:, None] + jnp.arange(BLK, dtype=jnp.int32)[None])
    mirror_tables = turn_tables(mirror_len[:, None] + jnp.arange(BLK, dtype=jnp.int32)[None])
    rank_tables = turn_tables(jnp.arange(n * cap, dtype=jnp.int32) * BLK)

    def scalars(phases):
        first = names.index(phases[0]) * in_plane
        picked = mine[:2, first : first + len(phases) * in_plane]
        return (picked[0], picked[1], *slots, tally)

    state = resident(cache_len, grouped, step_keys, step_values, cache_keys, cache_values)
    partial, stats = span(
        "partial", 0, cap, scalars("df"), mirrored,
        mirror_tables + rank_tables, got["d"] + got["f"], (), (), steps,
    )
    partial = lax.ppermute(partial, "seq", swap)
    stats = lax.ppermute(stats, "seq", swap)
    state = span(
        "state", 1, cap, scalars("dfg"), grouped,
        own_tables + rank_tables, got["d"] + got["f"] + got["g"], tuple(state),
        (partial, stats), steps,
    )
    return span(
        "final", 2, cap, scalars("b"), grouped,
        own_tables + rank_tables, got["b"], tuple(state), (), steps,
    )


def solution(mesh):
    placed = (
        P(("groups", "seq"), None),
        P(("groups", "seq"), None),
        P(("groups", "seq"), None),
        P(("groups", "seq")),
        P(("groups", "seq")),
        P(("groups", "seq"), None, None),
        P(("groups", "seq"), None, None),
        P(("groups", "seq"), None, None),
        P(("groups", "seq"), None, None),
        P(("groups", "seq"), None, None),
    )

    return jax.shard_map(
        body,
        mesh=mesh,
        in_specs=placed,
        out_specs=P(("groups", "seq"), None, None),
        check_vma=False,
    )
```

```python
import functools

import jax
import jax.numpy as jnp
import numpy as np
from jax import lax
from jax.experimental import pallas as pl
from jax.experimental.pallas import tpu as pltpu
from jax.sharding import PartitionSpec as P


KVH = 4
QH = 64
HD = 128
BLK = 8
PLANES = 4
CHUNK = 256
SPAN = 128
LANES = 128
GRANT = 20 * 2**20
UNROLL = 4
PACKED = 4
NEG = -1e30


def frequencies(half_width):
    freq_index = jnp.arange(half_width, dtype=jnp.float32)
    base_freq = 1.0 / 500000.0 ** (freq_index / half_width)
    wavelen = 2.0 * jnp.pi / base_freq
    smooth = (8192.0 / wavelen - 1.0) / 3.0
    blended = (1.0 - smooth) * base_freq / 8.0 + smooth * base_freq
    scaled = jnp.where(wavelen > 8192.0, base_freq / 8.0, blended)
    return jnp.where(wavelen < 2048.0, base_freq, scaled)


def turn_tables(positions):
    freq = frequencies(HD // 2)
    angles = positions.astype(jnp.float32)[..., None] * jnp.concatenate([freq, freq])
    sign = jnp.where(jnp.arange(HD) < HD // 2, -1.0, 1.0).astype(jnp.float32)
    return jnp.cos(angles), jnp.sin(angles) * sign


def pack_kernel(n, phase_table, target, keys, values, *refs):
    outs = refs[:n]
    slots, fill, rel, sems = refs[n:]
    blocks = keys.shape[0]
    in_plane = n // PLANES
    me = lax.axis_index("seq")
    plane, place = me // in_plane, me % in_plane

    def clear(p, _):
        for i in range(in_plane):
            fill[p * in_plane + i] = 0
            offset = i - place
            offset = jnp.where(offset < 0, offset + in_plane, offset)
            rel[p * in_plane + i] = phase_table[plane, p] * in_plane + offset
        return 0

    lax.fori_loop(0, PLANES, clear, 0)

    def put(step, _):
        ready = []
        for u in range(PACKED):
            b = step * PACKED + u
            dest = target[b]
            slot = fill[dest]
            fill[dest] = slot + 1
            ready.append((b, rel[dest], slot))
        for b, message, slot in ready:
            slots[message, 0, slot] = keys[b]
            slots[message, 1, slot] = values[b]
        return 0

    lax.fori_loop(0, blocks // PACKED, put, 0)
    copies = [pltpu.make_async_copy(slots.at[i], outs[i], sems.at[i]) for i in range(n)]
    for copy in copies:
        copy.start()
    for copy in copies:
        copy.wait()


def pack(n, cap, phase_table, target, keys, values):
    width = keys.shape[-1]
    message = jax.ShapeDtypeStruct((2, cap, BLK, width), jnp.bfloat16)
    smem = pl.BlockSpec(memory_space=pltpu.SMEM)
    vmem = pl.BlockSpec(memory_space=pltpu.VMEM)
    return pl.pallas_call(
        functools.partial(pack_kernel, n),
        out_shape=(message,) * n,
        in_specs=[smem] * 2 + [vmem] * 2,
        out_specs=(pl.BlockSpec(memory_space=pl.ANY),) * n,
        scratch_shapes=[
            pltpu.VMEM((n, 2, cap, BLK, width), jnp.bfloat16),
            pltpu.SMEM((n,), jnp.int32),
            pltpu.SMEM((n,), jnp.int32),
            pltpu.SemaphoreType.DMA((n,)),
        ],
        name="pack",
    )(phase_table, target, keys, values)


def note_kernel(n, target, rows, lens, notes, fill):
    in_plane = n // PLANES

    def clear(i, _):
        fill[i] = 0
        for k in range(lens.shape[0]):
            notes[i, 2 * LANES + k] = lens[k]
        return 0

    lax.fori_loop(0, n, clear, 0)

    def twin_of(dest):
        plane = dest // in_plane
        inner = (plane > 0) & (plane < PLANES - 1)
        return jnp.where(inner, (PLANES - 1 - 2 * plane) * in_plane + dest, dest)

    def put(step, _):
        ready = []
        for u in range(PACKED):
            b = step * PACKED + u
            dest = target[b]
            slot = fill[dest]
            fill[dest] = slot + 1
            ready.append((dest, twin_of(dest), slot, rows[b]))
        for dest, twin, slot, row in ready:
            notes[dest, slot] = row
            notes[twin, LANES + slot] = row
        return 0

    lax.fori_loop(0, rows.shape[0] // PACKED, put, 0)

    def close(i, _):
        notes[i, LANES - 1] = fill[i]
        notes[twin_of(i), 2 * LANES - 1] = fill[i]
        return 0

    lax.fori_loop(0, n, close, 0)


def note(n, target, rows, lens):
    smem = pl.BlockSpec(memory_space=pltpu.SMEM)
    return pl.pallas_call(
        functools.partial(note_kernel, n),
        out_shape=jax.ShapeDtypeStruct((n, 3 * LANES), jnp.int32),
        in_specs=[smem] * 3,
        out_specs=smem,
        scratch_shapes=[pltpu.SMEM((n,), jnp.int32)],
        compiler_params=pltpu.CompilerParams(vmem_limit_bytes=GRANT),
        name="note",
    )(target, rows, lens)


def index_kernel(n, cap, rows, notes, stages, place, row_of, rank_of, used, tally):
    f32 = jnp.float32

    def iotas(shape):
        return [lax.broadcasted_iota(jnp.int32, shape, d) for d in (0, 1)]

    a, b = iotas((cap, cap))
    before = (a < b).astype(f32)
    a, b = iotas((n, n))
    sooner = (b < a).astype(f32)
    lines = [jnp.broadcast_to(stages[i : i + 1, :n], (n, n)) for i in range(2)]
    posts = [
        jnp.sum(jnp.where(a == b, line, 0), axis=1, keepdims=True) for line in lines
    ]
    mates = [jnp.where(line == post, sooner, 0.0) for line, post in zip(lines, posts)]
    kernel, lane = iotas((8, LANES))
    counts = jnp.zeros((8, LANES), f32)
    for side in range(2):
        there = notes[:, side * LANES : (side + 1) * LANES]
        valid = lax.broadcasted_iota(jnp.int32, (n, cap), 1) < there[:, LANES - 1 :]
        rows_here = jnp.where(valid, there[:, :cap], -1)
        rank = jnp.zeros((n, cap), f32)
        local = jnp.zeros((n, cap), f32)
        for r in range(rows):
            hit = (rows_here == r).astype(f32)
            inside = jnp.dot(hit, before, preferred_element_type=f32)
            ahead = jnp.dot(sooner, hit, preferred_element_type=f32)
            near = jnp.dot(mates[side], hit, preferred_element_type=f32)
            rank += hit * (inside + jnp.sum(ahead, axis=1, keepdims=True))
            local += hit * (inside + jnp.sum(near, axis=1, keepdims=True))
            per_source = jnp.sum(hit, axis=1, keepdims=True)
            for stage in range(3):
                if (stage == 0) == (side == 1):
                    number = jnp.sum(
                        jnp.where(posts[side] == stage, per_source, 0.0), axis=0, keepdims=True
                    )
                    counts += jnp.where((kernel == stage) & (lane == r), number, 0.0)
        span = slice(side * n, side * n + n)
        place[span, :] = jnp.where(valid, local, -1.0).astype(jnp.int32)
        row_of[span, :] = jnp.maximum(rows_here, 0)
        rank_of[span, :] = rank.astype(jnp.int32)
        filled = jnp.sum(valid.astype(f32), axis=1, keepdims=True)
        used[span, :] = jnp.broadcast_to(filled, (n, cap)).astype(jnp.int32)
    a, b = iotas((LANES, LANES))
    begin = jnp.dot(counts, (a < b).astype(f32), preferred_element_type=f32)
    tally[0:8, :] = begin.astype(jnp.int32)
    tally[8:16, :] = (counts * BLK).astype(jnp.int32)


def index(n, cap, rows, notes, stages):
    vmem = pl.BlockSpec(memory_space=pltpu.VMEM)
    slots = jax.ShapeDtypeStruct((2 * n, cap), jnp.int32)
    return pl.pallas_call(
        functools.partial(index_kernel, n, cap, rows),
        out_shape=(slots,) * 4 + (jax.ShapeDtypeStruct((16, LANES), jnp.int32),),
        in_specs=[vmem] * 2,
        out_specs=(vmem,) * 5,
        compiler_params=pltpu.CompilerParams(vmem_limit_bytes=GRANT),
        name="index",
    )(notes, stages)


def as_wide(line, width):
    if width % HD == 0:
        return jnp.concatenate([line] * (width // HD), axis=1)
    return line[:, :width]


def blend(queries, pieces, old, guard=False):
    scale = HD ** (-0.5)
    heads = range(KVH)
    scores = [
        [
            jnp.where(
                piece[2],
                lax.dot_general(
                    queries[head],
                    piece[0][head],
                    (((1,), (1,)), ((), ())),
                    preferred_element_type=jnp.float32,
                )
                * scale,
                NEG,
            )
            for piece in pieces
        ]
        for head in heads
    ]
    new = []
    for head in heads:
        peak = functools.reduce(
            jnp.maximum, [jnp.max(one, axis=-1, keepdims=True) for one in scores[head]]
        )
        if old is None:
            new_top = jnp.broadcast_to(peak, (peak.shape[0], HD))
        else:
            old_acc, old_top, old_total = old[head]
            new_top = jnp.maximum(old_top, peak)
        raw = [jnp.exp(one - as_wide(new_top, one.shape[1])) for one in scores[head]]
        if guard:
            raw = [jnp.where(piece[2], one, 0.0) for piece, one in zip(pieces, raw)]
        added = sum(jnp.sum(one, axis=-1, keepdims=True) for one in raw)
        mixed = sum(
            jnp.dot(one.astype(jnp.bfloat16), piece[1][head], preferred_element_type=jnp.float32)
            for one, piece in zip(raw, pieces)
        )
        if old is None:
            new.append((mixed, new_top, jnp.broadcast_to(added, new_top.shape)))
        else:
            factor = jnp.exp(old_top - new_top)
            new.append((old_acc * factor + mixed, new_top, old_total * factor + added))
    return new


def held(row, state):
    return [tuple(one[row, head] for one in state) for head in range(KVH)]


def hold(row, state, new):
    for head in range(KVH):
        for one, value in zip(state, new[head]):
            one[row, head] = value


def row_queries(row, q_ref):
    return [q_ref[row, head] for head in range(KVH)]


def resident_kernel(
    lens, q_ref, step_k, step_v, keys, values, acc, top, total, kbuf, vbuf, sems
):
    rows, slot_count = kbuf.shape[0], kbuf.shape[1]
    piece = min(CHUNK, slot_count)
    pieces = slot_count // piece
    steps = step_k.shape[1]
    width = q_ref.shape[2]
    group = width // steps

    def copies(r, i):
        part = pl.ds(i * piece, piece)
        return (
            pltpu.make_async_copy(keys.at[r, part], kbuf.at[r, part], sems.at[0, r, i]),
            pltpu.make_async_copy(values.at[r, part], vbuf.at[r, part], sems.at[1, r, i]),
        )

    def fetch(r, _):
        for i in range(pieces):

            @pl.when((i == 0) | (i * piece < lens[r]))
            def _():
                for copy in copies(r, i):
                    copy.start()

        return 0

    lax.fori_loop(0, rows, fetch, 0)
    lane = lax.broadcasted_iota(jnp.int32, (width, piece), 1)
    causal = (
        lax.broadcasted_iota(jnp.int32, (width, steps), 1)
        <= lax.broadcasted_iota(jnp.int32, (width, steps), 0) // group
    )

    def one_row(r, _):
        def part(i):
            span = pl.ds(i * piece, piece)
            return (
                [kbuf[r, span, head * HD : (head + 1) * HD] for head in range(KVH)],
                [vbuf[r, span, head * HD : (head + 1) * HD] for head in range(KVH)],
                lane + i * piece < lens[r],
            )

        own = (
            [step_k[r, :, head * HD : (head + 1) * HD] for head in range(KVH)],
            [step_v[r, :, head * HD : (head + 1) * HD] for head in range(KVH)],
            causal,
        )
        state = (acc, top, total)
        for copy in copies(r, 0):
            copy.wait()
        hold(r, state, blend(row_queries(r, q_ref), [own, part(0)], None))
        for i in range(1, pieces):

            @pl.when(i * piece < lens[r])
            def _():
                for copy in copies(r, i):
                    copy.wait()
                hold(r, state, blend(row_queries(r, q_ref), [part(i)], held(r, state)))

        return 0

    lax.fori_loop(0, rows, one_row, 0)


def state_shapes(rows, width):
    shape = jax.ShapeDtypeStruct((rows, KVH, width, HD), jnp.float32)
    return (shape,) * 3


def resident(lens, grouped, step_k, step_v, keys, values):
    rows, slot_count, feature = keys.shape
    pieces = slot_count // min(CHUNK, slot_count)
    vmem = pl.BlockSpec(memory_space=pltpu.VMEM)
    hbm = pl.BlockSpec(memory_space=pltpu.HBM)
    return pl.pallas_call(
        resident_kernel,
        out_shape=state_shapes(rows, grouped.shape[2]),
        in_specs=[pl.BlockSpec(memory_space=pltpu.SMEM), vmem, vmem, vmem, hbm, hbm],
        out_specs=(vmem,) * 3,
        scratch_shapes=[
            pltpu.VMEM((rows, slot_count, feature), jnp.bfloat16),
            pltpu.VMEM((rows, slot_count, feature), jnp.bfloat16),
            pltpu.SemaphoreType.DMA((2, rows, pieces)),
        ],
        compiler_params=pltpu.CompilerParams(vmem_limit_bytes=GRANT),
        cost_estimate=pl.CostEstimate(
            flops=2 * 10**9, bytes_accessed=16 * 2**20, transcendentals=10**6
        ),
        name="resident",
    )(lens, grouped, step_k, step_v, keys, values)


def span_kernel(
    kind, kernel, count, cap, entry, stage, place_of, row_of, rank_of, used, tally,
    q_ref, ca, sa, cb, sb, *refs,
):
    messages = refs[:count]
    refs = refs[count:]
    before = refs[:3]
    if kind == "partial":
        out, stats, acc, top, total, kbuf, vbuf = refs
    elif kind == "state":
        part, stats, acc, top, total, kbuf, vbuf = refs[3:]
    else:
        out, acc, top, total, scr, kbuf, vbuf = refs[3:]
    state = (acc, top, total)
    rows = q_ref.shape[0]
    width = q_ref.shape[2]
    feature = kbuf.shape[1]
    last = tally[kernel, rows - 1] * BLK + tally[8 + kernel, rows - 1]
    tail = pl.ds(pl.multiple_of(last, BLK), SPAN)
    vbuf[tail, :] = jnp.zeros((SPAN, feature), jnp.float32)
    unroll = min(UNROLL, cap)
    trash = count * cap + SPAN // BLK
    for j in range(count):

        @pl.when(stage[j] == kernel)
        def _():
            source = entry[j]
            message = messages[j]

            def place(step, _):
                ready = []
                for u in range(unroll):
                    k = step * unroll + u
                    r = row_of[source, k]
                    rank = rank_of[source, k]
                    local = place_of[source, k]
                    slot = jnp.where(local < 0, trash, tally[kernel, r] + local)
                    c_a, s_a = ca[r], sa[r]
                    c_b, s_b = cb[pl.ds(rank, 1), :], sb[pl.ds(rank, 1), :]
                    cosine = c_a * c_b - s_a * s_b
                    sine = s_a * c_b + c_a * s_b
                    where = pl.ds(pl.multiple_of(slot * BLK, BLK), BLK)
                    value = message[1, k].astype(jnp.float32)
                    key = message[0, k].astype(jnp.float32)
                    turned = []
                    for head in range(KVH):
                        piece = key[:, head * HD : (head + 1) * HD]
                        turned.append(piece * cosine + pltpu.roll(piece, HD // 2, 1) * sine)
                    ready.append((where, turned, value))
                for where, turned, value in ready:
                    vbuf[where, :] = value
                    for head in range(KVH):
                        kbuf[where, head * HD : (head + 1) * HD] = turned[head]
                return 0

            lax.fori_loop(0, (used[source, 0] + unroll - 1) // unroll, place, 0)

    lane = lax.broadcasted_iota(jnp.int32, (width, SPAN), 1)
    eye = lax.broadcasted_iota(jnp.int32, (width, width), 0) == lax.broadcasted_iota(
        jnp.int32, (width, width), 1
    )

    def block(r, i):
        where = pl.ds(pl.multiple_of(tally[kernel, r] * BLK + i * SPAN, BLK), SPAN)
        return (
            [kbuf[where, h * HD : (h + 1) * HD].astype(jnp.bfloat16) for h in range(KVH)],
            [vbuf[where, h * HD : (h + 1) * HD].astype(jnp.bfloat16) for h in range(KVH)],
            lane + i * SPAN < tally[8 + kernel, r],
        )

    def beyond(r):
        def piece(i, _):
            hold(r, state, blend(row_queries(r, q_ref), [block(r, i)], held(r, state)))
            return 0

        lax.fori_loop(1, (tally[8 + kernel, r] + SPAN - 1) // SPAN, piece, 0)

    def partial_rows(pair):
        new = [blend(row_queries(r, q_ref), [block(r, 0)], None, guard=True) for r in pair]
        for r, one in zip(pair, new):
            hold(r, state, one)
        for r in pair:
            beyond(r)
        done = []
        for r in pair:
            for head in range(KVH):
                amount = total[r, head]
                safe = jnp.where(amount > 0.0, amount, 1.0)
                lines = [
                    jnp.sum(jnp.where(eye, one[:, :width], 0.0), axis=0, keepdims=True)
                    for one in (top[r, head], amount)
                ]
                done.append((r, head, (acc[r, head] / safe).astype(jnp.bfloat16), lines))
        for r, head, value, lines in done:
            out[r, head] = value
            for i in range(2):
                stats[r, head, pl.ds(i, 1), :] = lines[i]

    def with_part(r, new):
        merged = []
        for head in range(KVH):
            lines = []
            for i in range(2):
                line = jnp.broadcast_to(stats[r, head, pl.ds(i, 1), :], (width, width))
                lines.append(jnp.sum(jnp.where(eye, line, 0.0), axis=1, keepdims=True))
            other_top, other_total = lines
            other_top = jnp.where(other_total > 0.0, other_top, NEG)
            value, old_top, amount = new[head]
            new_top = jnp.maximum(old_top, other_top)
            mine = jnp.exp(old_top - new_top)
            theirs = jnp.exp(other_top - new_top) * other_total
            merged.append(
                (
                    value * mine + part[r, head].astype(jnp.float32) * theirs,
                    new_top,
                    amount * mine + theirs,
                )
            )
        return merged

    def state_rows(pair):
        new = [blend(row_queries(r, q_ref), [block(r, 0)], held(r, before)) for r in pair]
        new = [with_part(r, one) for r, one in zip(pair, new)]
        for r, one in zip(pair, new):
            hold(r, state, one)
        for r in pair:
            beyond(r)

    def put_out(pair, new):
        done = [value / amount for one in new for value, _, amount in one]
        for i, value in enumerate(done):
            scr[i] = value
        steps = out.shape[1]
        group = width // steps
        for i, r in enumerate(pair):
            for head in range(KVH):
                for g in range(group):
                    column = (head * group + g) * HD
                    out[r, :, column : column + HD] = scr[
                        i * KVH + head, pl.ds(g, steps, stride=group), :
                    ].astype(jnp.bfloat16)

    def final_rows(pair):
        new = [blend(row_queries(r, q_ref), [block(r, 0)], held(r, before)) for r in pair]
        put_out(pair, new)
        longest = functools.reduce(jnp.maximum, [tally[8 + kernel, r] for r in pair])

        @pl.when(longest > SPAN)
        def _():
            for r, one in zip(pair, new):
                hold(r, state, one)
            for r in pair:
                beyond(r)
            put_out(pair, [held(r, state) for r in pair])

    run = {"partial": partial_rows, "state": state_rows, "final": final_rows}[kind]
    together = 2 if rows % 2 == 0 else 1

    def some_rows(i, _):
        run([i * together + u for u in range(together)])
        return 0

    lax.fori_loop(0, rows // together, some_rows, 0)


def span(kind, kernel, cap, scalars, grouped, tables, messages, state, extra, steps):
    rows, _, width, _ = grouped.shape
    feature = messages[0].shape[-1]
    count = len(messages)
    room = (count * cap + 1) * BLK + SPAN
    smem = pl.BlockSpec(memory_space=pltpu.SMEM)
    vmem = pl.BlockSpec(memory_space=pltpu.VMEM)
    running = [pltpu.VMEM((rows, KVH, width, HD), jnp.float32)] * 3
    scratch = []
    if kind == "partial":
        out_shape = (
            jax.ShapeDtypeStruct((rows, KVH, width, HD), jnp.bfloat16),
            jax.ShapeDtypeStruct((rows, KVH, 2, width), jnp.float32),
        )
        scratch += running
    elif kind == "state":
        out_shape = state_shapes(rows, width)
    else:
        out_shape = jax.ShapeDtypeStruct((rows, steps, QH * HD), jnp.bfloat16)
        scratch += running + [pltpu.VMEM((2 * KVH, width, HD), jnp.float32)]
    scratch += [pltpu.VMEM((room, feature), jnp.float32)] * 2
    return pl.pallas_call(
        functools.partial(span_kernel, kind, kernel, count, cap),
        out_shape=out_shape,
        in_specs=[smem] * 7 + [vmem] * (5 + count + len(state) + len(extra)),
        out_specs=jax.tree.map(lambda _: vmem, out_shape),
        scratch_shapes=scratch,
        compiler_params=pltpu.CompilerParams(vmem_limit_bytes=GRANT),
        cost_estimate=pl.CostEstimate(
            flops=10**9, bytes_accessed=12 * 2**20, transcendentals=10**6
        ),
    )(*scalars, grouped, *tables, *messages, *state, *extra)


PHASES = {"d": (2, 2, 2, 2), "f": (0, 3, 3, 0), "g": (3, 0, 0, 3), "b": (1, 1, 1, 1)}


def site_plane(plane, flip):
    dest = plane ^ flip
    half = PLANES // 2
    if (plane < half) != (dest < half) and dest in (half - 1, half):
        return PLANES - 1 - dest
    return dest


def came_from(phase, plane):
    flips = PHASES[phase]
    return next(s for s in range(PLANES) if site_plane(s, flips[s]) == plane)


def for_mirror(phase, plane):
    source = came_from(phase, plane)
    return int(source ^ PHASES[phase][source] != plane)


def route(n, phase, offset):
    in_plane = n // PLANES
    return [
        (
            plane * in_plane + place,
            site_plane(plane, flip) * in_plane + (place + offset) % in_plane,
        )
        for plane, flip in enumerate(PHASES[phase])
        for place in range(in_plane)
    ]


STAGE = {"d": 1, "f": 1, "g": 1, "b": 2}


def device_tables(n):
    in_plane = n // PLANES
    lines = []
    for me in range(n):
        plane, place = me // in_plane, me % in_plane
        entry, stage = [], []
        post = [[-1] * n, [-1] * n]
        for phase in PHASES:
            mirror = for_mirror(phase, plane)
            for offset in range(in_plane):
                source = came_from(phase, plane) * in_plane + (place - offset) % in_plane
                entry.append(mirror * n + source)
                stage.append(0 if mirror else STAGE[phase])
                post[mirror][source] = stage[-1]
        lines.append((entry, stage, post[0], post[1]))
    return np.array(lines, np.int32)


def body(
    span_keys,
    span_values,
    block_device,
    block_row,
    cache_len,
    cache_keys,
    cache_values,
    queries,
    step_keys,
    step_values,
):
    n = lax.axis_size("seq")
    in_plane = n // PLANES
    me = lax.axis_index("seq").astype(jnp.int32)
    rows = cache_len.shape[0]
    feature = span_keys.shape[1]
    blocks = span_keys.shape[0] // BLK
    cap = max(2, (2 * blocks + n - 1) // n)
    steps = queries.shape[1]
    group = QH // KVH
    names = list(PHASES)

    phase_table = jnp.array(
        [
            [next(i for i, p in enumerate(names) if PHASES[p][z] == z ^ d) for d in range(PLANES)]
            for z in range(PLANES)
        ],
        jnp.int32,
    )
    half = PLANES // 2
    swap = [
        (a * in_plane + i, b * in_plane + i)
        for a, b in ((half - 1, half), (half, half - 1))
        for i in range(in_plane)
    ]
    mirrored = lax.ppermute(queries, "seq", swap)
    messages = pack(
        n,
        cap,
        phase_table,
        block_device[:, 0],
        span_keys.reshape(blocks, BLK, feature),
        span_values.reshape(blocks, BLK, feature),
    )
    packed = {p: messages[i * in_plane : (i + 1) * in_plane] for i, p in enumerate(names)}

    def send(phase):
        out = []
        for offset in range(in_plane):
            value = packed[phase][offset]
            pairs = route(n, phase, offset)
            if any(a != b for a, b in pairs):
                value = lax.ppermute(value, "seq", pairs)
            out.append(value)
        return out

    got = {phase: send(phase) for phase in names}

    def regroup(value):
        value = value.reshape(rows, steps, KVH, group, HD).transpose(0, 2, 1, 3, 4)
        return value.reshape(rows, KVH, steps * group, HD)

    mirrored = regroup(mirrored)

    notes = note(n, block_device[:, 0], block_row, cache_len)
    notes = lax.all_to_all(notes, "seq", split_axis=0, concat_axis=0, tiled=True)
    mine = lax.dynamic_index_in_dim(jnp.array(device_tables(n)), me, 0, keepdims=False)
    *slots, tally = index(n, cap, rows, notes, mine[2:])
    twin = [m if m // in_plane in (0, PLANES - 1) else (PLANES - 1 - m // in_plane) * in_plane
            + m % in_plane for m in range(n)]
    twin = jnp.sum(jnp.where(jnp.arange(n) == me, jnp.array(twin, jnp.int32), 0))
    mirror_len = lax.dynamic_index_in_dim(notes, twin, 0, keepdims=False)
    mirror_len = mirror_len[2 * LANES : 2 * LANES + rows]

    own_tables = turn_tables(cache_len[:, None] + jnp.arange(BLK, dtype=jnp.int32)[None])
    mirror_tables = turn_tables(mirror_len[:, None] + jnp.arange(BLK, dtype=jnp.int32)[None])
    rank_tables = turn_tables(jnp.arange(n * cap, dtype=jnp.int32) * BLK)

    def scalars(phases):
        first = names.index(phases[0]) * in_plane
        picked = mine[:2, first : first + len(phases) * in_plane]
        return (picked[0], picked[1], *slots, tally)

    partial, stats = span(
        "partial", 0, cap, scalars("df"), mirrored,
        mirror_tables + rank_tables, got["d"] + got["f"], (), (), steps,
    )
    queries, partial = lax.optimization_barrier((queries, partial))
    grouped = regroup(queries)
    state = resident(cache_len, grouped, step_keys, step_values, cache_keys, cache_values)
    partial = lax.ppermute(partial, "seq", swap)
    stats = lax.ppermute(stats, "seq", swap)
    state = span(
        "state", 1, cap, scalars("dfg"), grouped,
        own_tables + rank_tables, got["d"] + got["f"] + got["g"], tuple(state),
        (partial, stats), steps,
    )
    return span(
        "final", 2, cap, scalars("b"), grouped,
        own_tables + rank_tables, got["b"], tuple(state), (), steps,
    )


def solution(mesh):
    placed = (
        P(("groups", "seq"), None),
        P(("groups", "seq"), None),
        P(("groups", "seq"), None),
        P(("groups", "seq")),
        P(("groups", "seq")),
        P(("groups", "seq"), None, None),
        P(("groups", "seq"), None, None),
        P(("groups", "seq"), None, None),
        P(("groups", "seq"), None, None),
        P(("groups", "seq"), None, None),
    )

    return jax.shard_map(
        body,
        mesh=mesh,
        in_specs=placed,
        out_specs=P(("groups", "seq"), None, None),
        check_vma=False,
    )
```

```python
import functools

import jax
import jax.numpy as jnp
import numpy as np
from jax import lax
from jax.experimental import pallas as pl
from jax.experimental.pallas import tpu as pltpu
from jax.sharding import PartitionSpec as P


KVH = 4
QH = 64
HD = 128
BLK = 8
PLANES = 4
CHUNK = 256
SPAN = 128
LANES = 128
GRANT = 20 * 2**20
WIDE = 52 * 2**20
UNROLL = 4
PACKED = 4
NEG = -1e30


def frequencies(half_width):
    index = np.arange(half_width, dtype=np.float64)
    base = 1.0 / 500000.0 ** (index / half_width)
    wavelen = 2.0 * np.pi / base
    smooth = (8192.0 / wavelen - 1.0) / 3.0
    blended = (1.0 - smooth) * base / 8.0 + smooth * base
    scaled = np.where(wavelen > 8192.0, base / 8.0, blended)
    return np.where(wavelen < 2048.0, base, scaled)


def turn_tables(positions):
    freq = frequencies(HD // 2)
    angles = np.asarray(positions, np.float64)[:, None] * np.concatenate([freq, freq])[None]
    sign = np.where(np.arange(HD) < HD // 2, -1.0, 1.0)
    return jnp.array(np.cos(angles), jnp.float32), jnp.array(np.sin(angles) * sign, jnp.float32)


def pack_kernel(n, phase_table, target, keys, values, *refs):
    outs = refs[:n]
    slots, fill, rel, sems = refs[n:]
    blocks = keys.shape[0]
    in_plane = n // PLANES
    me = lax.axis_index("seq")
    plane, place = me // in_plane, me % in_plane

    def clear(p, _):
        for i in range(in_plane):
            fill[p * in_plane + i] = 0
            offset = i - place
            offset = jnp.where(offset < 0, offset + in_plane, offset)
            rel[p * in_plane + i] = phase_table[plane, p] * in_plane + offset
        return 0

    lax.fori_loop(0, PLANES, clear, 0)

    def put(step, _):
        ready = []
        for u in range(PACKED):
            b = step * PACKED + u
            dest = target[b]
            slot = fill[dest]
            fill[dest] = slot + 1
            ready.append((b, rel[dest], slot))
        for b, message, slot in ready:
            slots[message, 0, slot] = keys[b]
            slots[message, 1, slot] = values[b]
        return 0

    lax.fori_loop(0, blocks // PACKED, put, 0)
    copies = [pltpu.make_async_copy(slots.at[i], outs[i], sems.at[i]) for i in range(n)]
    for copy in copies:
        copy.start()
    for copy in copies:
        copy.wait()


def pack(n, cap, phase_table, target, keys, values):
    width = keys.shape[-1]
    message = jax.ShapeDtypeStruct((2, cap, BLK, width), jnp.bfloat16)
    smem = pl.BlockSpec(memory_space=pltpu.SMEM)
    vmem = pl.BlockSpec(memory_space=pltpu.VMEM)
    return pl.pallas_call(
        functools.partial(pack_kernel, n),
        out_shape=(message,) * n,
        in_specs=[smem] * 2 + [vmem] * 2,
        out_specs=(pl.BlockSpec(memory_space=pl.ANY),) * n,
        scratch_shapes=[
            pltpu.VMEM((n, 2, cap, BLK, width), jnp.bfloat16),
            pltpu.SMEM((n,), jnp.int32),
            pltpu.SMEM((n,), jnp.int32),
            pltpu.SemaphoreType.DMA((n,)),
        ],
        name="pack",
    )(phase_table, target, keys, values)


def twin_index(in_plane, index):
    plane = index // in_plane
    inner = (plane > 0) & (plane < PLANES - 1)
    return jnp.where(inner, (PLANES - 1 - 2 * plane) * in_plane + index, index)


def note_kernel(n, target, rows, lens, notes, fill):
    in_plane = n // PLANES

    def clear(i, _):
        fill[i] = 0
        return 0

    lax.fori_loop(0, n, clear, 0, unroll=min(n, 16))
    twin_of = functools.partial(twin_index, in_plane)
    my_twin = twin_of(lax.axis_index("seq"))
    for k in range(lens.shape[0]):
        notes[my_twin, 2 * LANES + k] = lens[k]

    def put(step, _):
        ready = []
        for u in range(PACKED):
            b = step * PACKED + u
            dest = target[b]
            slot = fill[dest]
            fill[dest] = slot + 1
            ready.append((dest, twin_of(dest), slot, rows[b]))
        for dest, twin, slot, row in ready:
            notes[dest, slot] = row
            notes[twin, LANES + slot] = row
        return 0

    lax.fori_loop(0, rows.shape[0] // PACKED, put, 0)

    def close(i, _):
        notes[i, LANES - 1] = fill[i]
        notes[twin_of(i), 2 * LANES - 1] = fill[i]
        return 0

    lax.fori_loop(0, n, close, 0, unroll=min(n, 4))


def note(n, target, rows, lens):
    smem = pl.BlockSpec(memory_space=pltpu.SMEM)
    return pl.pallas_call(
        functools.partial(note_kernel, n),
        out_shape=jax.ShapeDtypeStruct((n, 3 * LANES), jnp.int32),
        in_specs=[smem] * 3,
        out_specs=smem,
        scratch_shapes=[pltpu.SMEM((n,), jnp.int32)],
        name="note",
    )(target, rows, lens)


def index_kernel(n, cap, rows, notes, stages, place, row_of, rank_of, used, tally):
    f32 = jnp.float32

    def iotas(shape):
        return [lax.broadcasted_iota(jnp.int32, shape, d) for d in (0, 1)]

    a, b = iotas((cap, cap))
    before = (a < b).astype(f32)
    a, b = iotas((n, n))
    sooner = (b < a).astype(f32)
    lines = [jnp.broadcast_to(stages[i : i + 1, :n], (n, n)) for i in (2, 3)]
    posts = [
        jnp.sum(jnp.where(a == b, line, 0), axis=1, keepdims=True) for line in lines
    ]
    mates = [jnp.where(line == post, sooner, 0.0) for line, post in zip(lines, posts)]
    kernel, lane = iotas((8, LANES))
    counts = jnp.zeros((8, LANES), f32)
    for side in range(2):
        there = notes[:, side * LANES : (side + 1) * LANES]
        valid = lax.broadcasted_iota(jnp.int32, (n, cap), 1) < there[:, LANES - 1 :]
        rows_here = jnp.where(valid, there[:, :cap], -1)
        rank = jnp.zeros((n, cap), f32)
        local = jnp.zeros((n, cap), f32)
        for r in range(rows):
            hit = (rows_here == r).astype(f32)
            inside = jnp.dot(hit, before, preferred_element_type=f32)
            ahead = jnp.dot(sooner, hit, preferred_element_type=f32)
            near = jnp.dot(mates[side], hit, preferred_element_type=f32)
            rank += hit * (inside + jnp.sum(ahead, axis=1, keepdims=True))
            local += hit * (inside + jnp.sum(near, axis=1, keepdims=True))
            per_source = jnp.sum(hit, axis=1, keepdims=True)
            for stage in range(3):
                if (stage == 0) == (side == 1):
                    number = jnp.sum(
                        jnp.where(posts[side] == stage, per_source, 0.0), axis=0, keepdims=True
                    )
                    counts += jnp.where((kernel == stage) & (lane == r), number, 0.0)
        span = slice(side * n, side * n + n)
        place[span, :] = jnp.where(valid, local, -1.0).astype(jnp.int32)
        row_of[span, :] = jnp.maximum(rows_here, 0)
        rank_of[span, :] = rank.astype(jnp.int32)
        filled = jnp.sum(valid.astype(f32), axis=1, keepdims=True)
        used[span, :] = jnp.broadcast_to(filled, (n, cap)).astype(jnp.int32)
    a, b = iotas((LANES, LANES))
    begin = jnp.dot(counts, (a < b).astype(f32), preferred_element_type=f32)
    twin = twin_index(n // PLANES, lax.axis_index("seq"))
    source = lax.broadcasted_iota(jnp.int32, (n, LANES), 0)
    lens = jnp.sum(
        jnp.where(source == twin, notes[:, 2 * LANES :], 0), axis=0, keepdims=True
    )
    tally[0:8, :] = jnp.where(kernel == 3, lens, begin.astype(jnp.int32))
    tally[8:16, :] = (counts * BLK).astype(jnp.int32)


def index(n, cap, rows, notes, stages):
    vmem = pl.BlockSpec(memory_space=pltpu.VMEM)
    slots = jax.ShapeDtypeStruct((2 * n, cap), jnp.int32)
    return pl.pallas_call(
        functools.partial(index_kernel, n, cap, rows),
        out_shape=(slots,) * 4 + (jax.ShapeDtypeStruct((16, LANES), jnp.int32),),
        in_specs=[vmem] * 2,
        out_specs=(vmem,) * 5,
        compiler_params=pltpu.CompilerParams(vmem_limit_bytes=GRANT),
        name="index",
    )(notes, stages)


def as_wide(line, width):
    if width % HD == 0:
        return jnp.concatenate([line] * (width // HD), axis=1)
    return line[:, :width]


def blend(queries, pieces, old, guard=False):
    scale = HD ** (-0.5)
    heads = range(KVH)
    scores = [
        [
            jnp.where(
                piece[2],
                lax.dot_general(
                    queries[head],
                    piece[0][head],
                    (((1,), (1,)), ((), ())),
                    preferred_element_type=jnp.float32,
                )
                * scale,
                NEG,
            )
            for piece in pieces
        ]
        for head in heads
    ]
    new = []
    for head in heads:
        peak = functools.reduce(
            jnp.maximum, [jnp.max(one, axis=-1, keepdims=True) for one in scores[head]]
        )
        if old is None:
            new_top = jnp.broadcast_to(peak, (peak.shape[0], HD))
        else:
            old_acc, old_top, old_total = old[head]
            new_top = jnp.maximum(old_top, peak)
        raw = [jnp.exp(one - as_wide(new_top, one.shape[1])) for one in scores[head]]
        if guard:
            raw = [jnp.where(piece[2], one, 0.0) for piece, one in zip(pieces, raw)]
        added = sum(jnp.sum(one, axis=-1, keepdims=True) for one in raw)
        mixed = sum(
            jnp.dot(one.astype(jnp.bfloat16), piece[1][head], preferred_element_type=jnp.float32)
            for one, piece in zip(raw, pieces)
        )
        if old is None:
            new.append((mixed, new_top, jnp.broadcast_to(added, new_top.shape)))
        else:
            factor = jnp.exp(old_top - new_top)
            new.append((old_acc * factor + mixed, new_top, old_total * factor + added))
    return new


def held(row, state):
    return [tuple(one[row, head] for one in state) for head in range(KVH)]


def hold(row, state, new):
    for head in range(KVH):
        for one, value in zip(state, new[head]):
            one[row, head] = value


def row_queries(row, q_ref):
    return [q_ref[row, head] for head in range(KVH)]


def resident_kernel(
    lens, q_ref, step_k, step_v, keys, values, acc, top, total, kbuf, vbuf, sems
):
    rows, slot_count = kbuf.shape[0], kbuf.shape[1]
    piece = min(CHUNK, slot_count)
    pieces = slot_count // piece
    steps = step_k.shape[1]
    width = q_ref.shape[2]
    group = width // steps

    def copies(r, i):
        part = pl.ds(i * piece, piece)
        return (
            pltpu.make_async_copy(keys.at[r, part], kbuf.at[r, part], sems.at[0, r, i]),
            pltpu.make_async_copy(values.at[r, part], vbuf.at[r, part], sems.at[1, r, i]),
        )

    def fetch(r, _):
        for i in range(pieces):

            @pl.when((i == 0) | (i * piece < lens[r]))
            def _():
                for copy in copies(r, i):
                    copy.start()

        return 0

    lax.fori_loop(0, rows, fetch, 0)
    lane = lax.broadcasted_iota(jnp.int32, (width, piece), 1)
    causal = (
        lax.broadcasted_iota(jnp.int32, (width, steps), 1)
        <= lax.broadcasted_iota(jnp.int32, (width, steps), 0) // group
    )

    def one_row(r, _):
        def part(i):
            span = pl.ds(i * piece, piece)
            return (
                [kbuf[r, span, head * HD : (head + 1) * HD] for head in range(KVH)],
                [vbuf[r, span, head * HD : (head + 1) * HD] for head in range(KVH)],
                lane + i * piece < lens[r],
            )

        own = (
            [step_k[r, :, head * HD : (head + 1) * HD] for head in range(KVH)],
            [step_v[r, :, head * HD : (head + 1) * HD] for head in range(KVH)],
            causal,
        )
        state = (acc, top, total)
        for copy in copies(r, 0):
            copy.wait()
        hold(r, state, blend(row_queries(r, q_ref), [own, part(0)], None))
        for i in range(1, pieces):

            @pl.when(i * piece < lens[r])
            def _():
                for copy in copies(r, i):
                    copy.wait()
                hold(r, state, blend(row_queries(r, q_ref), [part(i)], held(r, state)))

        return 0

    lax.fori_loop(0, rows, one_row, 0)


def state_shapes(rows, width):
    shape = jax.ShapeDtypeStruct((rows, KVH, width, HD), jnp.float32)
    return (shape,) * 3


def resident(lens, grouped, step_k, step_v, keys, values):
    rows, slot_count, feature = keys.shape
    pieces = slot_count // min(CHUNK, slot_count)
    vmem = pl.BlockSpec(memory_space=pltpu.VMEM)
    hbm = pl.BlockSpec(memory_space=pltpu.HBM)
    return pl.pallas_call(
        resident_kernel,
        out_shape=state_shapes(rows, grouped.shape[2]),
        in_specs=[pl.BlockSpec(memory_space=pltpu.SMEM), vmem, vmem, vmem, hbm, hbm],
        out_specs=(vmem,) * 3,
        scratch_shapes=[
            pltpu.VMEM((rows, slot_count, feature), jnp.bfloat16),
            pltpu.VMEM((rows, slot_count, feature), jnp.bfloat16),
            pltpu.SemaphoreType.DMA((2, rows, pieces)),
        ],
        compiler_params=pltpu.CompilerParams(vmem_limit_bytes=WIDE),
        cost_estimate=pl.CostEstimate(
            flops=2 * 10**9, bytes_accessed=16 * 2**20, transcendentals=10**6
        ),
        name="resident",
    )(lens, grouped, step_k, step_v, keys, values)


def span_kernel(
    kind, kernel, first, count, cap, mine, place_of, row_of, rank_of, used, tally, lens,
    q_ref, ca, sa, cb, sb, *refs,
):
    messages = refs[:count]
    refs = refs[count:]
    before = refs[:3]
    if kind == "partial":
        out, stats, acc, top, total, kbuf, vbuf = refs
    elif kind == "state":
        part, stats, acc, top, total, kbuf, vbuf = refs[3:]
    else:
        out, acc, top, total, scr, kbuf, vbuf = refs[3:]
    state = (acc, top, total)
    rows = q_ref.shape[0]
    width = q_ref.shape[2]
    feature = kbuf.shape[1]
    last = tally[kernel, rows - 1] * BLK + tally[8 + kernel, rows - 1]
    tail = pl.ds(pl.multiple_of(last, BLK), SPAN)
    vbuf[tail, :] = jnp.zeros((SPAN, feature), jnp.float32)
    unroll = min(UNROLL, cap)
    trash = count * cap + SPAN // BLK
    for j in range(count):

        @pl.when(mine[1, first + j] == kernel)
        def _():
            source = mine[0, first + j]
            message = messages[j]

            def place(step, _):
                ready = []
                for u in range(unroll):
                    k = step * unroll + u
                    r = row_of[source, k]
                    rank = rank_of[source, k]
                    local = place_of[source, k]
                    slot = jnp.where(local < 0, trash, tally[kernel, r] + local)
                    length = tally[3, r] if kind == "partial" else lens[r]
                    fine, coarse = pl.ds(length % BLK, BLK), pl.ds(length // BLK + rank, 1)
                    c_a, s_a = ca[fine, :], sa[fine, :]
                    c_b, s_b = cb[coarse, :], sb[coarse, :]
                    cosine = c_a * c_b - s_a * s_b
                    sine = s_a * c_b + c_a * s_b
                    where = pl.ds(pl.multiple_of(slot * BLK, BLK), BLK)
                    value = message[1, k].astype(jnp.float32)
                    key = message[0, k].astype(jnp.float32)
                    turned = []
                    for head in range(KVH):
                        piece = key[:, head * HD : (head + 1) * HD]
                        turned.append(piece * cosine + pltpu.roll(piece, HD // 2, 1) * sine)
                    ready.append((where, turned, value))
                for where, turned, value in ready:
                    vbuf[where, :] = value
                    for head in range(KVH):
                        kbuf[where, head * HD : (head + 1) * HD] = turned[head]
                return 0

            lax.fori_loop(0, (used[source, 0] + unroll - 1) // unroll, place, 0)

    lane = lax.broadcasted_iota(jnp.int32, (width, SPAN), 1)
    eye = lax.broadcasted_iota(jnp.int32, (width, width), 0) == lax.broadcasted_iota(
        jnp.int32, (width, width), 1
    )

    def block(r, i):
        where = pl.ds(pl.multiple_of(tally[kernel, r] * BLK + i * SPAN, BLK), SPAN)
        return (
            [kbuf[where, h * HD : (h + 1) * HD].astype(jnp.bfloat16) for h in range(KVH)],
            [vbuf[where, h * HD : (h + 1) * HD].astype(jnp.bfloat16) for h in range(KVH)],
            lane + i * SPAN < tally[8 + kernel, r],
        )

    def beyond(r):
        def piece(i, _):
            hold(r, state, blend(row_queries(r, q_ref), [block(r, i)], held(r, state)))
            return 0

        lax.fori_loop(1, (tally[8 + kernel, r] + SPAN - 1) // SPAN, piece, 0)

    def partial_rows(pair):
        new = [blend(row_queries(r, q_ref), [block(r, 0)], None, guard=True) for r in pair]
        for r, one in zip(pair, new):
            hold(r, state, one)
        for r in pair:
            beyond(r)
        done = []
        for r in pair:
            for head in range(KVH):
                amount = total[r, head]
                safe = jnp.where(amount > 0.0, amount, 1.0)
                lines = [
                    jnp.sum(jnp.where(eye, one[:, :width], 0.0), axis=0, keepdims=True)
                    for one in (top[r, head], amount)
                ]
                done.append((r, head, (acc[r, head] / safe).astype(jnp.bfloat16), lines))
        for r, head, value, lines in done:
            out[r, head] = value
            for i in range(2):
                stats[r, head, pl.ds(i, 1), :] = lines[i]

    def with_part(r, new):
        merged = []
        for head in range(KVH):
            lines = []
            for i in range(2):
                line = jnp.broadcast_to(stats[r, head, pl.ds(i, 1), :], (width, width))
                lines.append(jnp.sum(jnp.where(eye, line, 0.0), axis=1, keepdims=True))
            other_top, other_total = lines
            other_top = jnp.where(other_total > 0.0, other_top, NEG)
            value, old_top, amount = new[head]
            new_top = jnp.maximum(old_top, other_top)
            mine = jnp.exp(old_top - new_top)
            theirs = jnp.exp(other_top - new_top) * other_total
            merged.append(
                (
                    value * mine + part[r, head].astype(jnp.float32) * theirs,
                    new_top,
                    amount * mine + theirs,
                )
            )
        return merged

    def state_rows(pair):
        new = [blend(row_queries(r, q_ref), [block(r, 0)], held(r, before)) for r in pair]
        new = [with_part(r, one) for r, one in zip(pair, new)]
        for r, one in zip(pair, new):
            hold(r, state, one)
        for r in pair:
            beyond(r)

    def put_out(pair, new):
        done = [value / amount for one in new for value, _, amount in one]
        for i, value in enumerate(done):
            scr[i] = value
        steps = out.shape[1]
        group = width // steps
        for i, r in enumerate(pair):
            for head in range(KVH):
                for g in range(group):
                    column = (head * group + g) * HD
                    out[r, :, column : column + HD] = scr[
                        i * KVH + head, pl.ds(g, steps, stride=group), :
                    ].astype(jnp.bfloat16)

    def final_rows(pair):
        new = [blend(row_queries(r, q_ref), [block(r, 0)], held(r, before)) for r in pair]
        put_out(pair, new)
        longest = functools.reduce(jnp.maximum, [tally[8 + kernel, r] for r in pair])

        @pl.when(longest > SPAN)
        def _():
            for r, one in zip(pair, new):
                hold(r, state, one)
            for r in pair:
                beyond(r)
            put_out(pair, [held(r, state) for r in pair])

    run = {"partial": partial_rows, "state": state_rows, "final": final_rows}[kind]
    together = 2 if rows % 2 == 0 else 1

    def some_rows(i, _):
        run([i * together + u for u in range(together)])
        return 0

    lax.fori_loop(0, rows // together, some_rows, 0)


def span(kind, kernel, first, cap, scalars, grouped, tables, messages, state, extra, steps):
    rows, _, width, _ = grouped.shape
    feature = messages[0].shape[-1]
    count = len(messages)
    room = (count * cap + 1) * BLK + SPAN
    smem = pl.BlockSpec(memory_space=pltpu.SMEM)
    vmem = pl.BlockSpec(memory_space=pltpu.VMEM)
    running = [pltpu.VMEM((rows, KVH, width, HD), jnp.float32)] * 3
    scratch = []
    if kind == "partial":
        out_shape = (
            jax.ShapeDtypeStruct((rows, KVH, width, HD), jnp.bfloat16),
            jax.ShapeDtypeStruct((rows, KVH, 2, width), jnp.float32),
        )
        scratch += running
    elif kind == "state":
        out_shape = state_shapes(rows, width)
    else:
        out_shape = jax.ShapeDtypeStruct((rows, steps, QH * HD), jnp.bfloat16)
        scratch += running + [pltpu.VMEM((2 * KVH, width, HD), jnp.float32)]
    scratch += [pltpu.VMEM((room, feature), jnp.float32)] * 2
    return pl.pallas_call(
        functools.partial(span_kernel, kind, kernel, first, count, cap),
        out_shape=out_shape,
        in_specs=[smem] * 7 + [vmem] * (5 + count + len(state) + len(extra)),
        out_specs=jax.tree.map(lambda _: vmem, out_shape),
        scratch_shapes=scratch,
        compiler_params=pltpu.CompilerParams(vmem_limit_bytes=GRANT),
        cost_estimate=pl.CostEstimate(
            flops=10**9, bytes_accessed=12 * 2**20, transcendentals=10**6
        ),
    )(*scalars, grouped, *tables, *messages, *state, *extra)


PHASES = {"d": (2, 2, 2, 2), "f": (0, 3, 3, 0), "g": (3, 0, 0, 3), "b": (1, 1, 1, 1)}


def site_plane(plane, flip):
    dest = plane ^ flip
    half = PLANES // 2
    if (plane < half) != (dest < half) and dest in (half - 1, half):
        return PLANES - 1 - dest
    return dest


def came_from(phase, plane):
    flips = PHASES[phase]
    return next(s for s in range(PLANES) if site_plane(s, flips[s]) == plane)


def for_mirror(phase, plane):
    source = came_from(phase, plane)
    return int(source ^ PHASES[phase][source] != plane)


def route(n, phase, offset):
    in_plane = n // PLANES
    return [
        (
            plane * in_plane + place,
            site_plane(plane, flip) * in_plane + (place + offset) % in_plane,
        )
        for plane, flip in enumerate(PHASES[phase])
        for place in range(in_plane)
    ]


STAGE = {"d": 1, "f": 1, "g": 1, "b": 2}


def device_tables(n):
    in_plane = n // PLANES
    lines = []
    for me in range(n):
        plane, place = me // in_plane, me % in_plane
        entry, stage = [], []
        post = [[-1] * n, [-1] * n]
        for phase in PHASES:
            mirror = for_mirror(phase, plane)
            for offset in range(in_plane):
                source = came_from(phase, plane) * in_plane + (place - offset) % in_plane
                entry.append(mirror * n + source)
                stage.append(0 if mirror else STAGE[phase])
                post[mirror][source] = stage[-1]
        lines.append((entry, stage, post[0], post[1]))
    return np.array(lines, np.int32)


def body(
    span_keys,
    span_values,
    block_device,
    block_row,
    cache_len,
    cache_keys,
    cache_values,
    queries,
    step_keys,
    step_values,
):
    n = lax.axis_size("seq")
    in_plane = n // PLANES
    me = lax.axis_index("seq").astype(jnp.int32)
    rows = cache_len.shape[0]
    feature = span_keys.shape[1]
    blocks = span_keys.shape[0] // BLK
    cap = max(2, (2 * blocks + n - 1) // n)
    steps = queries.shape[1]
    group = QH // KVH
    names = list(PHASES)

    phase_table = jnp.array(
        [
            [next(i for i, p in enumerate(names) if PHASES[p][z] == z ^ d) for d in range(PLANES)]
            for z in range(PLANES)
        ],
        jnp.int32,
    )
    half = PLANES // 2
    swap = [
        (a * in_plane + i, b * in_plane + i)
        for a, b in ((half - 1, half), (half, half - 1))
        for i in range(in_plane)
    ]
    mirrored = lax.ppermute(queries, "seq", swap)
    messages = pack(
        n,
        cap,
        phase_table,
        block_device[:, 0],
        span_keys.reshape(blocks, BLK, feature),
        span_values.reshape(blocks, BLK, feature),
    )
    packed = {p: messages[i * in_plane : (i + 1) * in_plane] for i, p in enumerate(names)}

    def send(phase):
        out = []
        for offset in range(in_plane):
            value = packed[phase][offset]
            pairs = route(n, phase, offset)
            if any(a != b for a, b in pairs):
                value = lax.ppermute(value, "seq", pairs)
            out.append(value)
        return out

    got = {phase: send(phase) for phase in names}

    def regroup(value):
        value = value.reshape(rows, steps, KVH, group, HD).transpose(0, 2, 1, 3, 4)
        return value.reshape(rows, KVH, steps * group, HD)

    mirrored = regroup(mirrored)

    notes = note(n, block_device[:, 0], block_row, cache_len)
    notes = lax.all_to_all(notes, "seq", split_axis=0, concat_axis=0, tiled=True)
    mine = lax.dynamic_index_in_dim(jnp.array(device_tables(n)), me, 0, keepdims=False)
    *slots, tally = index(n, cap, rows, notes, mine)
    reach = cache_keys.shape[1] // BLK + n * cap + 1
    tables = turn_tables(np.arange(2 * BLK)) + turn_tables(np.arange(reach) * BLK)
    scalars = (mine, *slots, tally, cache_len)

    partial, stats = span(
        "partial", 0, 0, cap, scalars, mirrored, tables,
        got["d"] + got["f"], (), (), steps,
    )
    queries, partial = lax.optimization_barrier((queries, partial))
    grouped = regroup(queries)
    state = resident(cache_len, grouped, step_keys, step_values, cache_keys, cache_values)
    partial = lax.ppermute(partial, "seq", swap)
    stats = lax.ppermute(stats, "seq", swap)
    state = span(
        "state", 1, 0, cap, scalars, grouped, tables,
        got["d"] + got["f"] + got["g"], tuple(state), (partial, stats), steps,
    )
    return span(
        "final", 2, 3 * in_plane, cap, scalars, grouped, tables,
        got["b"], tuple(state), (), steps,
    )


def solution(mesh):
    placed = (
        P(("groups", "seq"), None),
        P(("groups", "seq"), None),
        P(("groups", "seq"), None),
        P(("groups", "seq")),
        P(("groups", "seq")),
        P(("groups", "seq"), None, None),
        P(("groups", "seq"), None, None),
        P(("groups", "seq"), None, None),
        P(("groups", "seq"), None, None),
        P(("groups", "seq"), None, None),
    )

    return jax.shard_map(
        body,
        mesh=mesh,
        in_specs=placed,
        out_specs=P(("groups", "seq"), None, None),
        check_vma=False,
    )
```

```python
import functools

import jax
import jax.numpy as jnp
import numpy as np
from jax import lax
from jax.experimental import pallas as pl
from jax.experimental.pallas import tpu as pltpu
from jax.sharding import PartitionSpec as P


KVH = 4
QH = 64
HD = 128
BLK = 8
PLANES = 4
CHUNK = 256
SPAN = 128
LANES = 128
GRANT = 20 * 2**20
WIDE = 52 * 2**20
UNROLL = 4
PACKED = 4
NEG = -1e30


def frequencies(half_width):
    index = np.arange(half_width, dtype=np.float64)
    base = 1.0 / 500000.0 ** (index / half_width)
    wavelen = 2.0 * np.pi / base
    smooth = (8192.0 / wavelen - 1.0) / 3.0
    blended = (1.0 - smooth) * base / 8.0 + smooth * base
    scaled = np.where(wavelen > 8192.0, base / 8.0, blended)
    return np.where(wavelen < 2048.0, base, scaled)


def turn_tables(positions):
    freq = frequencies(HD // 2)
    angles = np.asarray(positions, np.float64)[:, None] * np.concatenate([freq, freq])[None]
    sign = np.where(np.arange(HD) < HD // 2, -1.0, 1.0)
    return jnp.array(np.cos(angles), jnp.float32), jnp.array(np.sin(angles) * sign, jnp.float32)


def pack_kernel(n, phase_table, target, keys, values, *refs):
    outs = refs[:n]
    slots, fill, rel, sems = refs[n:]
    blocks = keys.shape[0]
    in_plane = n // PLANES
    me = lax.axis_index("seq")
    plane, place = me // in_plane, me % in_plane

    def clear(p, _):
        for i in range(in_plane):
            fill[p * in_plane + i] = 0
            offset = i - place
            offset = jnp.where(offset < 0, offset + in_plane, offset)
            rel[p * in_plane + i] = phase_table[plane, p] * in_plane + offset
        return 0

    lax.fori_loop(0, PLANES, clear, 0)

    def put(step, _):
        ready = []
        for u in range(PACKED):
            b = step * PACKED + u
            dest = target[b]
            slot = fill[dest]
            fill[dest] = slot + 1
            ready.append((b, rel[dest], slot))
        for b, message, slot in ready:
            slots[message, 0, slot] = keys[b]
            slots[message, 1, slot] = values[b]
        return 0

    lax.fori_loop(0, blocks // PACKED, put, 0)
    copies = [pltpu.make_async_copy(slots.at[i], outs[i], sems.at[i]) for i in range(n)]
    for copy in copies:
        copy.start()
    for copy in copies:
        copy.wait()


def pack(n, cap, phase_table, target, keys, values):
    width = keys.shape[-1]
    message = jax.ShapeDtypeStruct((2, cap, BLK, width), jnp.bfloat16)
    smem = pl.BlockSpec(memory_space=pltpu.SMEM)
    vmem = pl.BlockSpec(memory_space=pltpu.VMEM)
    return pl.pallas_call(
        functools.partial(pack_kernel, n),
        out_shape=(message,) * n,
        in_specs=[smem] * 2 + [vmem] * 2,
        out_specs=(pl.BlockSpec(memory_space=pl.ANY),) * n,
        scratch_shapes=[
            pltpu.VMEM((n, 2, cap, BLK, width), jnp.bfloat16),
            pltpu.SMEM((n,), jnp.int32),
            pltpu.SMEM((n,), jnp.int32),
            pltpu.SemaphoreType.DMA((n,)),
        ],
        name="pack",
    )(phase_table, target, keys, values)


def twin_index(in_plane, index):
    plane = index // in_plane
    inner = (plane > 0) & (plane < PLANES - 1)
    return jnp.where(inner, (PLANES - 1 - 2 * plane) * in_plane + index, index)


def note_kernel(n, target, rows, lens, notes, fill, twins):
    in_plane = n // PLANES

    def clear(i, _):
        fill[i] = 0
        twins[i] = twin_index(in_plane, i)
        return 0

    lax.fori_loop(0, n, clear, 0, unroll=min(n, 16))
    my_twin = twins[lax.axis_index("seq")]
    for k in range(lens.shape[0]):
        notes[my_twin, 2 * LANES + k] = lens[k]

    def put(step, _):
        ready = []
        for u in range(PACKED):
            b = step * PACKED + u
            dest = target[b]
            slot = fill[dest]
            fill[dest] = slot + 1
            ready.append((dest, twins[dest], slot, rows[b]))
        for dest, twin, slot, row in ready:
            notes[dest, slot] = row
            notes[twin, LANES + slot] = row
        return 0

    lax.fori_loop(0, rows.shape[0] // PACKED, put, 0)

    def close(i, _):
        notes[i, LANES - 1] = fill[i]
        notes[twins[i], 2 * LANES - 1] = fill[i]
        return 0

    lax.fori_loop(0, n, close, 0, unroll=min(n, 4))


def note(n, target, rows, lens):
    smem = pl.BlockSpec(memory_space=pltpu.SMEM)
    return pl.pallas_call(
        functools.partial(note_kernel, n),
        out_shape=jax.ShapeDtypeStruct((n, 3 * LANES), jnp.int32),
        in_specs=[smem] * 3,
        out_specs=smem,
        scratch_shapes=[pltpu.SMEM((n,), jnp.int32), pltpu.SMEM((n,), jnp.int32)],
        name="note",
    )(target, rows, lens)


def index_kernel(n, cap, rows, notes, stages, place, row_of, rank_of, used, tally):
    f32 = jnp.float32

    def iotas(shape):
        return [lax.broadcasted_iota(jnp.int32, shape, d) for d in (0, 1)]

    a, b = iotas((cap, cap))
    before = (a < b).astype(f32)
    a, b = iotas((n, n))
    sooner = (b < a).astype(f32)
    lines = [jnp.broadcast_to(stages[i : i + 1, :n], (n, n)) for i in (2, 3)]
    posts = [
        jnp.sum(jnp.where(a == b, line, 0), axis=1, keepdims=True) for line in lines
    ]
    mates = [jnp.where(line == post, sooner, 0.0) for line, post in zip(lines, posts)]
    kernel, lane = iotas((8, LANES))
    counts = jnp.zeros((8, LANES), f32)
    for side in range(2):
        there = notes[:, side * LANES : (side + 1) * LANES]
        valid = lax.broadcasted_iota(jnp.int32, (n, cap), 1) < there[:, LANES - 1 :]
        rows_here = jnp.where(valid, there[:, :cap], -1)
        rank = jnp.zeros((n, cap), f32)
        local = jnp.zeros((n, cap), f32)
        for r in range(rows):
            hit = (rows_here == r).astype(f32)
            inside = jnp.dot(hit, before, preferred_element_type=f32)
            ahead = jnp.dot(sooner, hit, preferred_element_type=f32)
            near = jnp.dot(mates[side], hit, preferred_element_type=f32)
            rank += hit * (inside + jnp.sum(ahead, axis=1, keepdims=True))
            local += hit * (inside + jnp.sum(near, axis=1, keepdims=True))
            per_source = jnp.sum(hit, axis=1, keepdims=True)
            for stage in range(3):
                if (stage == 0) == (side == 1):
                    number = jnp.sum(
                        jnp.where(posts[side] == stage, per_source, 0.0), axis=0, keepdims=True
                    )
                    counts += jnp.where((kernel == stage) & (lane == r), number, 0.0)
        span = slice(side * n, side * n + n)
        place[span, :] = jnp.where(valid, local, -1.0).astype(jnp.int32)
        row_of[span, :] = jnp.maximum(rows_here, 0)
        rank_of[span, :] = rank.astype(jnp.int32)
        filled = jnp.sum(valid.astype(f32), axis=1, keepdims=True)
        used[span, :] = jnp.broadcast_to(filled, (n, cap)).astype(jnp.int32)
    a, b = iotas((LANES, LANES))
    begin = jnp.dot(counts, (a < b).astype(f32), preferred_element_type=f32)
    twin = twin_index(n // PLANES, lax.axis_index("seq"))
    source = lax.broadcasted_iota(jnp.int32, (n, LANES), 0)
    lens = jnp.sum(
        jnp.where(source == twin, notes[:, 2 * LANES :], 0), axis=0, keepdims=True
    )
    tally[0:8, :] = jnp.where(kernel == 3, lens, begin.astype(jnp.int32))
    tally[8:16, :] = (counts * BLK).astype(jnp.int32)


def index(n, cap, rows, notes, stages):
    vmem = pl.BlockSpec(memory_space=pltpu.VMEM)
    slots = jax.ShapeDtypeStruct((2 * n, cap), jnp.int32)
    return pl.pallas_call(
        functools.partial(index_kernel, n, cap, rows),
        out_shape=(slots,) * 4 + (jax.ShapeDtypeStruct((16, LANES), jnp.int32),),
        in_specs=[vmem] * 2,
        out_specs=(vmem,) * 5,
        compiler_params=pltpu.CompilerParams(vmem_limit_bytes=GRANT),
        name="index",
    )(notes, stages)


def as_wide(line, width):
    if width % HD == 0:
        return jnp.concatenate([line] * (width // HD), axis=1)
    return line[:, :width]


def blend(queries, pieces, old, guard=False):
    scale = HD ** (-0.5)
    heads = range(KVH)
    scores = [
        [
            jnp.where(
                piece[2],
                lax.dot_general(
                    queries[head],
                    piece[0][head],
                    (((1,), (1,)), ((), ())),
                    preferred_element_type=jnp.float32,
                )
                * scale,
                NEG,
            )
            for piece in pieces
        ]
        for head in heads
    ]
    new = []
    for head in heads:
        peak = functools.reduce(
            jnp.maximum, [jnp.max(one, axis=-1, keepdims=True) for one in scores[head]]
        )
        if old is None:
            new_top = jnp.broadcast_to(peak, (peak.shape[0], HD))
        else:
            old_acc, old_top, old_total = old[head]
            new_top = jnp.maximum(old_top, peak)
        raw = [jnp.exp(one - as_wide(new_top, one.shape[1])) for one in scores[head]]
        if guard:
            raw = [jnp.where(piece[2], one, 0.0) for piece, one in zip(pieces, raw)]
        added = sum(jnp.sum(one, axis=-1, keepdims=True) for one in raw)
        mixed = sum(
            jnp.dot(one.astype(jnp.bfloat16), piece[1][head], preferred_element_type=jnp.float32)
            for one, piece in zip(raw, pieces)
        )
        if old is None:
            new.append((mixed, new_top, jnp.broadcast_to(added, new_top.shape)))
        else:
            factor = jnp.exp(old_top - new_top)
            new.append((old_acc * factor + mixed, new_top, old_total * factor + added))
    return new


def held(row, state):
    return [tuple(one[row, head] for one in state) for head in range(KVH)]


def hold(row, state, new):
    for head in range(KVH):
        for one, value in zip(state, new[head]):
            one[row, head] = value


def row_queries(row, q_ref):
    return [q_ref[row, head] for head in range(KVH)]


def resident_kernel(
    lens, q_ref, step_k, step_v, keys, values, acc, top, total, kbuf, vbuf, sems
):
    rows, slot_count = kbuf.shape[0], kbuf.shape[1]
    piece = min(CHUNK, slot_count)
    pieces = slot_count // piece
    steps = step_k.shape[1]
    width = q_ref.shape[2]
    group = width // steps

    def copies(r, i):
        part = pl.ds(i * piece, piece)
        return (
            pltpu.make_async_copy(keys.at[r, part], kbuf.at[r, part], sems.at[0, r, i]),
            pltpu.make_async_copy(values.at[r, part], vbuf.at[r, part], sems.at[1, r, i]),
        )

    def fetch(r, _):
        for i in range(pieces):

            @pl.when((i == 0) | (i * piece < lens[r]))
            def _():
                for copy in copies(r, i):
                    copy.start()

        return 0

    lax.fori_loop(0, rows, fetch, 0)
    lane = lax.broadcasted_iota(jnp.int32, (width, piece), 1)
    causal = (
        lax.broadcasted_iota(jnp.int32, (width, steps), 1)
        <= lax.broadcasted_iota(jnp.int32, (width, steps), 0) // group
    )

    def one_row(r, _):
        def part(i):
            span = pl.ds(i * piece, piece)
            return (
                [kbuf[r, span, head * HD : (head + 1) * HD] for head in range(KVH)],
                [vbuf[r, span, head * HD : (head + 1) * HD] for head in range(KVH)],
                lane + i * piece < lens[r],
            )

        own = (
            [step_k[r, :, head * HD : (head + 1) * HD] for head in range(KVH)],
            [step_v[r, :, head * HD : (head + 1) * HD] for head in range(KVH)],
            causal,
        )
        state = (acc, top, total)
        for copy in copies(r, 0):
            copy.wait()
        hold(r, state, blend(row_queries(r, q_ref), [own, part(0)], None))
        for i in range(1, pieces):

            @pl.when(i * piece < lens[r])
            def _():
                for copy in copies(r, i):
                    copy.wait()
                hold(r, state, blend(row_queries(r, q_ref), [part(i)], held(r, state)))

        return 0

    lax.fori_loop(0, rows, one_row, 0)


def state_shapes(rows, width):
    shape = jax.ShapeDtypeStruct((rows, KVH, width, HD), jnp.float32)
    return (shape,) * 3


def resident(lens, grouped, step_k, step_v, keys, values):
    rows, slot_count, feature = keys.shape
    pieces = slot_count // min(CHUNK, slot_count)
    vmem = pl.BlockSpec(memory_space=pltpu.VMEM)
    hbm = pl.BlockSpec(memory_space=pltpu.HBM)
    return pl.pallas_call(
        resident_kernel,
        out_shape=state_shapes(rows, grouped.shape[2]),
        in_specs=[pl.BlockSpec(memory_space=pltpu.SMEM), vmem, vmem, vmem, hbm, hbm],
        out_specs=(vmem,) * 3,
        scratch_shapes=[
            pltpu.VMEM((rows, slot_count, feature), jnp.bfloat16),
            pltpu.VMEM((rows, slot_count, feature), jnp.bfloat16),
            pltpu.SemaphoreType.DMA((2, rows, pieces)),
        ],
        compiler_params=pltpu.CompilerParams(vmem_limit_bytes=WIDE),
        cost_estimate=pl.CostEstimate(
            flops=2 * 10**9, bytes_accessed=16 * 2**20, transcendentals=10**6
        ),
        name="resident",
    )(lens, grouped, step_k, step_v, keys, values)


def span_kernel(
    kind, kernel, first, count, cap, mine, place_of, row_of, rank_of, used, tally, lens,
    q_ref, ca, sa, cb, sb, *refs,
):
    messages = refs[:count]
    refs = refs[count:]
    before = refs[:3]
    if kind == "partial":
        out, stats, acc, top, total, kbuf, vbuf = refs
    elif kind == "state":
        part, stats, acc, top, total, kbuf, vbuf = refs[3:]
    else:
        out, acc, top, total, scr, kbuf, vbuf = refs[3:]
    state = (acc, top, total)
    rows = q_ref.shape[0]
    width = q_ref.shape[2]
    feature = kbuf.shape[1]
    last = tally[kernel, rows - 1] * BLK + tally[8 + kernel, rows - 1]
    tail = pl.ds(pl.multiple_of(last, BLK), SPAN)
    vbuf[tail, :] = jnp.zeros((SPAN, feature), jnp.float32)
    unroll = min(UNROLL, cap)
    trash = count * cap + SPAN // BLK
    for j in range(count):

        @pl.when(mine[1, first + j] == kernel)
        def _():
            source = mine[0, first + j]
            message = messages[j]

            def place(step, _):
                ready = []
                for u in range(unroll):
                    k = step * unroll + u
                    r = row_of[source, k]
                    rank = rank_of[source, k]
                    local = place_of[source, k]
                    slot = jnp.where(local < 0, trash, tally[kernel, r] + local)
                    length = tally[3, r] if kind == "partial" else lens[r]
                    fine, coarse = pl.ds(length % BLK, BLK), pl.ds(length // BLK + rank, 1)
                    c_a, s_a = ca[fine, :], sa[fine, :]
                    c_b, s_b = cb[coarse, :], sb[coarse, :]
                    cosine = c_a * c_b - s_a * s_b
                    sine = s_a * c_b + c_a * s_b
                    where = pl.ds(pl.multiple_of(slot * BLK, BLK), BLK)
                    value = message[1, k].astype(jnp.float32)
                    key = message[0, k].astype(jnp.float32)
                    turned = []
                    for head in range(KVH):
                        piece = key[:, head * HD : (head + 1) * HD]
                        turned.append(piece * cosine + pltpu.roll(piece, HD // 2, 1) * sine)
                    ready.append((where, turned, value))
                for where, turned, value in ready:
                    vbuf[where, :] = value
                    for head in range(KVH):
                        kbuf[where, head * HD : (head + 1) * HD] = turned[head]
                return 0

            lax.fori_loop(0, (used[source, 0] + unroll - 1) // unroll, place, 0)

    lane = lax.broadcasted_iota(jnp.int32, (width, SPAN), 1)
    eye = lax.broadcasted_iota(jnp.int32, (width, width), 0) == lax.broadcasted_iota(
        jnp.int32, (width, width), 1
    )

    def block(r, i):
        where = pl.ds(pl.multiple_of(tally[kernel, r] * BLK + i * SPAN, BLK), SPAN)
        return (
            [kbuf[where, h * HD : (h + 1) * HD].astype(jnp.bfloat16) for h in range(KVH)],
            [vbuf[where, h * HD : (h + 1) * HD].astype(jnp.bfloat16) for h in range(KVH)],
            lane + i * SPAN < tally[8 + kernel, r],
        )

    def beyond(r):
        def piece(i, _):
            hold(r, state, blend(row_queries(r, q_ref), [block(r, i)], held(r, state)))
            return 0

        lax.fori_loop(1, (tally[8 + kernel, r] + SPAN - 1) // SPAN, piece, 0)

    def partial_rows(pair):
        new = [blend(row_queries(r, q_ref), [block(r, 0)], None, guard=True) for r in pair]
        for r, one in zip(pair, new):
            hold(r, state, one)
        for r in pair:
            beyond(r)
        done = []
        for r in pair:
            for head in range(KVH):
                amount = total[r, head]
                safe = jnp.where(amount > 0.0, amount, 1.0)
                lines = [
                    jnp.sum(jnp.where(eye, one[:, :width], 0.0), axis=0, keepdims=True)
                    for one in (top[r, head], amount)
                ]
                done.append((r, head, (acc[r, head] / safe).astype(jnp.bfloat16), lines))
        for r, head, value, lines in done:
            out[r, head] = value
            for i in range(2):
                stats[r, head, pl.ds(i, 1), :] = lines[i]

    def with_part(r, new):
        merged = []
        for head in range(KVH):
            lines = []
            for i in range(2):
                line = jnp.broadcast_to(stats[r, head, pl.ds(i, 1), :], (width, width))
                lines.append(jnp.sum(jnp.where(eye, line, 0.0), axis=1, keepdims=True))
            other_top, other_total = lines
            other_top = jnp.where(other_total > 0.0, other_top, NEG)
            value, old_top, amount = new[head]
            new_top = jnp.maximum(old_top, other_top)
            mine = jnp.exp(old_top - new_top)
            theirs = jnp.exp(other_top - new_top) * other_total
            merged.append(
                (
                    value * mine + part[r, head].astype(jnp.float32) * theirs,
                    new_top,
                    amount * mine + theirs,
                )
            )
        return merged

    def state_rows(pair):
        new = [blend(row_queries(r, q_ref), [block(r, 0)], held(r, before)) for r in pair]
        new = [with_part(r, one) for r, one in zip(pair, new)]
        for r, one in zip(pair, new):
            hold(r, state, one)
        for r in pair:
            beyond(r)

    def put_out(pair, new):
        done = [value / amount for one in new for value, _, amount in one]
        for i, value in enumerate(done):
            scr[i] = value
        steps = out.shape[1]
        group = width // steps
        for i, r in enumerate(pair):
            for head in range(KVH):
                for g in range(group):
                    column = (head * group + g) * HD
                    out[r, :, column : column + HD] = scr[
                        i * KVH + head, pl.ds(g, steps, stride=group), :
                    ].astype(jnp.bfloat16)

    def final_rows(pair):
        new = [blend(row_queries(r, q_ref), [block(r, 0)], held(r, before)) for r in pair]
        put_out(pair, new)
        longest = functools.reduce(jnp.maximum, [tally[8 + kernel, r] for r in pair])

        @pl.when(longest > SPAN)
        def _():
            for r, one in zip(pair, new):
                hold(r, state, one)
            for r in pair:
                beyond(r)
            put_out(pair, [held(r, state) for r in pair])

    run = {"partial": partial_rows, "state": state_rows, "final": final_rows}[kind]
    together = 2 if rows % 2 == 0 else 1

    def some_rows(i, _):
        run([i * together + u for u in range(together)])
        return 0

    lax.fori_loop(0, rows // together, some_rows, 0)


def span(kind, kernel, first, cap, scalars, grouped, tables, messages, state, extra, steps):
    rows, _, width, _ = grouped.shape
    feature = messages[0].shape[-1]
    count = len(messages)
    room = (count * cap + 1) * BLK + SPAN
    smem = pl.BlockSpec(memory_space=pltpu.SMEM)
    vmem = pl.BlockSpec(memory_space=pltpu.VMEM)
    running = [pltpu.VMEM((rows, KVH, width, HD), jnp.float32)] * 3
    scratch = []
    if kind == "partial":
        out_shape = (
            jax.ShapeDtypeStruct((rows, KVH, width, HD), jnp.bfloat16),
            jax.ShapeDtypeStruct((rows, KVH, 2, width), jnp.float32),
        )
        scratch += running
    elif kind == "state":
        out_shape = state_shapes(rows, width)
    else:
        out_shape = jax.ShapeDtypeStruct((rows, steps, QH * HD), jnp.bfloat16)
        scratch += running + [pltpu.VMEM((2 * KVH, width, HD), jnp.float32)]
    scratch += [pltpu.VMEM((room, feature), jnp.float32)] * 2
    return pl.pallas_call(
        functools.partial(span_kernel, kind, kernel, first, count, cap),
        out_shape=out_shape,
        in_specs=[smem] * 7 + [vmem] * (5 + count + len(state) + len(extra)),
        out_specs=jax.tree.map(lambda _: vmem, out_shape),
        scratch_shapes=scratch,
        compiler_params=pltpu.CompilerParams(vmem_limit_bytes=GRANT),
        cost_estimate=pl.CostEstimate(
            flops=10**9, bytes_accessed=12 * 2**20, transcendentals=10**6
        ),
    )(*scalars, grouped, *tables, *messages, *state, *extra)


PHASES = {"e": (2, 1, 1, 2), "f": (0, 3, 3, 0), "g": (3, 0, 0, 3), "h": (1, 2, 2, 1)}


def site_plane(plane, flip):
    dest = plane ^ flip
    half = PLANES // 2
    if (plane < half) != (dest < half) and dest in (half - 1, half):
        return PLANES - 1 - dest
    return dest


def came_from(phase, plane):
    flips = PHASES[phase]
    return next(s for s in range(PLANES) if site_plane(s, flips[s]) == plane)


def for_mirror(phase, plane):
    source = came_from(phase, plane)
    return int(source ^ PHASES[phase][source] != plane)


def route(n, phase, offset):
    in_plane = n // PLANES
    return [
        (
            plane * in_plane + place,
            site_plane(plane, flip) * in_plane + (place + offset) % in_plane,
        )
        for plane, flip in enumerate(PHASES[phase])
        for place in range(in_plane)
    ]


STAGE = {"e": 1, "f": 1, "g": 1, "h": 2}


def device_tables(n):
    in_plane = n // PLANES
    lines = []
    for me in range(n):
        plane, place = me // in_plane, me % in_plane
        entry, stage = [], []
        post = [[-1] * n, [-1] * n]
        for phase in PHASES:
            mirror = for_mirror(phase, plane)
            for offset in range(in_plane):
                source = came_from(phase, plane) * in_plane + (place - offset) % in_plane
                entry.append(mirror * n + source)
                stage.append(0 if mirror else STAGE[phase])
                post[mirror][source] = stage[-1]
        lines.append((entry, stage, post[0], post[1]))
    return np.array(lines, np.int32)


def body(
    span_keys,
    span_values,
    block_device,
    block_row,
    cache_len,
    cache_keys,
    cache_values,
    queries,
    step_keys,
    step_values,
):
    n = lax.axis_size("seq")
    in_plane = n // PLANES
    me = lax.axis_index("seq").astype(jnp.int32)
    rows = cache_len.shape[0]
    feature = span_keys.shape[1]
    blocks = span_keys.shape[0] // BLK
    cap = max(2, (2 * blocks + n - 1) // n)
    steps = queries.shape[1]
    group = QH // KVH
    names = list(PHASES)

    phase_table = jnp.array(
        [
            [next(i for i, p in enumerate(names) if PHASES[p][z] == z ^ d) for d in range(PLANES)]
            for z in range(PLANES)
        ],
        jnp.int32,
    )
    half = PLANES // 2
    swap = [
        (a * in_plane + i, b * in_plane + i)
        for a, b in ((half - 1, half), (half, half - 1))
        for i in range(in_plane)
    ]
    mirrored = lax.ppermute(queries, "seq", swap)
    messages = pack(
        n,
        cap,
        phase_table,
        block_device[:, 0],
        span_keys.reshape(blocks, BLK, feature),
        span_values.reshape(blocks, BLK, feature),
    )
    packed = {p: messages[i * in_plane : (i + 1) * in_plane] for i, p in enumerate(names)}

    def send(phase):
        out = []
        for offset in range(in_plane):
            value = packed[phase][offset]
            pairs = route(n, phase, offset)
            if any(a != b for a, b in pairs):
                value = lax.ppermute(value, "seq", pairs)
            out.append(value)
        return out

    got = {phase: send(phase) for phase in names}

    def regroup(value):
        value = value.reshape(rows, steps, KVH, group, HD).transpose(0, 2, 1, 3, 4)
        return value.reshape(rows, KVH, steps * group, HD)

    mirrored = regroup(mirrored)

    notes = note(n, block_device[:, 0], block_row, cache_len)
    notes = lax.all_to_all(notes, "seq", split_axis=0, concat_axis=0, tiled=True)
    mine = lax.dynamic_index_in_dim(jnp.array(device_tables(n)), me, 0, keepdims=False)
    *slots, tally = index(n, cap, rows, notes, mine)
    reach = cache_keys.shape[1] // BLK + n * cap + 1
    tables = turn_tables(np.arange(2 * BLK)) + turn_tables(np.arange(reach) * BLK)
    scalars = (mine, *slots, tally, cache_len)

    partial, stats = span(
        "partial", 0, 0, cap, scalars, mirrored, tables,
        got["e"] + got["f"], (), (), steps,
    )
    queries, partial = lax.optimization_barrier((queries, partial))
    grouped = regroup(queries)
    state = resident(cache_len, grouped, step_keys, step_values, cache_keys, cache_values)
    partial = lax.ppermute(partial, "seq", swap)
    stats = lax.ppermute(stats, "seq", swap)
    state = span(
        "state", 1, 0, cap, scalars, grouped, tables,
        got["e"] + got["f"] + got["g"], tuple(state), (partial, stats), steps,
    )
    return span(
        "final", 2, 3 * in_plane, cap, scalars, grouped, tables,
        got["h"], tuple(state), (), steps,
    )


def solution(mesh):
    placed = (
        P(("groups", "seq"), None),
        P(("groups", "seq"), None),
        P(("groups", "seq"), None),
        P(("groups", "seq")),
        P(("groups", "seq")),
        P(("groups", "seq"), None, None),
        P(("groups", "seq"), None, None),
        P(("groups", "seq"), None, None),
        P(("groups", "seq"), None, None),
        P(("groups", "seq"), None, None),
    )

    return jax.shard_map(
        body,
        mesh=mesh,
        in_specs=placed,
        out_specs=P(("groups", "seq"), None, None),
        check_vma=False,
    )
```

```python
import functools

import jax
import jax.numpy as jnp
import numpy as np
from jax import lax
from jax.experimental import pallas as pl
from jax.experimental.pallas import tpu as pltpu
from jax.sharding import PartitionSpec as P


KVH = 4
QH = 64
HD = 128
BLK = 8
PLANES = 4
CHUNK = 256
SPAN = 128
LANES = 128
GRANT = 20 * 2**20
WIDE = 52 * 2**20
UNROLL = 4
PACKED = 4
NEG = -1e30


def frequencies(half_width):
    index = np.arange(half_width, dtype=np.float64)
    base = 1.0 / 500000.0 ** (index / half_width)
    wavelen = 2.0 * np.pi / base
    smooth = (8192.0 / wavelen - 1.0) / 3.0
    blended = (1.0 - smooth) * base / 8.0 + smooth * base
    scaled = np.where(wavelen > 8192.0, base / 8.0, blended)
    return np.where(wavelen < 2048.0, base, scaled)


def turn_tables(positions):
    freq = frequencies(HD // 2)
    angles = np.asarray(positions, np.float64)[:, None] * np.concatenate([freq, freq])[None]
    sign = np.where(np.arange(HD) < HD // 2, -1.0, 1.0)
    return jnp.array(np.cos(angles), jnp.float32), jnp.array(np.sin(angles) * sign, jnp.float32)


def pack_kernel(n, phase_table, target, keys, values, *refs):
    outs = refs[:n]
    slots, fill, rel, sems = refs[n:]
    blocks = keys.shape[0]
    in_plane = n // PLANES
    me = lax.axis_index("seq")
    plane, place = me // in_plane, me % in_plane

    def clear(p, _):
        for i in range(in_plane):
            fill[p * in_plane + i] = 0
            offset = i - place
            offset = jnp.where(offset < 0, offset + in_plane, offset)
            rel[p * in_plane + i] = phase_table[plane, p] * in_plane + offset
        return 0

    lax.fori_loop(0, PLANES, clear, 0)

    def put(step, _):
        ready = []
        for u in range(PACKED):
            b = step * PACKED + u
            dest = target[b]
            slot = fill[dest]
            fill[dest] = slot + 1
            ready.append((b, rel[dest], slot))
        for b, message, slot in ready:
            slots[message, 0, slot] = keys[b]
            slots[message, 1, slot] = values[b]
        return 0

    lax.fori_loop(0, blocks // PACKED, put, 0)
    copies = [pltpu.make_async_copy(slots.at[i], outs[i], sems.at[i]) for i in range(n)]
    for copy in copies:
        copy.start()
    for copy in copies:
        copy.wait()


def pack(n, cap, phase_table, target, keys, values):
    width = keys.shape[-1]
    message = jax.ShapeDtypeStruct((2, cap, BLK, width), jnp.bfloat16)
    smem = pl.BlockSpec(memory_space=pltpu.SMEM)
    vmem = pl.BlockSpec(memory_space=pltpu.VMEM)
    return pl.pallas_call(
        functools.partial(pack_kernel, n),
        out_shape=(message,) * n,
        in_specs=[smem] * 2 + [vmem] * 2,
        out_specs=(pl.BlockSpec(memory_space=pl.ANY),) * n,
        scratch_shapes=[
            pltpu.VMEM((n, 2, cap, BLK, width), jnp.bfloat16),
            pltpu.SMEM((n,), jnp.int32),
            pltpu.SMEM((n,), jnp.int32),
            pltpu.SemaphoreType.DMA((n,)),
        ],
        name="pack",
    )(phase_table, target, keys, values)


def twin_index(in_plane, index):
    plane = index // in_plane
    inner = (plane > 0) & (plane < PLANES - 1)
    return jnp.where(inner, (PLANES - 1 - 2 * plane) * in_plane + index, index)


def note_kernel(n, target, rows, lens, notes, fill, twins):
    in_plane = n // PLANES

    def clear(i, _):
        fill[i] = 0
        twins[i] = twin_index(in_plane, i)
        return 0

    lax.fori_loop(0, n, clear, 0, unroll=min(n, 16))
    my_twin = twins[lax.axis_index("seq")]
    for k in range(lens.shape[0]):
        notes[my_twin, 2 * LANES + k] = lens[k]

    def put(step, _):
        ready = []
        for u in range(PACKED):
            b = step * PACKED + u
            dest = target[b]
            slot = fill[dest]
            fill[dest] = slot + 1
            ready.append((dest, twins[dest], slot, rows[b]))
        for dest, twin, slot, row in ready:
            notes[dest, slot] = row
            notes[twin, LANES + slot] = row
        return 0

    lax.fori_loop(0, rows.shape[0] // PACKED, put, 0)

    def close(i, _):
        notes[i, LANES - 1] = fill[i]
        notes[twins[i], 2 * LANES - 1] = fill[i]
        return 0

    lax.fori_loop(0, n, close, 0, unroll=min(n, 4))


def note(n, target, rows, lens):
    smem = pl.BlockSpec(memory_space=pltpu.SMEM)
    return pl.pallas_call(
        functools.partial(note_kernel, n),
        out_shape=jax.ShapeDtypeStruct((n, 3 * LANES), jnp.int32),
        in_specs=[smem] * 3,
        out_specs=smem,
        scratch_shapes=[pltpu.SMEM((n,), jnp.int32), pltpu.SMEM((n,), jnp.int32)],
        name="note",
    )(target, rows, lens)


def index_kernel(n, cap, rows, notes, stages, place, row_of, rank_of, used, tally):
    f32 = jnp.float32

    def iotas(shape):
        return [lax.broadcasted_iota(jnp.int32, shape, d) for d in (0, 1)]

    a, b = iotas((cap, cap))
    before = (a < b).astype(f32)
    a, b = iotas((n, n))
    sooner = (b < a).astype(f32)
    lines = [jnp.broadcast_to(stages[i : i + 1, :n], (n, n)) for i in (2, 3)]
    posts = [
        jnp.sum(jnp.where(a == b, line, 0), axis=1, keepdims=True) for line in lines
    ]
    mates = [jnp.where(line == post, sooner, 0.0) for line, post in zip(lines, posts)]
    kernel, lane = iotas((8, LANES))
    counts = jnp.zeros((8, LANES), f32)
    for side in range(2):
        there = notes[:, side * LANES : (side + 1) * LANES]
        valid = lax.broadcasted_iota(jnp.int32, (n, cap), 1) < there[:, LANES - 1 :]
        rows_here = jnp.where(valid, there[:, :cap], -1)
        rank = jnp.zeros((n, cap), f32)
        local = jnp.zeros((n, cap), f32)
        for r in range(rows):
            hit = (rows_here == r).astype(f32)
            inside = jnp.dot(hit, before, preferred_element_type=f32)
            ahead = jnp.dot(sooner, hit, preferred_element_type=f32)
            near = jnp.dot(mates[side], hit, preferred_element_type=f32)
            rank += hit * (inside + jnp.sum(ahead, axis=1, keepdims=True))
            local += hit * (inside + jnp.sum(near, axis=1, keepdims=True))
            per_source = jnp.sum(hit, axis=1, keepdims=True)
            for stage in range(3):
                if (stage == 0) == (side == 1):
                    number = jnp.sum(
                        jnp.where(posts[side] == stage, per_source, 0.0), axis=0, keepdims=True
                    )
                    counts += jnp.where((kernel == stage) & (lane == r), number, 0.0)
        span = slice(side * n, side * n + n)
        place[span, :] = jnp.where(valid, local, -1.0).astype(jnp.int32)
        row_of[span, :] = jnp.maximum(rows_here, 0)
        rank_of[span, :] = rank.astype(jnp.int32)
        filled = jnp.sum(valid.astype(f32), axis=1, keepdims=True)
        used[span, :] = jnp.broadcast_to(filled, (n, cap)).astype(jnp.int32)
    a, b = iotas((LANES, LANES))
    begin = jnp.dot(counts, (a < b).astype(f32), preferred_element_type=f32)
    twin = twin_index(n // PLANES, lax.axis_index("seq"))
    source = lax.broadcasted_iota(jnp.int32, (n, LANES), 0)
    lens = jnp.sum(
        jnp.where(source == twin, notes[:, 2 * LANES :], 0), axis=0, keepdims=True
    )
    tally[0:8, :] = jnp.where(kernel == 3, lens, begin.astype(jnp.int32))
    tally[8:16, :] = (counts * BLK).astype(jnp.int32)


def index(n, cap, rows, notes, stages):
    vmem = pl.BlockSpec(memory_space=pltpu.VMEM)
    slots = jax.ShapeDtypeStruct((2 * n, cap), jnp.int32)
    return pl.pallas_call(
        functools.partial(index_kernel, n, cap, rows),
        out_shape=(slots,) * 4 + (jax.ShapeDtypeStruct((16, LANES), jnp.int32),),
        in_specs=[vmem] * 2,
        out_specs=(vmem,) * 5,
        compiler_params=pltpu.CompilerParams(vmem_limit_bytes=GRANT),
        name="index",
    )(notes, stages)


def as_wide(line, width):
    if width % HD == 0:
        return jnp.concatenate([line] * (width // HD), axis=1)
    return line[:, :width]


def blend(queries, pieces, old, guard=False):
    scale = HD ** (-0.5)
    heads = range(KVH)
    scores = [
        [
            jnp.where(
                piece[2],
                lax.dot_general(
                    queries[head],
                    piece[0][head],
                    (((1,), (1,)), ((), ())),
                    preferred_element_type=jnp.float32,
                )
                * scale,
                NEG,
            )
            for piece in pieces
        ]
        for head in heads
    ]
    new = []
    for head in heads:
        peak = functools.reduce(
            jnp.maximum, [jnp.max(one, axis=-1, keepdims=True) for one in scores[head]]
        )
        if old is None:
            new_top = jnp.broadcast_to(peak, (peak.shape[0], HD))
        else:
            old_acc, old_top, old_total = old[head]
            new_top = jnp.maximum(old_top, peak)
        raw = [jnp.exp(one - as_wide(new_top, one.shape[1])) for one in scores[head]]
        if guard:
            raw = [jnp.where(piece[2], one, 0.0) for piece, one in zip(pieces, raw)]
        added = sum(jnp.sum(one, axis=-1, keepdims=True) for one in raw)
        mixed = sum(
            jnp.dot(one.astype(jnp.bfloat16), piece[1][head], preferred_element_type=jnp.float32)
            for one, piece in zip(raw, pieces)
        )
        if old is None:
            new.append((mixed, new_top, jnp.broadcast_to(added, new_top.shape)))
        else:
            factor = jnp.exp(old_top - new_top)
            new.append((old_acc * factor + mixed, new_top, old_total * factor + added))
    return new


def held(row, state):
    return [tuple(one[row, head] for one in state) for head in range(KVH)]


def hold(row, state, new):
    for head in range(KVH):
        for one, value in zip(state, new[head]):
            one[row, head] = value


def row_queries(row, q_ref):
    return [q_ref[row, head] for head in range(KVH)]


def resident_kernel(
    lens, q_ref, step_k, step_v, keys, values, acc, top, total, kbuf, vbuf, sems
):
    rows, slot_count = kbuf.shape[0], kbuf.shape[1]
    piece = min(CHUNK, slot_count)
    pieces = slot_count // piece
    steps = step_k.shape[1]
    width = q_ref.shape[2]
    group = width // steps

    def copies(r, i):
        part = pl.ds(i * piece, piece)
        return (
            pltpu.make_async_copy(keys.at[r, part], kbuf.at[r, part], sems.at[0, r, i]),
            pltpu.make_async_copy(values.at[r, part], vbuf.at[r, part], sems.at[1, r, i]),
        )

    def fetch(r, _):
        for i in range(pieces):

            @pl.when((i == 0) | (i * piece < lens[r]))
            def _():
                for copy in copies(r, i):
                    copy.start()

        return 0

    lax.fori_loop(0, rows, fetch, 0)
    lane = lax.broadcasted_iota(jnp.int32, (width, piece), 1)
    causal = (
        lax.broadcasted_iota(jnp.int32, (width, steps), 1)
        <= lax.broadcasted_iota(jnp.int32, (width, steps), 0) // group
    )

    def one_row(r, _):
        def part(i):
            span = pl.ds(i * piece, piece)
            return (
                [kbuf[r, span, head * HD : (head + 1) * HD] for head in range(KVH)],
                [vbuf[r, span, head * HD : (head + 1) * HD] for head in range(KVH)],
                lane + i * piece < lens[r],
            )

        own = (
            [step_k[r, :, head * HD : (head + 1) * HD] for head in range(KVH)],
            [step_v[r, :, head * HD : (head + 1) * HD] for head in range(KVH)],
            causal,
        )
        state = (acc, top, total)
        for copy in copies(r, 0):
            copy.wait()
        hold(r, state, blend(row_queries(r, q_ref), [own, part(0)], None))
        for i in range(1, pieces):

            @pl.when(i * piece < lens[r])
            def _():
                for copy in copies(r, i):
                    copy.wait()
                hold(r, state, blend(row_queries(r, q_ref), [part(i)], held(r, state)))

        return 0

    lax.fori_loop(0, rows, one_row, 0)


def state_shapes(rows, width):
    shape = jax.ShapeDtypeStruct((rows, KVH, width, HD), jnp.float32)
    return (shape,) * 3


def resident(lens, grouped, step_k, step_v, keys, values):
    rows, slot_count, feature = keys.shape
    pieces = slot_count // min(CHUNK, slot_count)
    vmem = pl.BlockSpec(memory_space=pltpu.VMEM)
    hbm = pl.BlockSpec(memory_space=pltpu.HBM)
    return pl.pallas_call(
        resident_kernel,
        out_shape=state_shapes(rows, grouped.shape[2]),
        in_specs=[pl.BlockSpec(memory_space=pltpu.SMEM), vmem, vmem, vmem, hbm, hbm],
        out_specs=(vmem,) * 3,
        scratch_shapes=[
            pltpu.VMEM((rows, slot_count, feature), jnp.bfloat16),
            pltpu.VMEM((rows, slot_count, feature), jnp.bfloat16),
            pltpu.SemaphoreType.DMA((2, rows, pieces)),
        ],
        compiler_params=pltpu.CompilerParams(vmem_limit_bytes=WIDE),
        cost_estimate=pl.CostEstimate(
            flops=2 * 10**9, bytes_accessed=16 * 2**20, transcendentals=10**6
        ),
        name="resident",
    )(lens, grouped, step_k, step_v, keys, values)


def span_kernel(
    kind, kernel, first, count, cap, mine, place_of, row_of, rank_of, used, tally, lens,
    q_ref, ca, sa, cb, sb, *refs,
):
    messages = refs[:count]
    refs = refs[count:]
    before = refs[:3]
    if kind == "partial":
        out, stats, acc, top, total, kbuf, vbuf = refs
    elif kind == "state":
        part, stats, acc, top, total, kbuf, vbuf = refs[3:]
    else:
        out, acc, top, total, scr, kbuf, vbuf = refs[3:]
    state = (acc, top, total)
    rows = q_ref.shape[0]
    width = q_ref.shape[2]
    feature = kbuf.shape[1]
    last = tally[kernel, rows - 1] * BLK + tally[8 + kernel, rows - 1]
    tail = pl.ds(pl.multiple_of(last, BLK), SPAN)
    vbuf[tail, :] = jnp.zeros((SPAN, feature), jnp.float32)
    unroll = min(UNROLL, cap)
    trash = count * cap + SPAN // BLK
    for j in range(count):

        @pl.when(mine[1, first + j] == kernel)
        def _():
            source = mine[0, first + j]
            message = messages[j]

            def place(step, _):
                ready = []
                for u in range(unroll):
                    k = step * unroll + u
                    r = row_of[source, k]
                    rank = rank_of[source, k]
                    local = place_of[source, k]
                    slot = jnp.where(local < 0, trash, tally[kernel, r] + local)
                    length = tally[3, r] if kind == "partial" else lens[r]
                    fine, coarse = pl.ds(length % BLK, BLK), pl.ds(length // BLK + rank, 1)
                    c_a, s_a = ca[fine, :], sa[fine, :]
                    c_b, s_b = cb[coarse, :], sb[coarse, :]
                    cosine = c_a * c_b - s_a * s_b
                    sine = s_a * c_b + c_a * s_b
                    where = pl.ds(pl.multiple_of(slot * BLK, BLK), BLK)
                    value = message[1, k].astype(jnp.float32)
                    key = message[0, k].astype(jnp.float32)
                    turned = []
                    for head in range(KVH):
                        piece = key[:, head * HD : (head + 1) * HD]
                        turned.append(piece * cosine + pltpu.roll(piece, HD // 2, 1) * sine)
                    ready.append((where, turned, value))
                for where, turned, value in ready:
                    vbuf[where, :] = value
                    for head in range(KVH):
                        kbuf[where, head * HD : (head + 1) * HD] = turned[head]
                return 0

            lax.fori_loop(0, (used[source, 0] + unroll - 1) // unroll, place, 0)

    lane = lax.broadcasted_iota(jnp.int32, (width, SPAN), 1)
    eye = lax.broadcasted_iota(jnp.int32, (width, width), 0) == lax.broadcasted_iota(
        jnp.int32, (width, width), 1
    )

    def block(r, i):
        where = pl.ds(pl.multiple_of(tally[kernel, r] * BLK + i * SPAN, BLK), SPAN)
        return (
            [kbuf[where, h * HD : (h + 1) * HD].astype(jnp.bfloat16) for h in range(KVH)],
            [vbuf[where, h * HD : (h + 1) * HD].astype(jnp.bfloat16) for h in range(KVH)],
            lane + i * SPAN < tally[8 + kernel, r],
        )

    def beyond(r):
        def piece(i, _):
            hold(r, state, blend(row_queries(r, q_ref), [block(r, i)], held(r, state)))
            return 0

        lax.fori_loop(1, (tally[8 + kernel, r] + SPAN - 1) // SPAN, piece, 0)

    def partial_rows(pair):
        new = [blend(row_queries(r, q_ref), [block(r, 0)], None, guard=True) for r in pair]
        for r, one in zip(pair, new):
            hold(r, state, one)
        for r in pair:
            beyond(r)
        done = []
        for r in pair:
            for head in range(KVH):
                amount = total[r, head]
                safe = jnp.where(amount > 0.0, amount, 1.0)
                lines = [
                    jnp.sum(jnp.where(eye, one[:, :width], 0.0), axis=0, keepdims=True)
                    for one in (top[r, head], amount)
                ]
                done.append((r, head, (acc[r, head] / safe).astype(jnp.bfloat16), lines))
        for r, head, value, lines in done:
            out[r, head] = value
            for i in range(2):
                stats[r, head, pl.ds(i, 1), :] = lines[i]

    def with_part(r, new):
        merged = []
        for head in range(KVH):
            lines = []
            for i in range(2):
                line = jnp.broadcast_to(stats[r, head, pl.ds(i, 1), :], (width, width))
                lines.append(jnp.sum(jnp.where(eye, line, 0.0), axis=1, keepdims=True))
            other_top, other_total = lines
            other_top = jnp.where(other_total > 0.0, other_top, NEG)
            value, old_top, amount = new[head]
            new_top = jnp.maximum(old_top, other_top)
            mine = jnp.exp(old_top - new_top)
            theirs = jnp.exp(other_top - new_top) * other_total
            merged.append(
                (
                    value * mine + part[r, head].astype(jnp.float32) * theirs,
                    new_top,
                    amount * mine + theirs,
                )
            )
        return merged

    def state_rows(pair):
        new = [blend(row_queries(r, q_ref), [block(r, 0)], held(r, before)) for r in pair]
        new = [with_part(r, one) for r, one in zip(pair, new)]
        for r, one in zip(pair, new):
            hold(r, state, one)
        for r in pair:
            beyond(r)

    def put_out(pair, new):
        done = [value / amount for one in new for value, _, amount in one]
        for i, value in enumerate(done):
            scr[i] = value
        steps = out.shape[1]
        group = width // steps
        for i, r in enumerate(pair):
            for head in range(KVH):
                for g in range(group):
                    column = (head * group + g) * HD
                    out[r, :, column : column + HD] = scr[
                        i * KVH + head, pl.ds(g, steps, stride=group), :
                    ].astype(jnp.bfloat16)

    def final_rows(pair):
        new = [blend(row_queries(r, q_ref), [block(r, 0)], held(r, before)) for r in pair]
        put_out(pair, new)
        longest = functools.reduce(jnp.maximum, [tally[8 + kernel, r] for r in pair])

        @pl.when(longest > SPAN)
        def _():
            for r, one in zip(pair, new):
                hold(r, state, one)
            for r in pair:
                beyond(r)
            put_out(pair, [held(r, state) for r in pair])

    run = {"partial": partial_rows, "state": state_rows, "final": final_rows}[kind]
    together = 2 if rows % 2 == 0 else 1

    def some_rows(i, _):
        run([i * together + u for u in range(together)])
        return 0

    lax.fori_loop(0, rows // together, some_rows, 0)


def span(kind, kernel, first, cap, scalars, grouped, tables, messages, state, extra, steps):
    rows, _, width, _ = grouped.shape
    feature = messages[0].shape[-1]
    count = len(messages)
    room = (count * cap + 1) * BLK + SPAN
    smem = pl.BlockSpec(memory_space=pltpu.SMEM)
    vmem = pl.BlockSpec(memory_space=pltpu.VMEM)
    running = [pltpu.VMEM((rows, KVH, width, HD), jnp.float32)] * 3
    scratch = []
    if kind == "partial":
        out_shape = (
            jax.ShapeDtypeStruct((rows, KVH, width, HD), jnp.bfloat16),
            jax.ShapeDtypeStruct((rows, KVH, 2, width), jnp.float32),
        )
        scratch += running
    elif kind == "state":
        out_shape = state_shapes(rows, width)
    else:
        out_shape = jax.ShapeDtypeStruct((rows, steps, QH * HD), jnp.bfloat16)
        scratch += running + [pltpu.VMEM((2 * KVH, width, HD), jnp.float32)]
    scratch += [pltpu.VMEM((room, feature), jnp.float32)] * 2
    return pl.pallas_call(
        functools.partial(span_kernel, kind, kernel, first, count, cap),
        out_shape=out_shape,
        in_specs=[smem] * 7 + [vmem] * (5 + count + len(state) + len(extra)),
        out_specs=jax.tree.map(lambda _: vmem, out_shape),
        scratch_shapes=scratch,
        compiler_params=pltpu.CompilerParams(vmem_limit_bytes=GRANT),
        cost_estimate=pl.CostEstimate(
            flops=10**9, bytes_accessed=12 * 2**20, transcendentals=10**6
        ),
    )(*scalars, grouped, *tables, *messages, *state, *extra)


PHASES = {"e": (2, 1, 1, 2), "f": (0, 3, 3, 0), "g": (3, 0, 0, 3), "h": (1, 2, 2, 1)}


def site_plane(plane, flip):
    dest = plane ^ flip
    half = PLANES // 2
    if (plane < half) != (dest < half) and dest in (half - 1, half):
        return PLANES - 1 - dest
    return dest


def came_from(phase, plane):
    flips = PHASES[phase]
    return next(s for s in range(PLANES) if site_plane(s, flips[s]) == plane)


def for_mirror(phase, plane):
    source = came_from(phase, plane)
    return int(source ^ PHASES[phase][source] != plane)


def route(n, phase, offset):
    in_plane = n // PLANES
    return [
        (
            plane * in_plane + place,
            site_plane(plane, flip) * in_plane + (place + offset) % in_plane,
        )
        for plane, flip in enumerate(PHASES[phase])
        for place in range(in_plane)
    ]


STAGE = {"e": 1, "f": 1, "g": 1, "h": 2}


def device_tables(n):
    in_plane = n // PLANES
    lines = []
    for me in range(n):
        plane, place = me // in_plane, me % in_plane
        entry, stage = [], []
        post = [[-1] * n, [-1] * n]
        for phase in PHASES:
            mirror = for_mirror(phase, plane)
            for offset in range(in_plane):
                source = came_from(phase, plane) * in_plane + (place - offset) % in_plane
                entry.append(mirror * n + source)
                stage.append(0 if mirror else STAGE[phase])
                post[mirror][source] = stage[-1]
        lines.append((entry, stage, post[0], post[1]))
    return np.array(lines, np.int32)


def body(
    span_keys,
    span_values,
    block_device,
    block_row,
    cache_len,
    cache_keys,
    cache_values,
    queries,
    step_keys,
    step_values,
):
    n = lax.axis_size("seq")
    in_plane = n // PLANES
    me = lax.axis_index("seq").astype(jnp.int32)
    rows = cache_len.shape[0]
    feature = span_keys.shape[1]
    blocks = span_keys.shape[0] // BLK
    cap = max(2, (2 * blocks + n - 1) // n)
    steps = queries.shape[1]
    group = QH // KVH
    names = list(PHASES)

    phase_table = jnp.array(
        [
            [next(i for i, p in enumerate(names) if PHASES[p][z] == z ^ d) for d in range(PLANES)]
            for z in range(PLANES)
        ],
        jnp.int32,
    )
    half = PLANES // 2
    swap = [
        (a * in_plane + i, b * in_plane + i)
        for a, b in ((half - 1, half), (half, half - 1))
        for i in range(in_plane)
    ]
    mirrored = lax.ppermute(queries, "seq", swap)
    messages = pack(
        n,
        cap,
        phase_table,
        block_device[:, 0],
        span_keys.reshape(blocks, BLK, feature),
        span_values.reshape(blocks, BLK, feature),
    )
    packed = {p: messages[i * in_plane : (i + 1) * in_plane] for i, p in enumerate(names)}

    def send(phase):
        out = []
        for offset in range(in_plane):
            value = packed[phase][offset]
            pairs = route(n, phase, offset)
            if any(a != b for a, b in pairs):
                value = lax.ppermute(value, "seq", pairs)
            out.append(value)
        return out

    got = {phase: send(phase) for phase in names}

    def regroup(value):
        value = value.reshape(rows, steps, KVH, group, HD).transpose(0, 2, 1, 3, 4)
        return value.reshape(rows, KVH, steps * group, HD)

    queries, mirrored = lax.optimization_barrier((queries, mirrored))
    grouped, mirrored = regroup(queries), regroup(mirrored)
    state = resident(cache_len, grouped, step_keys, step_values, cache_keys, cache_values)

    notes = note(n, block_device[:, 0], block_row, cache_len)
    notes = lax.all_to_all(notes, "seq", split_axis=0, concat_axis=0, tiled=True)
    mine = lax.dynamic_index_in_dim(jnp.array(device_tables(n)), me, 0, keepdims=False)
    *slots, tally = index(n, cap, rows, notes, mine)
    reach = cache_keys.shape[1] // BLK + n * cap + 1
    tables = turn_tables(np.arange(2 * BLK)) + turn_tables(np.arange(reach) * BLK)
    scalars = (mine, *slots, tally, cache_len)

    partial, stats = span(
        "partial", 0, 0, cap, scalars, mirrored, tables,
        got["e"] + got["f"], (), (), steps,
    )
    partial = lax.ppermute(partial, "seq", swap)
    stats = lax.ppermute(stats, "seq", swap)
    state = span(
        "state", 1, 0, cap, scalars, grouped, tables,
        got["e"] + got["f"] + got["g"], tuple(state), (partial, stats), steps,
    )
    return span(
        "final", 2, 3 * in_plane, cap, scalars, grouped, tables,
        got["h"], tuple(state), (), steps,
    )


def solution(mesh):
    placed = (
        P(("groups", "seq"), None),
        P(("groups", "seq"), None),
        P(("groups", "seq"), None),
        P(("groups", "seq")),
        P(("groups", "seq")),
        P(("groups", "seq"), None, None),
        P(("groups", "seq"), None, None),
        P(("groups", "seq"), None, None),
        P(("groups", "seq"), None, None),
        P(("groups", "seq"), None, None),
    )

    return jax.shard_map(
        body,
        mesh=mesh,
        in_specs=placed,
        out_specs=P(("groups", "seq"), None, None),
        check_vma=False,
    )
```

```python
import functools

import jax
import jax.numpy as jnp
import numpy as np
from jax import lax
from jax.experimental import pallas as pl
from jax.experimental.pallas import tpu as pltpu
from jax.sharding import PartitionSpec as P


KVH = 4
QH = 64
HD = 128
BLK = 8
PLANES = 4
CHUNK = 256
SPAN = 128
LANES = 128
GRANT = 20 * 2**20
WIDE = 52 * 2**20
UNROLL = 4
PACKED = 4
NEG = -1e30


def frequencies(half_width):
    index = np.arange(half_width, dtype=np.float64)
    base = 1.0 / 500000.0 ** (index / half_width)
    wavelen = 2.0 * np.pi / base
    smooth = (8192.0 / wavelen - 1.0) / 3.0
    blended = (1.0 - smooth) * base / 8.0 + smooth * base
    scaled = np.where(wavelen > 8192.0, base / 8.0, blended)
    return np.where(wavelen < 2048.0, base, scaled)


def turn_tables(positions):
    freq = frequencies(HD // 2)
    angles = np.asarray(positions, np.float64)[:, None] * np.concatenate([freq, freq])[None]
    sign = np.where(np.arange(HD) < HD // 2, -1.0, 1.0)
    return jnp.array(np.cos(angles), jnp.float32), jnp.array(np.sin(angles) * sign, jnp.float32)


def pack_kernel(n, phase_table, target, keys, values, *refs):
    outs = refs[:n]
    slots, fill, rel, sems = refs[n:]
    blocks = keys.shape[0]
    in_plane = n // PLANES
    me = lax.axis_index("seq")
    plane, place = me // in_plane, me % in_plane

    def clear(p, _):
        for i in range(in_plane):
            fill[p * in_plane + i] = 0
            offset = i - place
            offset = jnp.where(offset < 0, offset + in_plane, offset)
            rel[p * in_plane + i] = phase_table[plane, p] * in_plane + offset
        return 0

    lax.fori_loop(0, PLANES, clear, 0)

    def put(step, _):
        ready = []
        for u in range(PACKED):
            b = step * PACKED + u
            dest = target[b]
            slot = fill[dest]
            fill[dest] = slot + 1
            ready.append((b, rel[dest], slot))
        for b, message, slot in ready:
            slots[message, 0, slot] = keys[b]
            slots[message, 1, slot] = values[b]
        return 0

    lax.fori_loop(0, blocks // PACKED, put, 0)
    copies = [pltpu.make_async_copy(slots.at[i], outs[i], sems.at[i]) for i in range(n)]
    for copy in copies:
        copy.start()
    for copy in copies:
        copy.wait()


def pack(n, cap, phase_table, target, keys, values):
    width = keys.shape[-1]
    message = jax.ShapeDtypeStruct((2, cap, BLK, width), jnp.bfloat16)
    smem = pl.BlockSpec(memory_space=pltpu.SMEM)
    vmem = pl.BlockSpec(memory_space=pltpu.VMEM)
    return pl.pallas_call(
        functools.partial(pack_kernel, n),
        out_shape=(message,) * n,
        in_specs=[smem] * 2 + [vmem] * 2,
        out_specs=(pl.BlockSpec(memory_space=pl.ANY),) * n,
        scratch_shapes=[
            pltpu.VMEM((n, 2, cap, BLK, width), jnp.bfloat16),
            pltpu.SMEM((n,), jnp.int32),
            pltpu.SMEM((n,), jnp.int32),
            pltpu.SemaphoreType.DMA((n,)),
        ],
        name="pack",
    )(phase_table, target, keys, values)


def twin_index(in_plane, index):
    plane = index // in_plane
    inner = (plane > 0) & (plane < PLANES - 1)
    return jnp.where(inner, (PLANES - 1 - 2 * plane) * in_plane + index, index)


def note_kernel(n, target, rows, lens, notes, fill, twins):
    in_plane = n // PLANES

    def clear(i, _):
        fill[i] = 0
        twins[i] = twin_index(in_plane, i)
        return 0

    lax.fori_loop(0, n, clear, 0, unroll=min(n, 16))
    my_twin = twins[lax.axis_index("seq")]
    for k in range(lens.shape[0]):
        notes[my_twin, 2 * LANES + k] = lens[k]

    def put(step, _):
        ready = []
        for u in range(PACKED):
            b = step * PACKED + u
            dest = target[b]
            slot = fill[dest]
            fill[dest] = slot + 1
            ready.append((dest, twins[dest], slot, rows[b]))
        for dest, twin, slot, row in ready:
            notes[dest, slot] = row
            notes[twin, LANES + slot] = row
        return 0

    lax.fori_loop(0, rows.shape[0] // PACKED, put, 0)

    def close(i, _):
        notes[i, LANES - 1] = fill[i]
        notes[twins[i], 2 * LANES - 1] = fill[i]
        return 0

    lax.fori_loop(0, n, close, 0, unroll=min(n, 4))


def note(n, target, rows, lens):
    smem = pl.BlockSpec(memory_space=pltpu.SMEM)
    return pl.pallas_call(
        functools.partial(note_kernel, n),
        out_shape=jax.ShapeDtypeStruct((n, 3 * LANES), jnp.int32),
        in_specs=[smem] * 3,
        out_specs=smem,
        scratch_shapes=[pltpu.SMEM((n,), jnp.int32), pltpu.SMEM((n,), jnp.int32)],
        name="note",
    )(target, rows, lens)


def index_kernel(n, cap, rows, notes, stages, place, row_of, rank_of, used, tally):
    f32 = jnp.float32

    def iotas(shape):
        return [lax.broadcasted_iota(jnp.int32, shape, d) for d in (0, 1)]

    a, b = iotas((cap, cap))
    before = (a < b).astype(f32)
    a, b = iotas((n, n))
    sooner = (b < a).astype(f32)
    lines = [jnp.broadcast_to(stages[i : i + 1, :n], (n, n)) for i in (2, 3)]
    posts = [
        jnp.sum(jnp.where(a == b, line, 0), axis=1, keepdims=True) for line in lines
    ]
    mates = [jnp.where(line == post, sooner, 0.0) for line, post in zip(lines, posts)]
    kernel, lane = iotas((8, LANES))
    counts = jnp.zeros((8, LANES), f32)
    for side in range(2):
        there = notes[:, side * LANES : (side + 1) * LANES]
        valid = lax.broadcasted_iota(jnp.int32, (n, cap), 1) < there[:, LANES - 1 :]
        rows_here = jnp.where(valid, there[:, :cap], -1)
        rank = jnp.zeros((n, cap), f32)
        local = jnp.zeros((n, cap), f32)
        for r in range(rows):
            hit = (rows_here == r).astype(f32)
            inside = jnp.dot(hit, before, preferred_element_type=f32)
            ahead = jnp.dot(sooner, hit, preferred_element_type=f32)
            near = jnp.dot(mates[side], hit, preferred_element_type=f32)
            rank += hit * (inside + jnp.sum(ahead, axis=1, keepdims=True))
            local += hit * (inside + jnp.sum(near, axis=1, keepdims=True))
            per_source = jnp.sum(hit, axis=1, keepdims=True)
            for stage in range(3):
                if (stage == 0) == (side == 1):
                    number = jnp.sum(
                        jnp.where(posts[side] == stage, per_source, 0.0), axis=0, keepdims=True
                    )
                    counts += jnp.where((kernel == stage) & (lane == r), number, 0.0)
        span = slice(side * n, side * n + n)
        place[span, :] = jnp.where(valid, local, -1.0).astype(jnp.int32)
        row_of[span, :] = jnp.maximum(rows_here, 0)
        rank_of[span, :] = rank.astype(jnp.int32)
        filled = jnp.sum(valid.astype(f32), axis=1, keepdims=True)
        used[span, :] = jnp.broadcast_to(filled, (n, cap)).astype(jnp.int32)
    a, b = iotas((LANES, LANES))
    begin = jnp.dot(counts, (a < b).astype(f32), preferred_element_type=f32)
    twin = twin_index(n // PLANES, lax.axis_index("seq"))
    source = lax.broadcasted_iota(jnp.int32, (n, LANES), 0)
    lens = jnp.sum(
        jnp.where(source == twin, notes[:, 2 * LANES :], 0), axis=0, keepdims=True
    )
    tally[0:8, :] = jnp.where(kernel == 3, lens, begin.astype(jnp.int32))
    tally[8:16, :] = (counts * BLK).astype(jnp.int32)


def index(n, cap, rows, notes, stages):
    vmem = pl.BlockSpec(memory_space=pltpu.VMEM)
    slots = jax.ShapeDtypeStruct((2 * n, cap), jnp.int32)
    return pl.pallas_call(
        functools.partial(index_kernel, n, cap, rows),
        out_shape=(slots,) * 4 + (jax.ShapeDtypeStruct((16, LANES), jnp.int32),),
        in_specs=[vmem] * 2,
        out_specs=(vmem,) * 5,
        compiler_params=pltpu.CompilerParams(vmem_limit_bytes=GRANT),
        name="index",
    )(notes, stages)


def as_wide(line, width):
    if width % HD == 0:
        return jnp.concatenate([line] * (width // HD), axis=1)
    return line[:, :width]


def blend(queries, pieces, old, guard=False):
    scale = HD ** (-0.5)
    heads = range(KVH)
    scores = [
        [
            jnp.where(
                piece[2],
                lax.dot_general(
                    queries[head],
                    piece[0][head],
                    (((1,), (1,)), ((), ())),
                    preferred_element_type=jnp.float32,
                )
                * scale,
                NEG,
            )
            for piece in pieces
        ]
        for head in heads
    ]
    new = []
    for head in heads:
        peak = functools.reduce(
            jnp.maximum, [jnp.max(one, axis=-1, keepdims=True) for one in scores[head]]
        )
        if old is None:
            new_top = jnp.broadcast_to(peak, (peak.shape[0], HD))
        else:
            old_acc, old_top, old_total = old[head]
            new_top = jnp.maximum(old_top, peak)
        raw = [jnp.exp(one - as_wide(new_top, one.shape[1])) for one in scores[head]]
        if guard:
            raw = [jnp.where(piece[2], one, 0.0) for piece, one in zip(pieces, raw)]
        added = sum(jnp.sum(one, axis=-1, keepdims=True) for one in raw)
        mixed = sum(
            jnp.dot(one.astype(jnp.bfloat16), piece[1][head], preferred_element_type=jnp.float32)
            for one, piece in zip(raw, pieces)
        )
        if old is None:
            new.append((mixed, new_top, jnp.broadcast_to(added, new_top.shape)))
        else:
            factor = jnp.exp(old_top - new_top)
            new.append((old_acc * factor + mixed, new_top, old_total * factor + added))
    return new


def held(row, state):
    return [tuple(one[row, head] for one in state) for head in range(KVH)]


def hold(row, state, new):
    for head in range(KVH):
        for one, value in zip(state, new[head]):
            one[row, head] = value


def row_queries(row, q_ref):
    return [q_ref[row, head] for head in range(KVH)]


def resident_kernel(
    lens, q_ref, step_k, step_v, keys, values, acc, top, total, kbuf, vbuf, sems
):
    rows, slot_count = kbuf.shape[0], kbuf.shape[1]
    piece = min(CHUNK, slot_count)
    pieces = slot_count // piece
    steps = step_k.shape[1]
    width = q_ref.shape[2]
    group = width // steps

    def copies(r, i):
        part = pl.ds(i * piece, piece)
        return (
            pltpu.make_async_copy(keys.at[r, part], kbuf.at[r, part], sems.at[0, r, i]),
            pltpu.make_async_copy(values.at[r, part], vbuf.at[r, part], sems.at[1, r, i]),
        )

    def fetch(r, _):
        for i in range(pieces):

            @pl.when((i == 0) | (i * piece < lens[r]))
            def _():
                for copy in copies(r, i):
                    copy.start()

        return 0

    lax.fori_loop(0, rows, fetch, 0)
    lane = lax.broadcasted_iota(jnp.int32, (width, piece), 1)
    causal = (
        lax.broadcasted_iota(jnp.int32, (width, steps), 1)
        <= lax.broadcasted_iota(jnp.int32, (width, steps), 0) // group
    )

    def one_row(r, _):
        def part(i):
            span = pl.ds(i * piece, piece)
            return (
                [kbuf[r, span, head * HD : (head + 1) * HD] for head in range(KVH)],
                [vbuf[r, span, head * HD : (head + 1) * HD] for head in range(KVH)],
                lane + i * piece < lens[r],
            )

        own = (
            [step_k[r, :, head * HD : (head + 1) * HD] for head in range(KVH)],
            [step_v[r, :, head * HD : (head + 1) * HD] for head in range(KVH)],
            causal,
        )
        state = (acc, top, total)
        for copy in copies(r, 0):
            copy.wait()
        hold(r, state, blend(row_queries(r, q_ref), [own, part(0)], None))
        for i in range(1, pieces):

            @pl.when(i * piece < lens[r])
            def _():
                for copy in copies(r, i):
                    copy.wait()
                hold(r, state, blend(row_queries(r, q_ref), [part(i)], held(r, state)))

        return 0

    lax.fori_loop(0, rows, one_row, 0)


def state_shapes(rows, width):
    shape = jax.ShapeDtypeStruct((rows, KVH, width, HD), jnp.float32)
    return (shape,) * 3


def resident(lens, grouped, step_k, step_v, keys, values):
    rows, slot_count, feature = keys.shape
    pieces = slot_count // min(CHUNK, slot_count)
    vmem = pl.BlockSpec(memory_space=pltpu.VMEM)
    hbm = pl.BlockSpec(memory_space=pltpu.HBM)
    return pl.pallas_call(
        resident_kernel,
        out_shape=state_shapes(rows, grouped.shape[2]),
        in_specs=[pl.BlockSpec(memory_space=pltpu.SMEM), vmem, vmem, vmem, hbm, hbm],
        out_specs=(vmem,) * 3,
        scratch_shapes=[
            pltpu.VMEM((rows, slot_count, feature), jnp.bfloat16),
            pltpu.VMEM((rows, slot_count, feature), jnp.bfloat16),
            pltpu.SemaphoreType.DMA((2, rows, pieces)),
        ],
        compiler_params=pltpu.CompilerParams(vmem_limit_bytes=WIDE),
        cost_estimate=pl.CostEstimate(
            flops=2 * 10**9, bytes_accessed=16 * 2**20, transcendentals=10**6
        ),
        name="resident",
    )(lens, grouped, step_k, step_v, keys, values)


def span_kernel(
    kind, kernel, first, count, cap, mine, place_of, row_of, rank_of, used, tally, lens,
    q_ref, ca, sa, cb, sb, *refs,
):
    messages = refs[:count]
    refs = refs[count:]
    before = refs[:3]
    if kind == "partial":
        out, stats, acc, top, total, kbuf, vbuf = refs
    elif kind == "state":
        acc, top, total, kbuf, vbuf = refs[3:]
    else:
        part, stats, out, acc, top, total, scr, kbuf, vbuf = refs[3:]
    state = (acc, top, total)
    rows = q_ref.shape[0]
    width = q_ref.shape[2]
    feature = kbuf.shape[1]
    last = tally[kernel, rows - 1] * BLK + tally[8 + kernel, rows - 1]
    tail = pl.ds(pl.multiple_of(last, BLK), SPAN)
    vbuf[tail, :] = jnp.zeros((SPAN, feature), jnp.float32)
    unroll = min(UNROLL, cap)
    trash = count * cap + SPAN // BLK
    for j in range(count):

        @pl.when(mine[1, first + j] == kernel)
        def _():
            source = mine[0, first + j]
            message = messages[j]

            def place(step, _):
                ready = []
                for u in range(unroll):
                    k = step * unroll + u
                    r = row_of[source, k]
                    rank = rank_of[source, k]
                    local = place_of[source, k]
                    slot = jnp.where(local < 0, trash, tally[kernel, r] + local)
                    length = tally[3, r] if kind == "partial" else lens[r]
                    fine, coarse = pl.ds(length % BLK, BLK), pl.ds(length // BLK + rank, 1)
                    c_a, s_a = ca[fine, :], sa[fine, :]
                    c_b, s_b = cb[coarse, :], sb[coarse, :]
                    cosine = c_a * c_b - s_a * s_b
                    sine = s_a * c_b + c_a * s_b
                    where = pl.ds(pl.multiple_of(slot * BLK, BLK), BLK)
                    value = message[1, k].astype(jnp.float32)
                    key = message[0, k].astype(jnp.float32)
                    turned = []
                    for head in range(KVH):
                        piece = key[:, head * HD : (head + 1) * HD]
                        turned.append(piece * cosine + pltpu.roll(piece, HD // 2, 1) * sine)
                    ready.append((where, turned, value))
                for where, turned, value in ready:
                    vbuf[where, :] = value
                    for head in range(KVH):
                        kbuf[where, head * HD : (head + 1) * HD] = turned[head]
                return 0

            lax.fori_loop(0, (used[source, 0] + unroll - 1) // unroll, place, 0)

    lane = lax.broadcasted_iota(jnp.int32, (width, SPAN), 1)
    eye = lax.broadcasted_iota(jnp.int32, (width, width), 0) == lax.broadcasted_iota(
        jnp.int32, (width, width), 1
    )

    def block(r, i):
        where = pl.ds(pl.multiple_of(tally[kernel, r] * BLK + i * SPAN, BLK), SPAN)
        return (
            [kbuf[where, h * HD : (h + 1) * HD].astype(jnp.bfloat16) for h in range(KVH)],
            [vbuf[where, h * HD : (h + 1) * HD].astype(jnp.bfloat16) for h in range(KVH)],
            lane + i * SPAN < tally[8 + kernel, r],
        )

    def beyond(r):
        def piece(i, _):
            hold(r, state, blend(row_queries(r, q_ref), [block(r, i)], held(r, state)))
            return 0

        lax.fori_loop(1, (tally[8 + kernel, r] + SPAN - 1) // SPAN, piece, 0)

    def partial_rows(pair):
        new = [blend(row_queries(r, q_ref), [block(r, 0)], None, guard=True) for r in pair]
        for r, one in zip(pair, new):
            hold(r, state, one)
        for r in pair:
            beyond(r)
        done = []
        for r in pair:
            for head in range(KVH):
                amount = total[r, head]
                safe = jnp.where(amount > 0.0, amount, 1.0)
                lines = [
                    jnp.sum(jnp.where(eye, one[:, :width], 0.0), axis=0, keepdims=True)
                    for one in (top[r, head], amount)
                ]
                done.append((r, head, (acc[r, head] / safe).astype(jnp.bfloat16), lines))
        for r, head, value, lines in done:
            out[r, head] = value
            for i in range(2):
                stats[r, head, pl.ds(i, 1), :] = lines[i]

    def with_part(r, new):
        merged = []
        for head in range(KVH):
            lines = []
            for i in range(2):
                line = jnp.broadcast_to(stats[r, head, pl.ds(i, 1), :], (width, width))
                lines.append(jnp.sum(jnp.where(eye, line, 0.0), axis=1, keepdims=True))
            other_top, other_total = lines
            other_top = jnp.where(other_total > 0.0, other_top, NEG)
            value, old_top, amount = new[head]
            new_top = jnp.maximum(old_top, other_top)
            mine = jnp.exp(old_top - new_top)
            theirs = jnp.exp(other_top - new_top) * other_total
            merged.append(
                (
                    value * mine + part[r, head].astype(jnp.float32) * theirs,
                    new_top,
                    amount * mine + theirs,
                )
            )
        return merged

    def state_rows(pair):
        new = [blend(row_queries(r, q_ref), [block(r, 0)], held(r, before)) for r in pair]
        for r, one in zip(pair, new):
            hold(r, state, one)
        for r in pair:
            beyond(r)

    def put_out(pair, new):
        done = [value / amount for one in new for value, _, amount in one]
        for i, value in enumerate(done):
            scr[i] = value
        steps = out.shape[1]
        group = width // steps
        for i, r in enumerate(pair):
            for head in range(KVH):
                for g in range(group):
                    column = (head * group + g) * HD
                    out[r, :, column : column + HD] = scr[
                        i * KVH + head, pl.ds(g, steps, stride=group), :
                    ].astype(jnp.bfloat16)

    def final_rows(pair):
        new = [blend(row_queries(r, q_ref), [block(r, 0)], held(r, before)) for r in pair]
        new = [with_part(r, one) for r, one in zip(pair, new)]
        put_out(pair, new)
        longest = functools.reduce(jnp.maximum, [tally[8 + kernel, r] for r in pair])

        @pl.when(longest > SPAN)
        def _():
            for r, one in zip(pair, new):
                hold(r, state, one)
            for r in pair:
                beyond(r)
            put_out(pair, [held(r, state) for r in pair])

    run = {"partial": partial_rows, "state": state_rows, "final": final_rows}[kind]
    together = 2 if rows % 2 == 0 else 1

    def some_rows(i, _):
        run([i * together + u for u in range(together)])
        return 0

    lax.fori_loop(0, rows // together, some_rows, 0)


def span(kind, kernel, first, cap, scalars, grouped, tables, messages, state, extra, steps):
    rows, _, width, _ = grouped.shape
    feature = messages[0].shape[-1]
    count = len(messages)
    room = (count * cap + 1) * BLK + SPAN
    smem = pl.BlockSpec(memory_space=pltpu.SMEM)
    vmem = pl.BlockSpec(memory_space=pltpu.VMEM)
    running = [pltpu.VMEM((rows, KVH, width, HD), jnp.float32)] * 3
    scratch = []
    if kind == "partial":
        out_shape = (
            jax.ShapeDtypeStruct((rows, KVH, width, HD), jnp.bfloat16),
            jax.ShapeDtypeStruct((rows, KVH, 2, width), jnp.float32),
        )
        scratch += running
    elif kind == "state":
        out_shape = state_shapes(rows, width)
    else:
        out_shape = jax.ShapeDtypeStruct((rows, steps, QH * HD), jnp.bfloat16)
        scratch += running + [pltpu.VMEM((2 * KVH, width, HD), jnp.float32)]
    scratch += [pltpu.VMEM((room, feature), jnp.float32)] * 2
    return pl.pallas_call(
        functools.partial(span_kernel, kind, kernel, first, count, cap),
        out_shape=out_shape,
        in_specs=[smem] * 7 + [vmem] * (5 + count + len(state) + len(extra)),
        out_specs=jax.tree.map(lambda _: vmem, out_shape),
        scratch_shapes=scratch,
        compiler_params=pltpu.CompilerParams(vmem_limit_bytes=GRANT),
        cost_estimate=pl.CostEstimate(
            flops=10**9, bytes_accessed=12 * 2**20, transcendentals=10**6
        ),
    )(*scalars, grouped, *tables, *messages, *state, *extra)


PHASES = {"d": (2, 2, 2, 2), "f": (0, 3, 3, 0), "g": (3, 0, 0, 3), "b": (1, 1, 1, 1)}


def site_plane(plane, flip):
    dest = plane ^ flip
    half = PLANES // 2
    if (plane < half) != (dest < half) and dest in (half - 1, half):
        return PLANES - 1 - dest
    return dest


def came_from(phase, plane):
    flips = PHASES[phase]
    return next(s for s in range(PLANES) if site_plane(s, flips[s]) == plane)


def for_mirror(phase, plane):
    source = came_from(phase, plane)
    return int(source ^ PHASES[phase][source] != plane)


def route(n, phase, offset):
    in_plane = n // PLANES
    return [
        (
            plane * in_plane + place,
            site_plane(plane, flip) * in_plane + (place + offset) % in_plane,
        )
        for plane, flip in enumerate(PHASES[phase])
        for place in range(in_plane)
    ]


STAGE = {"d": 1, "f": 1, "g": 1, "b": 2}


def device_tables(n):
    in_plane = n // PLANES
    lines = []
    for me in range(n):
        plane, place = me // in_plane, me % in_plane
        entry, stage = [], []
        post = [[-1] * n, [-1] * n]
        for phase in PHASES:
            mirror = for_mirror(phase, plane)
            for offset in range(in_plane):
                source = came_from(phase, plane) * in_plane + (place - offset) % in_plane
                entry.append(mirror * n + source)
                stage.append(0 if mirror else STAGE[phase])
                post[mirror][source] = stage[-1]
        lines.append((entry, stage, post[0], post[1]))
    return np.array(lines, np.int32)


def body(
    span_keys,
    span_values,
    block_device,
    block_row,
    cache_len,
    cache_keys,
    cache_values,
    queries,
    step_keys,
    step_values,
):
    n = lax.axis_size("seq")
    in_plane = n // PLANES
    me = lax.axis_index("seq").astype(jnp.int32)
    rows = cache_len.shape[0]
    feature = span_keys.shape[1]
    blocks = span_keys.shape[0] // BLK
    cap = max(2, (2 * blocks + n - 1) // n)
    steps = queries.shape[1]
    group = QH // KVH
    names = list(PHASES)

    phase_table = jnp.array(
        [
            [next(i for i, p in enumerate(names) if PHASES[p][z] == z ^ d) for d in range(PLANES)]
            for z in range(PLANES)
        ],
        jnp.int32,
    )
    half = PLANES // 2
    swap = [
        (a * in_plane + i, b * in_plane + i)
        for a, b in ((half - 1, half), (half, half - 1))
        for i in range(in_plane)
    ]
    mirrored = lax.ppermute(queries, "seq", swap)
    messages = pack(
        n,
        cap,
        phase_table,
        block_device[:, 0],
        span_keys.reshape(blocks, BLK, feature),
        span_values.reshape(blocks, BLK, feature),
    )
    packed = {p: messages[i * in_plane : (i + 1) * in_plane] for i, p in enumerate(names)}

    def send(phase):
        out = []
        for offset in range(in_plane):
            value = packed[phase][offset]
            pairs = route(n, phase, offset)
            if any(a != b for a, b in pairs):
                value = lax.ppermute(value, "seq", pairs)
            out.append(value)
        return out

    got = {phase: send(phase) for phase in names}

    def regroup(value):
        value = value.reshape(rows, steps, KVH, group, HD).transpose(0, 2, 1, 3, 4)
        return value.reshape(rows, KVH, steps * group, HD)

    queries, mirrored = lax.optimization_barrier((queries, mirrored))
    grouped, mirrored = regroup(queries), regroup(mirrored)
    state = resident(cache_len, grouped, step_keys, step_values, cache_keys, cache_values)

    notes = note(n, block_device[:, 0], block_row, cache_len)
    notes = lax.all_to_all(notes, "seq", split_axis=0, concat_axis=0, tiled=True)
    mine = lax.dynamic_index_in_dim(jnp.array(device_tables(n)), me, 0, keepdims=False)
    *slots, tally = index(n, cap, rows, notes, mine)
    reach = cache_keys.shape[1] // BLK + n * cap + 1
    tables = turn_tables(np.arange(2 * BLK)) + turn_tables(np.arange(reach) * BLK)
    scalars = (mine, *slots, tally, cache_len)

    partial, stats = span(
        "partial", 0, 0, cap, scalars, mirrored, tables,
        got["d"] + got["f"], (), (), steps,
    )
    partial = lax.ppermute(partial, "seq", swap)
    stats = lax.ppermute(stats, "seq", swap)
    state = span(
        "state", 1, 0, cap, scalars, grouped, tables,
        got["d"] + got["f"] + got["g"], tuple(state), (), steps,
    )
    return span(
        "final", 2, 3 * in_plane, cap, scalars, grouped, tables,
        got["b"], tuple(state), (partial, stats), steps,
    )


def solution(mesh):
    placed = (
        P(("groups", "seq"), None),
        P(("groups", "seq"), None),
        P(("groups", "seq"), None),
        P(("groups", "seq")),
        P(("groups", "seq")),
        P(("groups", "seq"), None, None),
        P(("groups", "seq"), None, None),
        P(("groups", "seq"), None, None),
        P(("groups", "seq"), None, None),
        P(("groups", "seq"), None, None),
    )

    return jax.shard_map(
        body,
        mesh=mesh,
        in_specs=placed,
        out_specs=P(("groups", "seq"), None, None),
        check_vma=False,
    )
```

```python
import functools

import jax
import jax.numpy as jnp
import numpy as np
from jax import lax
from jax.experimental import pallas as pl
from jax.experimental.pallas import tpu as pltpu
from jax.sharding import PartitionSpec as P


KVH = 4
QH = 64
HD = 128
BLK = 8
PLANES = 4
CHUNK = 256
SPAN = 128
LANES = 128
GRANT = 20 * 2**20
WIDE = 52 * 2**20
UNROLL = 4
PACKED = 4
NEG = -1e30


def frequencies(half_width):
    index = np.arange(half_width, dtype=np.float64)
    base = 1.0 / 500000.0 ** (index / half_width)
    wavelen = 2.0 * np.pi / base
    smooth = (8192.0 / wavelen - 1.0) / 3.0
    blended = (1.0 - smooth) * base / 8.0 + smooth * base
    scaled = np.where(wavelen > 8192.0, base / 8.0, blended)
    return np.where(wavelen < 2048.0, base, scaled)


def turn_tables(positions):
    freq = frequencies(HD // 2)
    angles = np.asarray(positions, np.float64)[:, None] * np.concatenate([freq, freq])[None]
    sign = np.where(np.arange(HD) < HD // 2, -1.0, 1.0)
    return jnp.array(np.cos(angles), jnp.float32), jnp.array(np.sin(angles) * sign, jnp.float32)


def pack_kernel(n, phase_table, target, keys, values, *refs):
    outs = refs[:n]
    slots, fill, rel, sems = refs[n:]
    blocks = keys.shape[0]
    in_plane = n // PLANES
    me = lax.axis_index("seq")
    plane, place = me // in_plane, me % in_plane

    def clear(p, _):
        for i in range(in_plane):
            fill[p * in_plane + i] = 0
            offset = i - place
            offset = jnp.where(offset < 0, offset + in_plane, offset)
            rel[p * in_plane + i] = phase_table[plane, p] * in_plane + offset
        return 0

    lax.fori_loop(0, PLANES, clear, 0)

    def put(step, _):
        ready = []
        for u in range(PACKED):
            b = step * PACKED + u
            dest = target[b]
            slot = fill[dest]
            fill[dest] = slot + 1
            ready.append((b, rel[dest], slot))
        for b, message, slot in ready:
            slots[message, 0, slot] = keys[b]
            slots[message, 1, slot] = values[b]
        return 0

    lax.fori_loop(0, blocks // PACKED, put, 0)
    copies = [pltpu.make_async_copy(slots.at[i], outs[i], sems.at[i]) for i in range(n)]
    for copy in copies:
        copy.start()
    for copy in copies:
        copy.wait()


def pack(n, cap, phase_table, target, keys, values):
    width = keys.shape[-1]
    message = jax.ShapeDtypeStruct((2, cap, BLK, width), jnp.bfloat16)
    smem = pl.BlockSpec(memory_space=pltpu.SMEM)
    vmem = pl.BlockSpec(memory_space=pltpu.VMEM)
    return pl.pallas_call(
        functools.partial(pack_kernel, n),
        out_shape=(message,) * n,
        in_specs=[smem] * 2 + [vmem] * 2,
        out_specs=(pl.BlockSpec(memory_space=pl.ANY),) * n,
        scratch_shapes=[
            pltpu.VMEM((n, 2, cap, BLK, width), jnp.bfloat16),
            pltpu.SMEM((n,), jnp.int32),
            pltpu.SMEM((n,), jnp.int32),
            pltpu.SemaphoreType.DMA((n,)),
        ],
        name="pack",
    )(phase_table, target, keys, values)


def twin_index(in_plane, index):
    plane = index // in_plane
    inner = (plane > 0) & (plane < PLANES - 1)
    return jnp.where(inner, (PLANES - 1 - 2 * plane) * in_plane + index, index)


def note_kernel(n, target, rows, lens, notes, fill, twins):
    in_plane = n // PLANES

    def clear(i, _):
        fill[i] = 0
        twins[i] = twin_index(in_plane, i)
        return 0

    lax.fori_loop(0, n, clear, 0, unroll=min(n, 16))
    my_twin = twins[lax.axis_index("seq")]
    for k in range(lens.shape[0]):
        notes[my_twin, 2 * LANES + k] = lens[k]

    def put(step, _):
        ready = []
        for u in range(PACKED):
            b = step * PACKED + u
            dest = target[b]
            slot = fill[dest]
            fill[dest] = slot + 1
            ready.append((dest, twins[dest], slot, rows[b]))
        for dest, twin, slot, row in ready:
            notes[dest, slot] = row
            notes[twin, LANES + slot] = row
        return 0

    lax.fori_loop(0, rows.shape[0] // PACKED, put, 0)

    def close(i, _):
        notes[i, LANES - 1] = fill[i]
        notes[twins[i], 2 * LANES - 1] = fill[i]
        return 0

    lax.fori_loop(0, n, close, 0, unroll=min(n, 4))


def note(n, target, rows, lens):
    smem = pl.BlockSpec(memory_space=pltpu.SMEM)
    return pl.pallas_call(
        functools.partial(note_kernel, n),
        out_shape=jax.ShapeDtypeStruct((n, 3 * LANES), jnp.int32),
        in_specs=[smem] * 3,
        out_specs=smem,
        scratch_shapes=[pltpu.SMEM((n,), jnp.int32), pltpu.SMEM((n,), jnp.int32)],
        name="note",
    )(target, rows, lens)


def index_kernel(n, cap, rows, notes, stages, place, row_of, rank_of, used, tally):
    f32 = jnp.float32

    def iotas(shape):
        return [lax.broadcasted_iota(jnp.int32, shape, d) for d in (0, 1)]

    a, b = iotas((cap, cap))
    before = (a < b).astype(f32)
    a, b = iotas((n, n))
    sooner = (b < a).astype(f32)
    lines = [jnp.broadcast_to(stages[i : i + 1, :n], (n, n)) for i in (2, 3)]
    posts = [
        jnp.sum(jnp.where(a == b, line, 0), axis=1, keepdims=True) for line in lines
    ]
    mates = [jnp.where(line == post, sooner, 0.0) for line, post in zip(lines, posts)]
    kernel, lane = iotas((8, LANES))
    counts = jnp.zeros((8, LANES), f32)
    for side in range(2):
        there = notes[:, side * LANES : (side + 1) * LANES]
        valid = lax.broadcasted_iota(jnp.int32, (n, cap), 1) < there[:, LANES - 1 :]
        rows_here = jnp.where(valid, there[:, :cap], -1)
        rank = jnp.zeros((n, cap), f32)
        local = jnp.zeros((n, cap), f32)
        for r in range(rows):
            hit = (rows_here == r).astype(f32)
            inside = jnp.dot(hit, before, preferred_element_type=f32)
            ahead = jnp.dot(sooner, hit, preferred_element_type=f32)
            near = jnp.dot(mates[side], hit, preferred_element_type=f32)
            rank += hit * (inside + jnp.sum(ahead, axis=1, keepdims=True))
            local += hit * (inside + jnp.sum(near, axis=1, keepdims=True))
            per_source = jnp.sum(hit, axis=1, keepdims=True)
            for stage in range(3):
                if (stage == 0) == (side == 1):
                    number = jnp.sum(
                        jnp.where(posts[side] == stage, per_source, 0.0), axis=0, keepdims=True
                    )
                    counts += jnp.where((kernel == stage) & (lane == r), number, 0.0)
        span = slice(side * n, side * n + n)
        place[span, :] = jnp.where(valid, local, -1.0).astype(jnp.int32)
        row_of[span, :] = jnp.maximum(rows_here, 0)
        rank_of[span, :] = rank.astype(jnp.int32)
        filled = jnp.sum(valid.astype(f32), axis=1, keepdims=True)
        used[span, :] = jnp.broadcast_to(filled, (n, cap)).astype(jnp.int32)
    a, b = iotas((LANES, LANES))
    begin = jnp.dot(counts, (a < b).astype(f32), preferred_element_type=f32)
    twin = twin_index(n // PLANES, lax.axis_index("seq"))
    source = lax.broadcasted_iota(jnp.int32, (n, LANES), 0)
    lens = jnp.sum(
        jnp.where(source == twin, notes[:, 2 * LANES :], 0), axis=0, keepdims=True
    )
    tally[0:8, :] = jnp.where(kernel == 3, lens, begin.astype(jnp.int32))
    tally[8:16, :] = (counts * BLK).astype(jnp.int32)


def index(n, cap, rows, notes, stages):
    vmem = pl.BlockSpec(memory_space=pltpu.VMEM)
    slots = jax.ShapeDtypeStruct((2 * n, cap), jnp.int32)
    return pl.pallas_call(
        functools.partial(index_kernel, n, cap, rows),
        out_shape=(slots,) * 4 + (jax.ShapeDtypeStruct((16, LANES), jnp.int32),),
        in_specs=[vmem] * 2,
        out_specs=(vmem,) * 5,
        compiler_params=pltpu.CompilerParams(vmem_limit_bytes=GRANT),
        name="index",
    )(notes, stages)


def as_wide(line, width):
    if width % HD == 0:
        return jnp.concatenate([line] * (width // HD), axis=1)
    return line[:, :width]


def blend(queries, pieces, old, guard=False):
    scale = HD ** (-0.5)
    heads = range(KVH)
    scores = [
        [
            jnp.where(
                piece[2],
                lax.dot_general(
                    queries[head],
                    piece[0][head],
                    (((1,), (1,)), ((), ())),
                    preferred_element_type=jnp.float32,
                )
                * scale,
                NEG,
            )
            for piece in pieces
        ]
        for head in heads
    ]
    new = []
    for head in heads:
        peak = functools.reduce(
            jnp.maximum, [jnp.max(one, axis=-1, keepdims=True) for one in scores[head]]
        )
        if old is None:
            new_top = jnp.broadcast_to(peak, (peak.shape[0], HD))
        else:
            old_acc, old_top, old_total = old[head]
            new_top = jnp.maximum(old_top, peak)
        raw = [jnp.exp(one - as_wide(new_top, one.shape[1])) for one in scores[head]]
        if guard:
            raw = [jnp.where(piece[2], one, 0.0) for piece, one in zip(pieces, raw)]
        added = sum(jnp.sum(one, axis=-1, keepdims=True) for one in raw)
        mixed = sum(
            jnp.dot(one.astype(jnp.bfloat16), piece[1][head], preferred_element_type=jnp.float32)
            for one, piece in zip(raw, pieces)
        )
        if old is None:
            new.append((mixed, new_top, jnp.broadcast_to(added, new_top.shape)))
        else:
            factor = jnp.exp(old_top - new_top)
            new.append((old_acc * factor + mixed, new_top, old_total * factor + added))
    return new


def held(row, state):
    return [tuple(one[row, head] for one in state) for head in range(KVH)]


def hold(row, state, new):
    for head in range(KVH):
        for one, value in zip(state, new[head]):
            one[row, head] = value


def row_queries(row, q_ref):
    return [q_ref[row, head] for head in range(KVH)]


def resident_kernel(
    lens, q_ref, step_k, step_v, keys, values, acc, top, total, kbuf, vbuf, sems
):
    rows, slot_count = kbuf.shape[0], kbuf.shape[1]
    piece = min(CHUNK, slot_count)
    pieces = slot_count // piece
    steps = step_k.shape[1]
    width = q_ref.shape[2]
    group = width // steps

    def copies(r, i):
        part = pl.ds(i * piece, piece)
        return (
            pltpu.make_async_copy(keys.at[r, part], kbuf.at[r, part], sems.at[0, r, i]),
            pltpu.make_async_copy(values.at[r, part], vbuf.at[r, part], sems.at[1, r, i]),
        )

    def fetch(r, _):
        for i in range(pieces):

            @pl.when((i == 0) | (i * piece < lens[r]))
            def _():
                for copy in copies(r, i):
                    copy.start()

        return 0

    lax.fori_loop(0, rows, fetch, 0)
    lane = lax.broadcasted_iota(jnp.int32, (width, piece), 1)
    causal = (
        lax.broadcasted_iota(jnp.int32, (width, steps), 1)
        <= lax.broadcasted_iota(jnp.int32, (width, steps), 0) // group
    )

    def one_row(r, _):
        def part(i):
            span = pl.ds(i * piece, piece)
            return (
                [kbuf[r, span, head * HD : (head + 1) * HD] for head in range(KVH)],
                [vbuf[r, span, head * HD : (head + 1) * HD] for head in range(KVH)],
                lane + i * piece < lens[r],
            )

        own = (
            [step_k[r, :, head * HD : (head + 1) * HD] for head in range(KVH)],
            [step_v[r, :, head * HD : (head + 1) * HD] for head in range(KVH)],
            causal,
        )
        state = (acc, top, total)
        for copy in copies(r, 0):
            copy.wait()
        hold(r, state, blend(row_queries(r, q_ref), [own, part(0)], None))
        for i in range(1, pieces):

            @pl.when(i * piece < lens[r])
            def _():
                for copy in copies(r, i):
                    copy.wait()
                hold(r, state, blend(row_queries(r, q_ref), [part(i)], held(r, state)))

        return 0

    lax.fori_loop(0, rows, one_row, 0)


def state_shapes(rows, width):
    shape = jax.ShapeDtypeStruct((rows, KVH, width, HD), jnp.float32)
    return (shape,) * 3


def resident(lens, grouped, step_k, step_v, keys, values):
    rows, slot_count, feature = keys.shape
    pieces = slot_count // min(CHUNK, slot_count)
    vmem = pl.BlockSpec(memory_space=pltpu.VMEM)
    hbm = pl.BlockSpec(memory_space=pltpu.HBM)
    return pl.pallas_call(
        resident_kernel,
        out_shape=state_shapes(rows, grouped.shape[2]),
        in_specs=[pl.BlockSpec(memory_space=pltpu.SMEM), vmem, vmem, vmem, hbm, hbm],
        out_specs=(vmem,) * 3,
        scratch_shapes=[
            pltpu.VMEM((rows, slot_count, feature), jnp.bfloat16),
            pltpu.VMEM((rows, slot_count, feature), jnp.bfloat16),
            pltpu.SemaphoreType.DMA((2, rows, pieces)),
        ],
        compiler_params=pltpu.CompilerParams(vmem_limit_bytes=WIDE),
        cost_estimate=pl.CostEstimate(
            flops=2 * 10**9, bytes_accessed=16 * 2**20, transcendentals=10**6
        ),
        name="resident",
    )(lens, grouped, step_k, step_v, keys, values)


def span_kernel(
    kind, kernel, first, count, cap, mine, place_of, row_of, rank_of, used, tally, lens,
    q_ref, ca, sa, cb, sb, *refs,
):
    messages = refs[:count]
    refs = refs[count:]
    before = refs[: 4 if kind == "final" else 3]
    if kind == "partial":
        out, stats, acc, top, total, kbuf, vbuf = refs
    elif kind == "state":
        stats, acc, top, total, theirs, kbuf, vbuf = refs[3:]
    else:
        part, out, acc, top, total, scr, kbuf, vbuf = refs[4:]
    state = (acc, top, total)
    rows = q_ref.shape[0]
    width = q_ref.shape[2]
    feature = kbuf.shape[1]
    last = tally[kernel, rows - 1] * BLK + tally[8 + kernel, rows - 1]
    tail = pl.ds(pl.multiple_of(last, BLK), SPAN)
    vbuf[tail, :] = jnp.zeros((SPAN, feature), jnp.float32)
    unroll = min(UNROLL, cap)
    trash = count * cap + SPAN // BLK
    for j in range(count):

        @pl.when(mine[1, first + j] == kernel)
        def _():
            source = mine[0, first + j]
            message = messages[j]

            def place(step, _):
                ready = []
                for u in range(unroll):
                    k = step * unroll + u
                    r = row_of[source, k]
                    rank = rank_of[source, k]
                    local = place_of[source, k]
                    slot = jnp.where(local < 0, trash, tally[kernel, r] + local)
                    length = tally[3, r] if kind == "partial" else lens[r]
                    fine, coarse = pl.ds(length % BLK, BLK), pl.ds(length // BLK + rank, 1)
                    c_a, s_a = ca[fine, :], sa[fine, :]
                    c_b, s_b = cb[coarse, :], sb[coarse, :]
                    cosine = c_a * c_b - s_a * s_b
                    sine = s_a * c_b + c_a * s_b
                    where = pl.ds(pl.multiple_of(slot * BLK, BLK), BLK)
                    value = message[1, k].astype(jnp.float32)
                    key = message[0, k].astype(jnp.float32)
                    turned = []
                    for head in range(KVH):
                        piece = key[:, head * HD : (head + 1) * HD]
                        turned.append(piece * cosine + pltpu.roll(piece, HD // 2, 1) * sine)
                    ready.append((where, turned, value))
                for where, turned, value in ready:
                    vbuf[where, :] = value
                    for head in range(KVH):
                        kbuf[where, head * HD : (head + 1) * HD] = turned[head]
                return 0

            lax.fori_loop(0, (used[source, 0] + unroll - 1) // unroll, place, 0)

    lane = lax.broadcasted_iota(jnp.int32, (width, SPAN), 1)
    eye = lax.broadcasted_iota(jnp.int32, (width, width), 0) == lax.broadcasted_iota(
        jnp.int32, (width, width), 1
    )

    def block(r, i):
        where = pl.ds(pl.multiple_of(tally[kernel, r] * BLK + i * SPAN, BLK), SPAN)
        return (
            [kbuf[where, h * HD : (h + 1) * HD].astype(jnp.bfloat16) for h in range(KVH)],
            [vbuf[where, h * HD : (h + 1) * HD].astype(jnp.bfloat16) for h in range(KVH)],
            lane + i * SPAN < tally[8 + kernel, r],
        )

    def beyond(r):
        def piece(i, _):
            hold(r, state, blend(row_queries(r, q_ref), [block(r, i)], held(r, state)))
            return 0

        lax.fori_loop(1, (tally[8 + kernel, r] + SPAN - 1) // SPAN, piece, 0)

    def partial_rows(pair):
        new = [blend(row_queries(r, q_ref), [block(r, 0)], None, guard=True) for r in pair]
        for r, one in zip(pair, new):
            hold(r, state, one)
        for r in pair:
            beyond(r)
        done = []
        for r in pair:
            for head in range(KVH):
                amount = total[r, head]
                safe = jnp.where(amount > 0.0, amount, 1.0)
                lines = [
                    jnp.sum(jnp.where(eye, one[:, :width], 0.0), axis=0, keepdims=True)
                    for one in (top[r, head], amount)
                ]
                done.append((r, head, (acc[r, head] / safe).astype(jnp.bfloat16), lines))
        for r, head, value, lines in done:
            out[r, head] = value
            for i in range(2):
                stats[r, head, pl.ds(i, 1), :] = lines[i]

    def with_stats(r, new):
        merged, factors = [], []
        for head in range(KVH):
            lines = []
            for i in range(2):
                line = jnp.broadcast_to(stats[r, head, pl.ds(i, 1), :], (width, width))
                lines.append(jnp.sum(jnp.where(eye, line, 0.0), axis=1, keepdims=True))
            other_top, other_total = lines
            other_top = jnp.where(other_total > 0.0, other_top, NEG)
            value, old_top, amount = new[head]
            new_top = jnp.maximum(old_top, other_top)
            mine = jnp.exp(old_top - new_top)
            factor = jnp.exp(other_top - new_top) * other_total
            merged.append((value * mine, new_top, amount * mine + factor))
            factors.append(factor)
        return merged, factors

    def state_rows(pair):
        for r in pair:
            hold(r, state, held(r, before))
            beyond(r)
        new = [blend(row_queries(r, q_ref), [block(r, 0)], held(r, state)) for r in pair]
        done = [with_stats(r, one) for r, one in zip(pair, new)]
        for r, (one, factors) in zip(pair, done):
            hold(r, state, one)
            for head in range(KVH):
                theirs[r, head] = factors[head]

    def with_values(r):
        return [
            (value + part[r, head].astype(jnp.float32) * before[3][r, head], old_top, amount)
            for head, (value, old_top, amount) in enumerate(held(r, before[:3]))
        ]

    def put_out(pair, new):
        done = [value / amount for one in new for value, _, amount in one]
        for i, value in enumerate(done):
            scr[i] = value
        steps = out.shape[1]
        group = width // steps
        for i, r in enumerate(pair):
            for head in range(KVH):
                for g in range(group):
                    column = (head * group + g) * HD
                    out[r, :, column : column + HD] = scr[
                        i * KVH + head, pl.ds(g, steps, stride=group), :
                    ].astype(jnp.bfloat16)

    def final_rows(pair):
        new = [blend(row_queries(r, q_ref), [block(r, 0)], with_values(r)) for r in pair]
        put_out(pair, new)
        longest = functools.reduce(jnp.maximum, [tally[8 + kernel, r] for r in pair])

        @pl.when(longest > SPAN)
        def _():
            for r, one in zip(pair, new):
                hold(r, state, one)
            for r in pair:
                beyond(r)
            put_out(pair, [held(r, state) for r in pair])

    run = {"partial": partial_rows, "state": state_rows, "final": final_rows}[kind]
    together = 2 if rows % 2 == 0 else 1

    def some_rows(i, _):
        run([i * together + u for u in range(together)])
        return 0

    lax.fori_loop(0, rows // together, some_rows, 0)


def span(kind, kernel, first, cap, scalars, grouped, tables, messages, state, extra, steps):
    rows, _, width, _ = grouped.shape
    feature = messages[0].shape[-1]
    count = len(messages)
    room = (count * cap + 1) * BLK + SPAN
    smem = pl.BlockSpec(memory_space=pltpu.SMEM)
    vmem = pl.BlockSpec(memory_space=pltpu.VMEM)
    running = [pltpu.VMEM((rows, KVH, width, HD), jnp.float32)] * 3
    scratch = []
    if kind == "partial":
        out_shape = (
            jax.ShapeDtypeStruct((rows, KVH, width, HD), jnp.bfloat16),
            jax.ShapeDtypeStruct((rows, KVH, 2, width), jnp.float32),
        )
        scratch += running
    elif kind == "state":
        out_shape = state_shapes(rows, width)
        out_shape += out_shape[:1]
    else:
        out_shape = jax.ShapeDtypeStruct((rows, steps, QH * HD), jnp.bfloat16)
        scratch += running + [pltpu.VMEM((2 * KVH, width, HD), jnp.float32)]
    scratch += [pltpu.VMEM((room, feature), jnp.float32)] * 2
    return pl.pallas_call(
        functools.partial(span_kernel, kind, kernel, first, count, cap),
        out_shape=out_shape,
        in_specs=[smem] * 7 + [vmem] * (5 + count + len(state) + len(extra)),
        out_specs=jax.tree.map(lambda _: vmem, out_shape),
        scratch_shapes=scratch,
        compiler_params=pltpu.CompilerParams(vmem_limit_bytes=GRANT),
        cost_estimate=pl.CostEstimate(
            flops=10**9, bytes_accessed=12 * 2**20, transcendentals=10**6
        ),
    )(*scalars, grouped, *tables, *messages, *state, *extra)


PHASES = {"d": (2, 2, 2, 2), "f": (0, 3, 3, 0), "g": (3, 0, 0, 3), "b": (1, 1, 1, 1)}


def site_plane(plane, flip):
    dest = plane ^ flip
    half = PLANES // 2
    if (plane < half) != (dest < half) and dest in (half - 1, half):
        return PLANES - 1 - dest
    return dest


def came_from(phase, plane):
    flips = PHASES[phase]
    return next(s for s in range(PLANES) if site_plane(s, flips[s]) == plane)


def for_mirror(phase, plane):
    source = came_from(phase, plane)
    return int(source ^ PHASES[phase][source] != plane)


def route(n, phase, offset):
    in_plane = n // PLANES
    return [
        (
            plane * in_plane + place,
            site_plane(plane, flip) * in_plane + (place + offset) % in_plane,
        )
        for plane, flip in enumerate(PHASES[phase])
        for place in range(in_plane)
    ]


STAGE = {"d": 1, "f": 1, "g": 1, "b": 2}


def device_tables(n):
    in_plane = n // PLANES
    lines = []
    for me in range(n):
        plane, place = me // in_plane, me % in_plane
        entry, stage = [], []
        post = [[-1] * n, [-1] * n]
        for phase in PHASES:
            mirror = for_mirror(phase, plane)
            for offset in range(in_plane):
                source = came_from(phase, plane) * in_plane + (place - offset) % in_plane
                entry.append(mirror * n + source)
                stage.append(0 if mirror else STAGE[phase])
                post[mirror][source] = stage[-1]
        lines.append((entry, stage, post[0], post[1]))
    return np.array(lines, np.int32)


def body(
    span_keys,
    span_values,
    block_device,
    block_row,
    cache_len,
    cache_keys,
    cache_values,
    queries,
    step_keys,
    step_values,
):
    n = lax.axis_size("seq")
    in_plane = n // PLANES
    me = lax.axis_index("seq").astype(jnp.int32)
    rows = cache_len.shape[0]
    feature = span_keys.shape[1]
    blocks = span_keys.shape[0] // BLK
    cap = max(2, (2 * blocks + n - 1) // n)
    steps = queries.shape[1]
    group = QH // KVH
    names = list(PHASES)

    phase_table = jnp.array(
        [
            [next(i for i, p in enumerate(names) if PHASES[p][z] == z ^ d) for d in range(PLANES)]
            for z in range(PLANES)
        ],
        jnp.int32,
    )
    half = PLANES // 2
    swap = [
        (a * in_plane + i, b * in_plane + i)
        for a, b in ((half - 1, half), (half, half - 1))
        for i in range(in_plane)
    ]
    mirrored = lax.ppermute(queries, "seq", swap)
    messages = pack(
        n,
        cap,
        phase_table,
        block_device[:, 0],
        span_keys.reshape(blocks, BLK, feature),
        span_values.reshape(blocks, BLK, feature),
    )
    packed = {p: messages[i * in_plane : (i + 1) * in_plane] for i, p in enumerate(names)}

    def send(phase):
        out = []
        for offset in range(in_plane):
            value = packed[phase][offset]
            pairs = route(n, phase, offset)
            if any(a != b for a, b in pairs):
                value = lax.ppermute(value, "seq", pairs)
            out.append(value)
        return out

    got = {phase: send(phase) for phase in names}

    def regroup(value):
        value = value.reshape(rows, steps, KVH, group, HD).transpose(0, 2, 1, 3, 4)
        return value.reshape(rows, KVH, steps * group, HD)

    queries, mirrored = lax.optimization_barrier((queries, mirrored))
    grouped, mirrored = regroup(queries), regroup(mirrored)
    state = resident(cache_len, grouped, step_keys, step_values, cache_keys, cache_values)

    notes = note(n, block_device[:, 0], block_row, cache_len)
    notes = lax.all_to_all(notes, "seq", split_axis=0, concat_axis=0, tiled=True)
    mine = lax.dynamic_index_in_dim(jnp.array(device_tables(n)), me, 0, keepdims=False)
    *slots, tally = index(n, cap, rows, notes, mine)
    reach = cache_keys.shape[1] // BLK + n * cap + 1
    tables = turn_tables(np.arange(2 * BLK)) + turn_tables(np.arange(reach) * BLK)
    scalars = (mine, *slots, tally, cache_len)

    partial, stats = span(
        "partial", 0, 0, cap, scalars, mirrored, tables,
        got["d"] + got["f"], (), (), steps,
    )
    partial = lax.ppermute(partial, "seq", swap)
    stats = lax.ppermute(stats, "seq", swap)
    state = span(
        "state", 1, 0, cap, scalars, grouped, tables,
        got["d"] + got["f"] + got["g"], tuple(state), (stats,), steps,
    )
    return span(
        "final", 2, 3 * in_plane, cap, scalars, grouped, tables,
        got["b"], tuple(state), (partial,), steps,
    )


def solution(mesh):
    placed = (
        P(("groups", "seq"), None),
        P(("groups", "seq"), None),
        P(("groups", "seq"), None),
        P(("groups", "seq")),
        P(("groups", "seq")),
        P(("groups", "seq"), None, None),
        P(("groups", "seq"), None, None),
        P(("groups", "seq"), None, None),
        P(("groups", "seq"), None, None),
        P(("groups", "seq"), None, None),
    )

    return jax.shard_map(
        body,
        mesh=mesh,
        in_specs=placed,
        out_specs=P(("groups", "seq"), None, None),
        check_vma=False,
    )
```

```python
import functools

import jax
import jax.numpy as jnp
import numpy as np
from jax import lax
from jax.experimental import pallas as pl
from jax.experimental.pallas import tpu as pltpu
from jax.sharding import PartitionSpec as P


KVH = 4
QH = 64
HD = 128
BLK = 8
PLANES = 4
CHUNK = 256
SPAN = 128
LANES = 128
GRANT = 20 * 2**20
WIDE = 52 * 2**20
UNROLL = 4
PACKED = 4
NEG = -1e30


def frequencies(half_width):
    index = np.arange(half_width, dtype=np.float64)
    base = 1.0 / 500000.0 ** (index / half_width)
    wavelen = 2.0 * np.pi / base
    smooth = (8192.0 / wavelen - 1.0) / 3.0
    blended = (1.0 - smooth) * base / 8.0 + smooth * base
    scaled = np.where(wavelen > 8192.0, base / 8.0, blended)
    return np.where(wavelen < 2048.0, base, scaled)


def turn_tables(positions):
    freq = frequencies(HD // 2)
    angles = np.asarray(positions, np.float64)[:, None] * np.concatenate([freq, freq])[None]
    sign = np.where(np.arange(HD) < HD // 2, -1.0, 1.0)
    return jnp.array(np.cos(angles), jnp.float32), jnp.array(np.sin(angles) * sign, jnp.float32)


def pack_kernel(n, phase_table, target, keys, values, *refs):
    outs = refs[:n]
    slots, fill, rel, sems = refs[n:]
    blocks = keys.shape[0]
    in_plane = n // PLANES
    me = lax.axis_index("seq")
    plane, place = me // in_plane, me % in_plane

    def clear(p, _):
        for i in range(in_plane):
            fill[p * in_plane + i] = 0
            offset = i - place
            offset = jnp.where(offset < 0, offset + in_plane, offset)
            rel[p * in_plane + i] = phase_table[plane, p] * in_plane + offset
        return 0

    lax.fori_loop(0, PLANES, clear, 0)

    def put(step, _):
        ready = []
        for u in range(PACKED):
            b = step * PACKED + u
            dest = target[b]
            slot = fill[dest]
            fill[dest] = slot + 1
            ready.append((b, rel[dest], slot))
        for b, message, slot in ready:
            slots[message, 0, slot] = keys[b]
            slots[message, 1, slot] = values[b]
        return 0

    lax.fori_loop(0, blocks // PACKED, put, 0)
    copies = [pltpu.make_async_copy(slots.at[i], outs[i], sems.at[i]) for i in range(n)]
    for copy in copies:
        copy.start()
    for copy in copies:
        copy.wait()


def pack(n, cap, phase_table, target, keys, values):
    width = keys.shape[-1]
    message = jax.ShapeDtypeStruct((2, cap, BLK, width), jnp.bfloat16)
    smem = pl.BlockSpec(memory_space=pltpu.SMEM)
    vmem = pl.BlockSpec(memory_space=pltpu.VMEM)
    return pl.pallas_call(
        functools.partial(pack_kernel, n),
        out_shape=(message,) * n,
        in_specs=[smem] * 2 + [vmem] * 2,
        out_specs=(pl.BlockSpec(memory_space=pl.ANY),) * n,
        scratch_shapes=[
            pltpu.VMEM((n, 2, cap, BLK, width), jnp.bfloat16),
            pltpu.SMEM((n,), jnp.int32),
            pltpu.SMEM((n,), jnp.int32),
            pltpu.SemaphoreType.DMA((n,)),
        ],
        name="pack",
    )(phase_table, target, keys, values)


def twin_index(in_plane, index):
    plane = index // in_plane
    inner = (plane > 0) & (plane < PLANES - 1)
    return jnp.where(inner, (PLANES - 1 - 2 * plane) * in_plane + index, index)


def note_kernel(n, target, rows, lens, notes, fill, twins):
    in_plane = n // PLANES

    def clear(i, _):
        fill[i] = 0
        twins[i] = twin_index(in_plane, i)
        return 0

    lax.fori_loop(0, n, clear, 0, unroll=min(n, 16))
    my_twin = twins[lax.axis_index("seq")]
    for k in range(lens.shape[0]):
        notes[my_twin, 2 * LANES + k] = lens[k]

    def put(step, _):
        ready = []
        for u in range(PACKED):
            b = step * PACKED + u
            dest = target[b]
            slot = fill[dest]
            fill[dest] = slot + 1
            ready.append((dest, twins[dest], slot, rows[b]))
        for dest, twin, slot, row in ready:
            notes[dest, slot] = row
            notes[twin, LANES + slot] = row
        return 0

    lax.fori_loop(0, rows.shape[0] // PACKED, put, 0)

    def close(i, _):
        notes[i, LANES - 1] = fill[i]
        notes[twins[i], 2 * LANES - 1] = fill[i]
        return 0

    lax.fori_loop(0, n, close, 0, unroll=min(n, 4))


def note(n, target, rows, lens):
    smem = pl.BlockSpec(memory_space=pltpu.SMEM)
    return pl.pallas_call(
        functools.partial(note_kernel, n),
        out_shape=jax.ShapeDtypeStruct((n, 3 * LANES), jnp.int32),
        in_specs=[smem] * 3,
        out_specs=smem,
        scratch_shapes=[pltpu.SMEM((n,), jnp.int32), pltpu.SMEM((n,), jnp.int32)],
        name="note",
    )(target, rows, lens)


def index_kernel(n, cap, rows, notes, stages, place, row_of, rank_of, used, tally):
    f32 = jnp.float32

    def iotas(shape):
        return [lax.broadcasted_iota(jnp.int32, shape, d) for d in (0, 1)]

    a, b = iotas((cap, cap))
    before = (a < b).astype(f32)
    a, b = iotas((n, n))
    sooner = (b < a).astype(f32)
    lines = [jnp.broadcast_to(stages[i : i + 1, :n], (n, n)) for i in (2, 3)]
    posts = [
        jnp.sum(jnp.where(a == b, line, 0), axis=1, keepdims=True) for line in lines
    ]
    mates = [jnp.where(line == post, sooner, 0.0) for line, post in zip(lines, posts)]
    kernel, lane = iotas((8, LANES))
    counts = jnp.zeros((8, LANES), f32)
    locals_ = []
    for side in range(2):
        there = notes[:, side * LANES : (side + 1) * LANES]
        valid = lax.broadcasted_iota(jnp.int32, (n, cap), 1) < there[:, LANES - 1 :]
        rows_here = jnp.where(valid, there[:, :cap], -1)
        rank = jnp.zeros((n, cap), f32)
        local = jnp.zeros((n, cap), f32)
        for r in range(rows):
            hit = (rows_here == r).astype(f32)
            inside = jnp.dot(hit, before, preferred_element_type=f32)
            ahead = jnp.dot(sooner, hit, preferred_element_type=f32)
            near = jnp.dot(mates[side], hit, preferred_element_type=f32)
            rank += hit * (inside + jnp.sum(ahead, axis=1, keepdims=True))
            local += hit * (inside + jnp.sum(near, axis=1, keepdims=True))
            per_source = jnp.sum(hit, axis=1, keepdims=True)
            for stage in range(3):
                if (stage == 0) == (side == 1):
                    number = jnp.sum(
                        jnp.where(posts[side] == stage, per_source, 0.0), axis=0, keepdims=True
                    )
                    counts += jnp.where((kernel == stage) & (lane == r), number, 0.0)
        span = slice(side * n, side * n + n)
        locals_.append((span, valid, rows_here, local))
        row_of[span, :] = jnp.maximum(rows_here, 0)
        rank_of[span, :] = rank.astype(jnp.int32)
        filled = jnp.sum(valid.astype(f32), axis=1, keepdims=True)
        used[span, :] = jnp.broadcast_to(filled, (n, cap)).astype(jnp.int32)
    a, b = iotas((LANES, LANES))
    begin = jnp.dot(counts, (a < b).astype(f32), preferred_element_type=f32)
    in_plane = n // PLANES
    messages = {0: 2 * in_plane, 1: 3 * in_plane, 2: in_plane}
    for side, (span, valid, rows_here, local) in enumerate(locals_):
        unfilled = jnp.zeros((n, 1), f32)
        for stage in range(3):
            if (stage == 0) != (side == 1):
                continue
            mine = posts[side] == stage
            unfilled += jnp.where(mine, float(messages[stage] * cap + SPAN // BLK), 0.0)
            for r in range(rows):
                here = jnp.where(mine, begin[stage : stage + 1, r : r + 1], 0.0)
                local += jnp.where(rows_here == r, here, 0.0)
        place[span, :] = (jnp.where(valid, local, unfilled) * BLK).astype(jnp.int32)
    twin = twin_index(in_plane, lax.axis_index("seq"))
    source = lax.broadcasted_iota(jnp.int32, (n, LANES), 0)
    lens = jnp.sum(
        jnp.where(source == twin, notes[:, 2 * LANES :], 0), axis=0, keepdims=True
    )
    tally[0:8, :] = jnp.where(kernel == 3, lens, begin.astype(jnp.int32))
    tally[8:16, :] = (counts * BLK).astype(jnp.int32)


def index(n, cap, rows, notes, stages):
    vmem = pl.BlockSpec(memory_space=pltpu.VMEM)
    slots = jax.ShapeDtypeStruct((2 * n, cap), jnp.int32)
    return pl.pallas_call(
        functools.partial(index_kernel, n, cap, rows),
        out_shape=(slots,) * 4 + (jax.ShapeDtypeStruct((16, LANES), jnp.int32),),
        in_specs=[vmem] * 2,
        out_specs=(vmem,) * 5,
        compiler_params=pltpu.CompilerParams(vmem_limit_bytes=GRANT),
        name="index",
    )(notes, stages)


def as_wide(line, width):
    if width % HD == 0:
        return jnp.concatenate([line] * (width // HD), axis=1)
    return line[:, :width]


def blend(queries, pieces, old, guard=False):
    scale = HD ** (-0.5)
    heads = range(KVH)
    scores = [
        [
            jnp.where(
                piece[2],
                lax.dot_general(
                    queries[head],
                    piece[0][head],
                    (((1,), (1,)), ((), ())),
                    preferred_element_type=jnp.float32,
                )
                * scale,
                NEG,
            )
            for piece in pieces
        ]
        for head in heads
    ]
    new = []
    for head in heads:
        peak = functools.reduce(
            jnp.maximum, [jnp.max(one, axis=-1, keepdims=True) for one in scores[head]]
        )
        if old is None:
            new_top = jnp.broadcast_to(peak, (peak.shape[0], HD))
        else:
            old_acc, old_top, old_total = old[head]
            new_top = jnp.maximum(old_top, peak)
        raw = [jnp.exp(one - as_wide(new_top, one.shape[1])) for one in scores[head]]
        if guard:
            raw = [jnp.where(piece[2], one, 0.0) for piece, one in zip(pieces, raw)]
        added = sum(jnp.sum(one, axis=-1, keepdims=True) for one in raw)
        mixed = sum(
            jnp.dot(one.astype(jnp.bfloat16), piece[1][head], preferred_element_type=jnp.float32)
            for one, piece in zip(raw, pieces)
        )
        if old is None:
            new.append((mixed, new_top, jnp.broadcast_to(added, new_top.shape)))
        else:
            factor = jnp.exp(old_top - new_top)
            new.append((old_acc * factor + mixed, new_top, old_total * factor + added))
    return new


def held(row, state):
    return [tuple(one[row, head] for one in state) for head in range(KVH)]


def hold(row, state, new):
    for head in range(KVH):
        for one, value in zip(state, new[head]):
            one[row, head] = value


def row_queries(row, q_ref):
    return [q_ref[row, head] for head in range(KVH)]


def resident_kernel(
    lens, q_ref, step_k, step_v, keys, values, acc, top, total, kbuf, vbuf, sems
):
    rows, slot_count = kbuf.shape[0], kbuf.shape[1]
    piece = min(CHUNK, slot_count)
    pieces = slot_count // piece
    steps = step_k.shape[1]
    width = q_ref.shape[2]
    group = width // steps

    def copies(r, i):
        part = pl.ds(i * piece, piece)
        return (
            pltpu.make_async_copy(keys.at[r, part], kbuf.at[r, part], sems.at[0, r, i]),
            pltpu.make_async_copy(values.at[r, part], vbuf.at[r, part], sems.at[1, r, i]),
        )

    def fetch(r, _):
        for i in range(pieces):

            @pl.when((i == 0) | (i * piece < lens[r]))
            def _():
                for copy in copies(r, i):
                    copy.start()

        return 0

    lax.fori_loop(0, rows, fetch, 0)
    lane = lax.broadcasted_iota(jnp.int32, (width, piece), 1)
    causal = (
        lax.broadcasted_iota(jnp.int32, (width, steps), 1)
        <= lax.broadcasted_iota(jnp.int32, (width, steps), 0) // group
    )

    def one_row(r, _):
        def part(i):
            span = pl.ds(i * piece, piece)
            return (
                [kbuf[r, span, head * HD : (head + 1) * HD] for head in range(KVH)],
                [vbuf[r, span, head * HD : (head + 1) * HD] for head in range(KVH)],
                lane + i * piece < lens[r],
            )

        own = (
            [step_k[r, :, head * HD : (head + 1) * HD] for head in range(KVH)],
            [step_v[r, :, head * HD : (head + 1) * HD] for head in range(KVH)],
            causal,
        )
        state = (acc, top, total)
        for copy in copies(r, 0):
            copy.wait()
        hold(r, state, blend(row_queries(r, q_ref), [own, part(0)], None))
        for i in range(1, pieces):

            @pl.when(i * piece < lens[r])
            def _():
                for copy in copies(r, i):
                    copy.wait()
                hold(r, state, blend(row_queries(r, q_ref), [part(i)], held(r, state)))

        return 0

    lax.fori_loop(0, rows, one_row, 0)


def state_shapes(rows, width):
    shape = jax.ShapeDtypeStruct((rows, KVH, width, HD), jnp.float32)
    return (shape,) * 3


def resident(lens, grouped, step_k, step_v, keys, values):
    rows, slot_count, feature = keys.shape
    pieces = slot_count // min(CHUNK, slot_count)
    vmem = pl.BlockSpec(memory_space=pltpu.VMEM)
    hbm = pl.BlockSpec(memory_space=pltpu.HBM)
    return pl.pallas_call(
        resident_kernel,
        out_shape=state_shapes(rows, grouped.shape[2]),
        in_specs=[pl.BlockSpec(memory_space=pltpu.SMEM), vmem, vmem, vmem, hbm, hbm],
        out_specs=(vmem,) * 3,
        scratch_shapes=[
            pltpu.VMEM((rows, slot_count, feature), jnp.bfloat16),
            pltpu.VMEM((rows, slot_count, feature), jnp.bfloat16),
            pltpu.SemaphoreType.DMA((2, rows, pieces)),
        ],
        compiler_params=pltpu.CompilerParams(vmem_limit_bytes=WIDE),
        cost_estimate=pl.CostEstimate(
            flops=2 * 10**9, bytes_accessed=16 * 2**20, transcendentals=10**6
        ),
        name="resident",
    )(lens, grouped, step_k, step_v, keys, values)


def span_kernel(
    kind, kernel, first, count, cap, mine, place_of, row_of, rank_of, used, tally, lens,
    q_ref, ca, sa, cb, sb, *refs,
):
    messages = refs[:count]
    refs = refs[count:]
    before = refs[: 4 if kind == "final" else 3]
    if kind == "partial":
        out, stats, acc, top, total, kbuf, vbuf = refs
    elif kind == "state":
        stats, acc, top, total, theirs, kbuf, vbuf = refs[3:]
    else:
        part, out, acc, top, total, scr, kbuf, vbuf = refs[4:]
    state = (acc, top, total)
    rows = q_ref.shape[0]
    width = q_ref.shape[2]
    feature = kbuf.shape[1]
    last = tally[kernel, rows - 1] * BLK + tally[8 + kernel, rows - 1]
    tail = pl.ds(pl.multiple_of(last, BLK), SPAN)
    vbuf[tail, :] = jnp.zeros((SPAN, feature), jnp.float32)
    unroll = min(UNROLL, cap)
    for j in range(count):

        @pl.when(mine[1, first + j] == kernel)
        def _():
            source = mine[0, first + j]
            message = messages[j]

            def place(step, _):
                ready = []
                for u in range(unroll):
                    k = step * unroll + u
                    r = row_of[source, k]
                    rank = rank_of[source, k]
                    length = tally[3, r] if kind == "partial" else lens[r]
                    fine = pl.ds(length & (BLK - 1), BLK)
                    coarse = pl.ds(lax.shift_right_logical(length, BLK.bit_length() - 1) + rank, 1)
                    c_a, s_a = ca[fine, :], sa[fine, :]
                    c_b, s_b = cb[coarse, :], sb[coarse, :]
                    cosine = c_a * c_b - s_a * s_b
                    sine = s_a * c_b + c_a * s_b
                    where = pl.ds(pl.multiple_of(place_of[source, k], BLK), BLK)
                    value = message[1, k].astype(jnp.float32)
                    key = message[0, k].astype(jnp.float32)
                    turned = []
                    for head in range(KVH):
                        piece = key[:, head * HD : (head + 1) * HD]
                        turned.append(piece * cosine + pltpu.roll(piece, HD // 2, 1) * sine)
                    ready.append((where, turned, value))
                for where, turned, value in ready:
                    vbuf[where, :] = value
                    for head in range(KVH):
                        kbuf[where, head * HD : (head + 1) * HD] = turned[head]
                return 0

            lax.fori_loop(0, (used[source, 0] + unroll - 1) // unroll, place, 0)

    lane = lax.broadcasted_iota(jnp.int32, (width, SPAN), 1)
    eye = lax.broadcasted_iota(jnp.int32, (width, width), 0) == lax.broadcasted_iota(
        jnp.int32, (width, width), 1
    )

    def block(r, i):
        where = pl.ds(pl.multiple_of(tally[kernel, r] * BLK + i * SPAN, BLK), SPAN)
        return (
            [kbuf[where, h * HD : (h + 1) * HD].astype(jnp.bfloat16) for h in range(KVH)],
            [vbuf[where, h * HD : (h + 1) * HD].astype(jnp.bfloat16) for h in range(KVH)],
            lane + i * SPAN < tally[8 + kernel, r],
        )

    def beyond(r):
        def piece(i, _):
            hold(r, state, blend(row_queries(r, q_ref), [block(r, i)], held(r, state)))
            return 0

        lax.fori_loop(1, (tally[8 + kernel, r] + SPAN - 1) // SPAN, piece, 0)

    def partial_rows(pair):
        new = [blend(row_queries(r, q_ref), [block(r, 0)], None, guard=True) for r in pair]
        for r, one in zip(pair, new):
            hold(r, state, one)
        for r in pair:
            beyond(r)
        done = []
        for r in pair:
            for head in range(KVH):
                amount = total[r, head]
                safe = jnp.where(amount > 0.0, amount, 1.0)
                lines = [
                    jnp.sum(jnp.where(eye, one[:, :width], 0.0), axis=0, keepdims=True)
                    for one in (top[r, head], amount)
                ]
                done.append((r, head, (acc[r, head] / safe).astype(jnp.bfloat16), lines))
        for r, head, value, lines in done:
            out[r, head] = value
            for i in range(2):
                stats[r, head, pl.ds(i, 1), :] = lines[i]

    def with_stats(r, new):
        merged, factors = [], []
        for head in range(KVH):
            lines = []
            for i in range(2):
                line = jnp.broadcast_to(stats[r, head, pl.ds(i, 1), :], (width, width))
                lines.append(jnp.sum(jnp.where(eye, line, 0.0), axis=1, keepdims=True))
            other_top, other_total = lines
            other_top = jnp.where(other_total > 0.0, other_top, NEG)
            value, old_top, amount = new[head]
            new_top = jnp.maximum(old_top, other_top)
            mine = jnp.exp(old_top - new_top)
            factor = jnp.exp(other_top - new_top) * other_total
            merged.append((value * mine, new_top, amount * mine + factor))
            factors.append(factor)
        return merged, factors

    def state_rows(pair):
        for r in pair:
            hold(r, state, held(r, before))
            beyond(r)
        new = [blend(row_queries(r, q_ref), [block(r, 0)], held(r, state)) for r in pair]
        done = [with_stats(r, one) for r, one in zip(pair, new)]
        for r, (one, factors) in zip(pair, done):
            hold(r, state, one)
            for head in range(KVH):
                theirs[r, head] = factors[head]

    def with_values(r):
        return [
            (value + part[r, head].astype(jnp.float32) * before[3][r, head], old_top, amount)
            for head, (value, old_top, amount) in enumerate(held(r, before[:3]))
        ]

    def put_out(pair, new):
        done = [value / amount for one in new for value, _, amount in one]
        for i, value in enumerate(done):
            scr[i] = value
        steps = out.shape[1]
        group = width // steps
        for i, r in enumerate(pair):
            for head in range(KVH):
                for g in range(group):
                    column = (head * group + g) * HD
                    out[r, :, column : column + HD] = scr[
                        i * KVH + head, pl.ds(g, steps, stride=group), :
                    ].astype(jnp.bfloat16)

    def final_rows(pair):
        new = [blend(row_queries(r, q_ref), [block(r, 0)], with_values(r)) for r in pair]
        put_out(pair, new)
        longest = functools.reduce(jnp.maximum, [tally[8 + kernel, r] for r in pair])

        @pl.when(longest > SPAN)
        def _():
            for r, one in zip(pair, new):
                hold(r, state, one)
            for r in pair:
                beyond(r)
            put_out(pair, [held(r, state) for r in pair])

    run = {"partial": partial_rows, "state": state_rows, "final": final_rows}[kind]
    together = 2 if rows % 2 == 0 else 1

    def some_rows(i, _):
        run([i * together + u for u in range(together)])
        return 0

    lax.fori_loop(0, rows // together, some_rows, 0)


def span(kind, kernel, first, cap, scalars, grouped, tables, messages, state, extra, steps):
    rows, _, width, _ = grouped.shape
    feature = messages[0].shape[-1]
    count = len(messages)
    room = (count * cap + 1) * BLK + SPAN
    smem = pl.BlockSpec(memory_space=pltpu.SMEM)
    vmem = pl.BlockSpec(memory_space=pltpu.VMEM)
    running = [pltpu.VMEM((rows, KVH, width, HD), jnp.float32)] * 3
    scratch = []
    if kind == "partial":
        out_shape = (
            jax.ShapeDtypeStruct((rows, KVH, width, HD), jnp.bfloat16),
            jax.ShapeDtypeStruct((rows, KVH, 2, width), jnp.float32),
        )
        scratch += running
    elif kind == "state":
        out_shape = state_shapes(rows, width)
        out_shape += out_shape[:1]
    else:
        out_shape = jax.ShapeDtypeStruct((rows, steps, QH * HD), jnp.bfloat16)
        scratch += running + [pltpu.VMEM((2 * KVH, width, HD), jnp.float32)]
    scratch += [pltpu.VMEM((room, feature), jnp.float32)] * 2
    return pl.pallas_call(
        functools.partial(span_kernel, kind, kernel, first, count, cap),
        out_shape=out_shape,
        in_specs=[smem] * 7 + [vmem] * (5 + count + len(state) + len(extra)),
        out_specs=jax.tree.map(lambda _: vmem, out_shape),
        scratch_shapes=scratch,
        compiler_params=pltpu.CompilerParams(vmem_limit_bytes=GRANT),
        cost_estimate=pl.CostEstimate(
            flops=10**9, bytes_accessed=12 * 2**20, transcendentals=10**6
        ),
    )(*scalars, grouped, *tables, *messages, *state, *extra)


PHASES = {"d": (2, 2, 2, 2), "f": (0, 3, 3, 0), "g": (3, 0, 0, 3), "b": (1, 1, 1, 1)}


def site_plane(plane, flip):
    dest = plane ^ flip
    half = PLANES // 2
    if (plane < half) != (dest < half) and dest in (half - 1, half):
        return PLANES - 1 - dest
    return dest


def came_from(phase, plane):
    flips = PHASES[phase]
    return next(s for s in range(PLANES) if site_plane(s, flips[s]) == plane)


def for_mirror(phase, plane):
    source = came_from(phase, plane)
    return int(source ^ PHASES[phase][source] != plane)


def route(n, phase, offset):
    in_plane = n // PLANES
    return [
        (
            plane * in_plane + place,
            site_plane(plane, flip) * in_plane + (place + offset) % in_plane,
        )
        for plane, flip in enumerate(PHASES[phase])
        for place in range(in_plane)
    ]


STAGE = {"d": 1, "f": 1, "g": 1, "b": 2}


def device_tables(n):
    in_plane = n // PLANES
    lines = []
    for me in range(n):
        plane, place = me // in_plane, me % in_plane
        entry, stage = [], []
        post = [[-1] * n, [-1] * n]
        for phase in PHASES:
            mirror = for_mirror(phase, plane)
            for offset in range(in_plane):
                source = came_from(phase, plane) * in_plane + (place - offset) % in_plane
                entry.append(mirror * n + source)
                stage.append(0 if mirror else STAGE[phase])
                post[mirror][source] = stage[-1]
        lines.append((entry, stage, post[0], post[1]))
    return np.array(lines, np.int32)


def body(
    span_keys,
    span_values,
    block_device,
    block_row,
    cache_len,
    cache_keys,
    cache_values,
    queries,
    step_keys,
    step_values,
):
    n = lax.axis_size("seq")
    in_plane = n // PLANES
    me = lax.axis_index("seq").astype(jnp.int32)
    rows = cache_len.shape[0]
    feature = span_keys.shape[1]
    blocks = span_keys.shape[0] // BLK
    cap = max(2, (2 * blocks + n - 1) // n)
    steps = queries.shape[1]
    group = QH // KVH
    names = list(PHASES)

    phase_table = jnp.array(
        [
            [next(i for i, p in enumerate(names) if PHASES[p][z] == z ^ d) for d in range(PLANES)]
            for z in range(PLANES)
        ],
        jnp.int32,
    )
    half = PLANES // 2
    swap = [
        (a * in_plane + i, b * in_plane + i)
        for a, b in ((half - 1, half), (half, half - 1))
        for i in range(in_plane)
    ]
    mirrored = lax.ppermute(queries, "seq", swap)
    messages = pack(
        n,
        cap,
        phase_table,
        block_device[:, 0],
        span_keys.reshape(blocks, BLK, feature),
        span_values.reshape(blocks, BLK, feature),
    )
    packed = {p: messages[i * in_plane : (i + 1) * in_plane] for i, p in enumerate(names)}

    def send(phase):
        out = []
        for offset in range(in_plane):
            value = packed[phase][offset]
            pairs = route(n, phase, offset)
            if any(a != b for a, b in pairs):
                value = lax.ppermute(value, "seq", pairs)
            out.append(value)
        return out

    got = {phase: send(phase) for phase in names}

    def regroup(value):
        value = value.reshape(rows, steps, KVH, group, HD).transpose(0, 2, 1, 3, 4)
        return value.reshape(rows, KVH, steps * group, HD)

    queries, mirrored = lax.optimization_barrier((queries, mirrored))
    grouped, mirrored = regroup(queries), regroup(mirrored)
    state = resident(cache_len, grouped, step_keys, step_values, cache_keys, cache_values)

    notes = note(n, block_device[:, 0], block_row, cache_len)
    notes = lax.all_to_all(notes, "seq", split_axis=0, concat_axis=0, tiled=True)
    mine = lax.dynamic_index_in_dim(jnp.array(device_tables(n)), me, 0, keepdims=False)
    *slots, tally = index(n, cap, rows, notes, mine)
    reach = cache_keys.shape[1] // BLK + n * cap + 1
    tables = turn_tables(np.arange(2 * BLK)) + turn_tables(np.arange(reach) * BLK)
    scalars = (mine, *slots, tally, cache_len)

    partial, stats = span(
        "partial", 0, 0, cap, scalars, mirrored, tables,
        got["d"] + got["f"], (), (), steps,
    )
    partial = lax.ppermute(partial, "seq", swap)
    stats = lax.ppermute(stats, "seq", swap)
    state = span(
        "state", 1, 0, cap, scalars, grouped, tables,
        got["d"] + got["f"] + got["g"], tuple(state), (stats,), steps,
    )
    return span(
        "final", 2, 3 * in_plane, cap, scalars, grouped, tables,
        got["b"], tuple(state), (partial,), steps,
    )


def solution(mesh):
    placed = (
        P(("groups", "seq"), None),
        P(("groups", "seq"), None),
        P(("groups", "seq"), None),
        P(("groups", "seq")),
        P(("groups", "seq")),
        P(("groups", "seq"), None, None),
        P(("groups", "seq"), None, None),
        P(("groups", "seq"), None, None),
        P(("groups", "seq"), None, None),
        P(("groups", "seq"), None, None),
    )

    return jax.shard_map(
        body,
        mesh=mesh,
        in_specs=placed,
        out_specs=P(("groups", "seq"), None, None),
        check_vma=False,
    )
```

```python
import functools

import jax
import jax.numpy as jnp
import numpy as np
from jax import lax
from jax.experimental import pallas as pl
from jax.experimental.pallas import tpu as pltpu
from jax.sharding import PartitionSpec as P


KVH = 4
QH = 64
HD = 128
BLK = 8
PLANES = 4
CHUNK = 256
SPAN = 128
LANES = 128
GRANT = 20 * 2**20
WIDE = 52 * 2**20
UNROLL = 4
PACKED = 4
NEG = -1e30


def frequencies(half_width):
    index = np.arange(half_width, dtype=np.float64)
    base = 1.0 / 500000.0 ** (index / half_width)
    wavelen = 2.0 * np.pi / base
    smooth = (8192.0 / wavelen - 1.0) / 3.0
    blended = (1.0 - smooth) * base / 8.0 + smooth * base
    scaled = np.where(wavelen > 8192.0, base / 8.0, blended)
    return np.where(wavelen < 2048.0, base, scaled)


def turn_tables(positions):
    freq = frequencies(HD // 2)
    angles = np.asarray(positions, np.float64)[:, None] * np.concatenate([freq, freq])[None]
    sign = np.where(np.arange(HD) < HD // 2, -1.0, 1.0)
    return jnp.array(np.cos(angles), jnp.float32), jnp.array(np.sin(angles) * sign, jnp.float32)


def pack_kernel(n, phase_table, target, keys, values, *refs):
    outs = refs[:n]
    slots, fill, rel, sems = refs[n:]
    blocks = keys.shape[0]
    in_plane = n // PLANES
    me = lax.axis_index("seq")
    plane, place = me // in_plane, me % in_plane

    def clear(p, _):
        for i in range(in_plane):
            fill[p * in_plane + i] = 0
            offset = i - place
            offset = jnp.where(offset < 0, offset + in_plane, offset)
            rel[p * in_plane + i] = phase_table[plane, p] * in_plane + offset
        return 0

    lax.fori_loop(0, PLANES, clear, 0)

    def put(step, _):
        ready = []
        for u in range(PACKED):
            b = step * PACKED + u
            dest = target[b]
            slot = fill[dest]
            fill[dest] = slot + 1
            ready.append((b, rel[dest], slot))
        for b, message, slot in ready:
            slots[message, 0, slot] = keys[b]
            slots[message, 1, slot] = values[b]
        return 0

    lax.fori_loop(0, blocks // PACKED, put, 0)
    copies = [pltpu.make_async_copy(slots.at[i], outs[i], sems.at[i]) for i in range(n)]
    for copy in copies:
        copy.start()
    for copy in copies:
        copy.wait()


def pack(n, cap, phase_table, target, keys, values):
    width = keys.shape[-1]
    message = jax.ShapeDtypeStruct((2, cap, BLK, width), jnp.bfloat16)
    smem = pl.BlockSpec(memory_space=pltpu.SMEM)
    vmem = pl.BlockSpec(memory_space=pltpu.VMEM)
    return pl.pallas_call(
        functools.partial(pack_kernel, n),
        out_shape=(message,) * n,
        in_specs=[smem] * 2 + [vmem] * 2,
        out_specs=(pl.BlockSpec(memory_space=pl.ANY),) * n,
        scratch_shapes=[
            pltpu.VMEM((n, 2, cap, BLK, width), jnp.bfloat16),
            pltpu.SMEM((n,), jnp.int32),
            pltpu.SMEM((n,), jnp.int32),
            pltpu.SemaphoreType.DMA((n,)),
        ],
        name="pack",
    )(phase_table, target, keys, values)


def twin_index(in_plane, index):
    plane = index // in_plane
    inner = (plane > 0) & (plane < PLANES - 1)
    return jnp.where(inner, (PLANES - 1 - 2 * plane) * in_plane + index, index)


def note_kernel(n, target, rows, lens, notes, fill, twins):
    in_plane = n // PLANES

    def clear(i, _):
        fill[i] = 0
        twins[i] = twin_index(in_plane, i)
        return 0

    lax.fori_loop(0, n, clear, 0, unroll=min(n, 16))
    my_twin = twins[lax.axis_index("seq")]
    for k in range(lens.shape[0]):
        notes[my_twin, 0, 2 * LANES + k] = lens[k]

    def put(step, _):
        ready = []
        for u in range(PACKED):
            b = step * PACKED + u
            dest = target[b]
            slot = fill[dest]
            fill[dest] = slot + 1
            ready.append((dest, twins[dest], slot, rows[b]))
        for dest, twin, slot, row in ready:
            notes[dest, 0, slot] = row
            notes[twin, 0, LANES + slot] = row
        return 0

    lax.fori_loop(0, rows.shape[0] // PACKED, put, 0)

    def close(i, _):
        notes[i, 0, LANES - 1] = fill[i]
        notes[twins[i], 0, 2 * LANES - 1] = fill[i]
        return 0

    lax.fori_loop(0, n, close, 0, unroll=min(n, 4))


def note(n, target, rows, lens):
    smem = pl.BlockSpec(memory_space=pltpu.SMEM)
    return pl.pallas_call(
        functools.partial(note_kernel, n),
        out_shape=jax.ShapeDtypeStruct((n, 1, 3 * LANES), jnp.int32),
        in_specs=[smem] * 3,
        out_specs=smem,
        scratch_shapes=[pltpu.SMEM((n,), jnp.int32), pltpu.SMEM((n,), jnp.int32)],
        name="note",
    )(target, rows, lens)


def index_kernel(n, cap, rows, notes, stages, place, row_of, rank_of, used, tally):
    f32 = jnp.float32

    def iotas(shape):
        return [lax.broadcasted_iota(jnp.int32, shape, d) for d in (0, 1)]

    a, b = iotas((cap, cap))
    before = (a < b).astype(f32)
    a, b = iotas((n, n))
    sooner = (b < a).astype(f32)
    lines = [jnp.broadcast_to(stages[i : i + 1, :n], (n, n)) for i in (2, 3)]
    posts = [
        jnp.sum(jnp.where(a == b, line, 0), axis=1, keepdims=True) for line in lines
    ]
    mates = [jnp.where(line == post, sooner, 0.0) for line, post in zip(lines, posts)]
    kernel, lane = iotas((8, LANES))
    counts = jnp.zeros((8, LANES), f32)
    locals_ = []
    for side in range(2):
        there = notes[:, 0, side * LANES : (side + 1) * LANES]
        valid = lax.broadcasted_iota(jnp.int32, (n, cap), 1) < there[:, LANES - 1 :]
        rows_here = jnp.where(valid, there[:, :cap], -1)
        rank = jnp.zeros((n, cap), f32)
        local = jnp.zeros((n, cap), f32)
        for r in range(rows):
            hit = (rows_here == r).astype(f32)
            inside = jnp.dot(hit, before, preferred_element_type=f32)
            ahead = jnp.dot(sooner, hit, preferred_element_type=f32)
            near = jnp.dot(mates[side], hit, preferred_element_type=f32)
            rank += hit * (inside + jnp.sum(ahead, axis=1, keepdims=True))
            local += hit * (inside + jnp.sum(near, axis=1, keepdims=True))
            per_source = jnp.sum(hit, axis=1, keepdims=True)
            for stage in range(3):
                if (stage == 0) == (side == 1):
                    number = jnp.sum(
                        jnp.where(posts[side] == stage, per_source, 0.0), axis=0, keepdims=True
                    )
                    counts += jnp.where((kernel == stage) & (lane == r), number, 0.0)
        span = slice(side * n, side * n + n)
        locals_.append((span, valid, rows_here, local))
        row_of[span, :] = jnp.maximum(rows_here, 0)
        rank_of[span, :] = rank.astype(jnp.int32)
        filled = jnp.sum(valid.astype(f32), axis=1, keepdims=True)
        used[span, :] = jnp.broadcast_to(filled, (n, cap)).astype(jnp.int32)
    a, b = iotas((LANES, LANES))
    begin = jnp.dot(counts, (a < b).astype(f32), preferred_element_type=f32)
    in_plane = n // PLANES
    messages = {0: 2 * in_plane, 1: 3 * in_plane, 2: in_plane}
    for side, (span, valid, rows_here, local) in enumerate(locals_):
        unfilled = jnp.zeros((n, 1), f32)
        for stage in range(3):
            if (stage == 0) != (side == 1):
                continue
            mine = posts[side] == stage
            unfilled += jnp.where(mine, float(messages[stage] * cap + SPAN // BLK), 0.0)
            for r in range(rows):
                here = jnp.where(mine, begin[stage : stage + 1, r : r + 1], 0.0)
                local += jnp.where(rows_here == r, here, 0.0)
        place[span, :] = (jnp.where(valid, local, unfilled) * BLK).astype(jnp.int32)
    twin = twin_index(in_plane, lax.axis_index("seq"))
    source = lax.broadcasted_iota(jnp.int32, (n, LANES), 0)
    lens = jnp.sum(
        jnp.where(source == twin, notes[:, 0, 2 * LANES :], 0), axis=0, keepdims=True
    )
    tally[0:8, :] = jnp.where(kernel == 3, lens, begin.astype(jnp.int32))
    tally[8:16, :] = (counts * BLK).astype(jnp.int32)


def index(n, cap, rows, notes, stages):
    vmem = pl.BlockSpec(memory_space=pltpu.VMEM)
    slots = jax.ShapeDtypeStruct((2 * n, cap), jnp.int32)
    return pl.pallas_call(
        functools.partial(index_kernel, n, cap, rows),
        out_shape=(slots,) * 4 + (jax.ShapeDtypeStruct((16, LANES), jnp.int32),),
        in_specs=[vmem] * 2,
        out_specs=(vmem,) * 5,
        compiler_params=pltpu.CompilerParams(vmem_limit_bytes=GRANT),
        name="index",
    )(notes, stages)


def as_wide(line, width):
    if width % HD == 0:
        return jnp.concatenate([line] * (width // HD), axis=1)
    return line[:, :width]


def blend(queries, pieces, old, guard=False):
    scale = HD ** (-0.5)
    heads = range(KVH)
    scores = [
        [
            jnp.where(
                piece[2],
                lax.dot_general(
                    queries[head],
                    piece[0][head],
                    (((1,), (1,)), ((), ())),
                    preferred_element_type=jnp.float32,
                )
                * scale,
                NEG,
            )
            for piece in pieces
        ]
        for head in heads
    ]
    new = []
    for head in heads:
        peak = functools.reduce(
            jnp.maximum, [jnp.max(one, axis=-1, keepdims=True) for one in scores[head]]
        )
        if old is None:
            new_top = jnp.broadcast_to(peak, (peak.shape[0], HD))
        else:
            old_acc, old_top, old_total = old[head]
            new_top = jnp.maximum(old_top, peak)
        raw = [jnp.exp(one - as_wide(new_top, one.shape[1])) for one in scores[head]]
        if guard:
            raw = [jnp.where(piece[2], one, 0.0) for piece, one in zip(pieces, raw)]
        added = sum(jnp.sum(one, axis=-1, keepdims=True) for one in raw)
        mixed = sum(
            jnp.dot(one.astype(jnp.bfloat16), piece[1][head], preferred_element_type=jnp.float32)
            for one, piece in zip(raw, pieces)
        )
        if old is None:
            new.append((mixed, new_top, jnp.broadcast_to(added, new_top.shape)))
        else:
            factor = jnp.exp(old_top - new_top)
            new.append((old_acc * factor + mixed, new_top, old_total * factor + added))
    return new


def held(row, state):
    return [tuple(one[row, head] for one in state) for head in range(KVH)]


def hold(row, state, new):
    for head in range(KVH):
        for one, value in zip(state, new[head]):
            one[row, head] = value


def row_queries(row, q_ref):
    return [q_ref[row, head] for head in range(KVH)]


def resident_kernel(
    lens, q_ref, step_k, step_v, keys, values, acc, top, total, kbuf, vbuf, sems
):
    rows, slot_count = kbuf.shape[0], kbuf.shape[1]
    piece = min(CHUNK, slot_count)
    pieces = slot_count // piece
    steps = step_k.shape[1]
    width = q_ref.shape[2]
    group = width // steps

    def copies(r, i):
        part = pl.ds(i * piece, piece)
        return (
            pltpu.make_async_copy(keys.at[r, part], kbuf.at[r, part], sems.at[0, r, i]),
            pltpu.make_async_copy(values.at[r, part], vbuf.at[r, part], sems.at[1, r, i]),
        )

    def fetch(r, _):
        for i in range(pieces):

            @pl.when((i == 0) | (i * piece < lens[r]))
            def _():
                for copy in copies(r, i):
                    copy.start()

        return 0

    lax.fori_loop(0, rows, fetch, 0)
    lane = lax.broadcasted_iota(jnp.int32, (width, piece), 1)
    causal = (
        lax.broadcasted_iota(jnp.int32, (width, steps), 1)
        <= lax.broadcasted_iota(jnp.int32, (width, steps), 0) // group
    )

    def one_row(r, _):
        def part(i):
            span = pl.ds(i * piece, piece)
            return (
                [kbuf[r, span, head * HD : (head + 1) * HD] for head in range(KVH)],
                [vbuf[r, span, head * HD : (head + 1) * HD] for head in range(KVH)],
                lane + i * piece < lens[r],
            )

        own = (
            [step_k[r, :, head * HD : (head + 1) * HD] for head in range(KVH)],
            [step_v[r, :, head * HD : (head + 1) * HD] for head in range(KVH)],
            causal,
        )
        state = (acc, top, total)
        for copy in copies(r, 0):
            copy.wait()
        hold(r, state, blend(row_queries(r, q_ref), [own, part(0)], None))
        for i in range(1, pieces):

            @pl.when(i * piece < lens[r])
            def _():
                for copy in copies(r, i):
                    copy.wait()
                hold(r, state, blend(row_queries(r, q_ref), [part(i)], held(r, state)))

        return 0

    lax.fori_loop(0, rows, one_row, 0)


def state_shapes(rows, width):
    shape = jax.ShapeDtypeStruct((rows, KVH, width, HD), jnp.float32)
    return (shape,) * 3


def resident(lens, grouped, step_k, step_v, keys, values):
    rows, slot_count, feature = keys.shape
    pieces = slot_count // min(CHUNK, slot_count)
    vmem = pl.BlockSpec(memory_space=pltpu.VMEM)
    hbm = pl.BlockSpec(memory_space=pltpu.HBM)
    return pl.pallas_call(
        resident_kernel,
        out_shape=state_shapes(rows, grouped.shape[2]),
        in_specs=[pl.BlockSpec(memory_space=pltpu.SMEM), vmem, vmem, vmem, hbm, hbm],
        out_specs=(vmem,) * 3,
        scratch_shapes=[
            pltpu.VMEM((rows, slot_count, feature), jnp.bfloat16),
            pltpu.VMEM((rows, slot_count, feature), jnp.bfloat16),
            pltpu.SemaphoreType.DMA((2, rows, pieces)),
        ],
        compiler_params=pltpu.CompilerParams(vmem_limit_bytes=WIDE),
        cost_estimate=pl.CostEstimate(
            flops=2 * 10**9, bytes_accessed=16 * 2**20, transcendentals=10**6
        ),
        name="resident",
    )(lens, grouped, step_k, step_v, keys, values)


def span_kernel(
    kind, kernel, first, count, cap, mine, place_of, row_of, rank_of, used, tally, lens,
    q_ref, ca, sa, cb, sb, *refs,
):
    messages = refs[:count]
    refs = refs[count:]
    before = refs[:3]
    if kind == "partial":
        out, stats, acc, top, total, kbuf, vbuf = refs
    elif kind == "state":
        acc, top, total, kbuf, vbuf = refs[3:]
    else:
        part, stats, out_all, acc, top, total, scr, out, sems, kbuf, vbuf = refs[3:]
    state = (acc, top, total)
    rows = q_ref.shape[0]
    width = q_ref.shape[2]
    feature = kbuf.shape[1]
    last = tally[kernel, rows - 1] * BLK + tally[8 + kernel, rows - 1]
    tail = pl.ds(pl.multiple_of(last, BLK), SPAN)
    vbuf[tail, :] = jnp.zeros((SPAN, feature), jnp.float32)
    unroll = min(UNROLL, cap)
    for j in range(count):

        @pl.when(mine[1, first + j] == kernel)
        def _():
            source = mine[0, first + j]
            message = messages[j]

            def place(step, _):
                ready = []
                for u in range(unroll):
                    k = step * unroll + u
                    r = row_of[source, k]
                    rank = rank_of[source, k]
                    length = tally[3, r] if kind == "partial" else lens[r]
                    fine = pl.ds(length & (BLK - 1), BLK)
                    coarse = pl.ds(lax.shift_right_logical(length, BLK.bit_length() - 1) + rank, 1)
                    c_a, s_a = ca[fine, :], sa[fine, :]
                    c_b, s_b = cb[coarse, :], sb[coarse, :]
                    cosine = c_a * c_b - s_a * s_b
                    sine = s_a * c_b + c_a * s_b
                    where = pl.ds(pl.multiple_of(place_of[source, k], BLK), BLK)
                    value = message[1, k].astype(jnp.float32)
                    key = message[0, k].astype(jnp.float32)
                    turned = []
                    for head in range(KVH):
                        piece = key[:, head * HD : (head + 1) * HD]
                        turned.append(piece * cosine + pltpu.roll(piece, HD // 2, 1) * sine)
                    ready.append((where, turned, value))
                for where, turned, value in ready:
                    vbuf[where, :] = value
                    for head in range(KVH):
                        kbuf[where, head * HD : (head + 1) * HD] = turned[head]
                return 0

            lax.fori_loop(0, (used[source, 0] + unroll - 1) // unroll, place, 0)

    lane = lax.broadcasted_iota(jnp.int32, (width, SPAN), 1)
    eye = lax.broadcasted_iota(jnp.int32, (width, width), 0) == lax.broadcasted_iota(
        jnp.int32, (width, width), 1
    )

    def block(r, i):
        where = pl.ds(pl.multiple_of(tally[kernel, r] * BLK + i * SPAN, BLK), SPAN)
        return (
            [kbuf[where, h * HD : (h + 1) * HD].astype(jnp.bfloat16) for h in range(KVH)],
            [vbuf[where, h * HD : (h + 1) * HD].astype(jnp.bfloat16) for h in range(KVH)],
            lane + i * SPAN < tally[8 + kernel, r],
        )

    def beyond(r):
        def piece(i, _):
            hold(r, state, blend(row_queries(r, q_ref), [block(r, i)], held(r, state)))
            return 0

        lax.fori_loop(1, (tally[8 + kernel, r] + SPAN - 1) // SPAN, piece, 0)

    def partial_rows(pair):
        new = [blend(row_queries(r, q_ref), [block(r, 0)], None, guard=True) for r in pair]
        for r, one in zip(pair, new):
            hold(r, state, one)
        for r in pair:
            beyond(r)
        done = []
        for r in pair:
            for head in range(KVH):
                amount = total[r, head]
                safe = jnp.where(amount > 0.0, amount, 1.0)
                lines = [
                    jnp.sum(jnp.where(eye, one[:, :width], 0.0), axis=0, keepdims=True)
                    for one in (top[r, head], amount)
                ]
                done.append((r, head, (acc[r, head] / safe).astype(jnp.bfloat16), lines))
        for r, head, value, lines in done:
            out[r, head] = value
            for i in range(2):
                stats[r, head, pl.ds(i, 1), :] = lines[i]

    def with_part(r, new):
        merged = []
        for head in range(KVH):
            lines = []
            for i in range(2):
                line = jnp.broadcast_to(stats[r, head, pl.ds(i, 1), :], (width, width))
                lines.append(jnp.sum(jnp.where(eye, line, 0.0), axis=1, keepdims=True))
            other_top, other_total = lines
            other_top = jnp.where(other_total > 0.0, other_top, NEG)
            value, old_top, amount = new[head]
            new_top = jnp.maximum(old_top, other_top)
            mine = jnp.exp(old_top - new_top)
            theirs = jnp.exp(other_top - new_top) * other_total
            merged.append(
                (
                    value * mine + part[r, head].astype(jnp.float32) * theirs,
                    new_top,
                    amount * mine + theirs,
                )
            )
        return merged

    def state_rows(pair):
        new = [blend(row_queries(r, q_ref), [block(r, 0)], held(r, before)) for r in pair]
        for r, one in zip(pair, new):
            hold(r, state, one)
        for r in pair:
            beyond(r)

    def put_out(pair, new):
        done = [value / amount for one in new for value, _, amount in one]
        for i, value in enumerate(done):
            scr[i] = value
        steps = out.shape[1]
        group = width // steps
        for i, r in enumerate(pair):
            for head in range(KVH):
                for g in range(group):
                    column = (head * group + g) * HD
                    out[r, :, column : column + HD] = scr[
                        i * KVH + head, pl.ds(g, steps, stride=group), :
                    ].astype(jnp.bfloat16)

    def final_rows(pair):
        new = [blend(row_queries(r, q_ref), [block(r, 0)], held(r, before)) for r in pair]
        new = [with_part(r, one) for r, one in zip(pair, new)]
        put_out(pair, new)
        longest = functools.reduce(jnp.maximum, [tally[8 + kernel, r] for r in pair])

        @pl.when(longest > SPAN)
        def _():
            for r, one in zip(pair, new):
                hold(r, state, one)
            for r in pair:
                beyond(r)
            put_out(pair, [held(r, state) for r in pair])

        for r in pair:
            write(r).start()

    def write(r):
        return pltpu.make_async_copy(out.at[r], out_all.at[r], sems.at[r])

    run = {"partial": partial_rows, "state": state_rows, "final": final_rows}[kind]
    together = 2 if rows % 2 == 0 else 1

    def some_rows(i, _):
        run([i * together + u for u in range(together)])
        return 0

    lax.fori_loop(0, rows // together, some_rows, 0)
    if kind == "final":
        for r in range(rows):
            write(r).wait()


def span(kind, kernel, first, cap, scalars, grouped, tables, messages, state, extra, steps):
    rows, _, width, _ = grouped.shape
    feature = messages[0].shape[-1]
    count = len(messages)
    room = (count * cap + 1) * BLK + SPAN
    smem = pl.BlockSpec(memory_space=pltpu.SMEM)
    vmem = pl.BlockSpec(memory_space=pltpu.VMEM)
    running = [pltpu.VMEM((rows, KVH, width, HD), jnp.float32)] * 3
    scratch = []
    if kind == "partial":
        out_shape = (
            jax.ShapeDtypeStruct((rows, KVH, width, HD), jnp.bfloat16),
            jax.ShapeDtypeStruct((rows, KVH, 2, width), jnp.float32),
        )
        scratch += running
    elif kind == "state":
        out_shape = state_shapes(rows, width)
    else:
        out_shape = jax.ShapeDtypeStruct((rows, steps, QH * HD), jnp.bfloat16)
        scratch += running + [
            pltpu.VMEM((2 * KVH, width, HD), jnp.float32),
            pltpu.VMEM((rows, steps, QH * HD), jnp.bfloat16),
            pltpu.SemaphoreType.DMA((rows,)),
        ]
    scratch += [pltpu.VMEM((room, feature), jnp.float32)] * 2
    return pl.pallas_call(
        functools.partial(span_kernel, kind, kernel, first, count, cap),
        out_shape=out_shape,
        in_specs=[smem] * 7 + [vmem] * (5 + count + len(state) + len(extra)),
        out_specs=pl.BlockSpec(memory_space=pltpu.HBM)
        if kind == "final"
        else jax.tree.map(lambda _: vmem, out_shape),
        scratch_shapes=scratch,
        compiler_params=pltpu.CompilerParams(vmem_limit_bytes=GRANT),
        cost_estimate=pl.CostEstimate(
            flops=10**9, bytes_accessed=12 * 2**20, transcendentals=10**6
        ),
    )(*scalars, grouped, *tables, *messages, *state, *extra)


PHASES = {"d": (2, 2, 2, 2), "f": (0, 3, 3, 0), "g": (3, 0, 0, 3), "b": (1, 1, 1, 1)}


def site_plane(plane, flip):
    dest = plane ^ flip
    half = PLANES // 2
    if (plane < half) != (dest < half) and dest in (half - 1, half):
        return PLANES - 1 - dest
    return dest


def came_from(phase, plane):
    flips = PHASES[phase]
    return next(s for s in range(PLANES) if site_plane(s, flips[s]) == plane)


def for_mirror(phase, plane):
    source = came_from(phase, plane)
    return int(source ^ PHASES[phase][source] != plane)


def route(n, phase, offset):
    in_plane = n // PLANES
    return [
        (
            plane * in_plane + place,
            site_plane(plane, flip) * in_plane + (place + offset) % in_plane,
        )
        for plane, flip in enumerate(PHASES[phase])
        for place in range(in_plane)
    ]


STAGE = {"d": 1, "f": 1, "g": 1, "b": 2}


def device_tables(n):
    in_plane = n // PLANES
    lines = []
    for me in range(n):
        plane, place = me // in_plane, me % in_plane
        entry, stage = [], []
        post = [[-1] * n, [-1] * n]
        for phase in PHASES:
            mirror = for_mirror(phase, plane)
            for offset in range(in_plane):
                source = came_from(phase, plane) * in_plane + (place - offset) % in_plane
                entry.append(mirror * n + source)
                stage.append(0 if mirror else STAGE[phase])
                post[mirror][source] = stage[-1]
        lines.append((entry, stage, post[0], post[1]))
    return np.array(lines, np.int32)


def body(
    span_keys,
    span_values,
    block_device,
    block_row,
    cache_len,
    cache_keys,
    cache_values,
    queries,
    step_keys,
    step_values,
):
    n = lax.axis_size("seq")
    in_plane = n // PLANES
    me = lax.axis_index("seq").astype(jnp.int32)
    rows = cache_len.shape[0]
    feature = span_keys.shape[1]
    blocks = span_keys.shape[0] // BLK
    cap = max(2, (2 * blocks + n - 1) // n)
    steps = queries.shape[1]
    group = QH // KVH
    names = list(PHASES)

    phase_table = jnp.array(
        [
            [next(i for i, p in enumerate(names) if PHASES[p][z] == z ^ d) for d in range(PLANES)]
            for z in range(PLANES)
        ],
        jnp.int32,
    )
    half = PLANES // 2
    swap = [
        (a * in_plane + i, b * in_plane + i)
        for a, b in ((half - 1, half), (half, half - 1))
        for i in range(in_plane)
    ]
    mirrored = lax.ppermute(queries, "seq", swap)
    messages = pack(
        n,
        cap,
        phase_table,
        block_device[:, 0],
        span_keys.reshape(blocks, BLK, feature),
        span_values.reshape(blocks, BLK, feature),
    )
    packed = {p: messages[i * in_plane : (i + 1) * in_plane] for i, p in enumerate(names)}

    def send(phase):
        out = []
        for offset in range(in_plane):
            value = packed[phase][offset]
            pairs = route(n, phase, offset)
            if any(a != b for a, b in pairs):
                value = lax.ppermute(value, "seq", pairs)
            out.append(value)
        return out

    got = {phase: send(phase) for phase in names}

    def regroup(value):
        value = value.reshape(rows, steps, KVH, group, HD).transpose(0, 2, 1, 3, 4)
        return value.reshape(rows, KVH, steps * group, HD)

    queries, mirrored = lax.optimization_barrier((queries, mirrored))
    grouped, mirrored = regroup(queries), regroup(mirrored)
    state = resident(cache_len, grouped, step_keys, step_values, cache_keys, cache_values)

    notes = note(n, block_device[:, 0], block_row, cache_len)
    notes = lax.all_to_all(notes, "seq", split_axis=0, concat_axis=0, tiled=True)
    mine = lax.dynamic_index_in_dim(jnp.array(device_tables(n)), me, 0, keepdims=False)
    *slots, tally = index(n, cap, rows, notes, mine)
    reach = cache_keys.shape[1] // BLK + n * cap + 1
    tables = turn_tables(np.arange(2 * BLK)) + turn_tables(np.arange(reach) * BLK)
    scalars = (mine, *slots, tally, cache_len)

    partial, stats = span(
        "partial", 0, 0, cap, scalars, mirrored, tables,
        got["d"] + got["f"], (), (), steps,
    )
    partial = lax.ppermute(partial, "seq", swap)
    stats = lax.ppermute(stats, "seq", swap)
    state = span(
        "state", 1, 0, cap, scalars, grouped, tables,
        got["d"] + got["f"] + got["g"], tuple(state), (), steps,
    )
    return span(
        "final", 2, 3 * in_plane, cap, scalars, grouped, tables,
        got["b"], tuple(state), (partial, stats), steps,
    )


def solution(mesh):
    placed = (
        P(("groups", "seq"), None),
        P(("groups", "seq"), None),
        P(("groups", "seq"), None),
        P(("groups", "seq")),
        P(("groups", "seq")),
        P(("groups", "seq"), None, None),
        P(("groups", "seq"), None, None),
        P(("groups", "seq"), None, None),
        P(("groups", "seq"), None, None),
        P(("groups", "seq"), None, None),
    )

    return jax.shard_map(
        body,
        mesh=mesh,
        in_specs=placed,
        out_specs=P(("groups", "seq"), None, None),
        check_vma=False,
    )
```

```python
import functools

import jax
import jax.numpy as jnp
import numpy as np
from jax import lax
from jax.experimental import pallas as pl
from jax.experimental.pallas import tpu as pltpu
from jax.sharding import PartitionSpec as P


KVH = 4
QH = 64
HD = 128
BLK = 8
PLANES = 4
CHUNK = 256
SPAN = 128
LANES = 128
GRANT = 20 * 2**20
WIDE = 52 * 2**20
UNROLL = 4
PACKED = 4
NEG = -1e30


def frequencies(half_width):
    index = np.arange(half_width, dtype=np.float64)
    base = 1.0 / 500000.0 ** (index / half_width)
    wavelen = 2.0 * np.pi / base
    smooth = (8192.0 / wavelen - 1.0) / 3.0
    blended = (1.0 - smooth) * base / 8.0 + smooth * base
    scaled = np.where(wavelen > 8192.0, base / 8.0, blended)
    return np.where(wavelen < 2048.0, base, scaled)


def turn_tables(positions):
    freq = frequencies(HD // 2)
    angles = np.asarray(positions, np.float64)[:, None] * np.concatenate([freq, freq])[None]
    sign = np.where(np.arange(HD) < HD // 2, -1.0, 1.0)
    return jnp.array(np.cos(angles), jnp.float32), jnp.array(np.sin(angles) * sign, jnp.float32)


def pack_kernel(n, phase_table, target, keys, values, *refs):
    outs = refs[:n]
    slots, fill, rel, sems = refs[n:]
    blocks = keys.shape[0]
    in_plane = n // PLANES
    me = lax.axis_index("seq")
    plane, place = me // in_plane, me % in_plane

    def clear(p, _):
        for i in range(in_plane):
            fill[p * in_plane + i] = 0
            offset = i - place
            offset = jnp.where(offset < 0, offset + in_plane, offset)
            rel[p * in_plane + i] = phase_table[plane, p] * in_plane + offset
        return 0

    lax.fori_loop(0, PLANES, clear, 0)

    def put(step, _):
        ready = []
        for u in range(PACKED):
            b = step * PACKED + u
            dest = target[b]
            slot = fill[dest]
            fill[dest] = slot + 1
            ready.append((b, rel[dest], slot))
        for b, message, slot in ready:
            slots[message, 0, slot] = keys[b]
            slots[message, 1, slot] = values[b]
        return 0

    lax.fori_loop(0, blocks // PACKED, put, 0)
    copies = [pltpu.make_async_copy(slots.at[i], outs[i], sems.at[i]) for i in range(n)]
    for copy in copies:
        copy.start()
    for copy in copies:
        copy.wait()


def pack(n, cap, phase_table, target, keys, values):
    width = keys.shape[-1]
    message = jax.ShapeDtypeStruct((2, cap, BLK, width), jnp.bfloat16)
    smem = pl.BlockSpec(memory_space=pltpu.SMEM)
    vmem = pl.BlockSpec(memory_space=pltpu.VMEM)
    return pl.pallas_call(
        functools.partial(pack_kernel, n),
        out_shape=(message,) * n,
        in_specs=[smem] * 2 + [vmem] * 2,
        out_specs=(pl.BlockSpec(memory_space=pl.ANY),) * n,
        scratch_shapes=[
            pltpu.VMEM((n, 2, cap, BLK, width), jnp.bfloat16),
            pltpu.SMEM((n,), jnp.int32),
            pltpu.SMEM((n,), jnp.int32),
            pltpu.SemaphoreType.DMA((n,)),
        ],
        name="pack",
    )(phase_table, target, keys, values)


def twin_index(in_plane, index):
    plane = index // in_plane
    inner = (plane > 0) & (plane < PLANES - 1)
    return jnp.where(inner, (PLANES - 1 - 2 * plane) * in_plane + index, index)


def note_kernel(n, target, rows, lens, notes, fill, twins):
    in_plane = n // PLANES

    def clear(i, _):
        fill[i] = 0
        twins[i] = twin_index(in_plane, i)
        return 0

    lax.fori_loop(0, n, clear, 0, unroll=min(n, 16))
    my_twin = twins[lax.axis_index("seq")]
    for k in range(lens.shape[0]):
        notes[my_twin, 0, 2 * LANES + k] = lens[k]

    def put(step, _):
        ready = []
        for u in range(PACKED):
            b = step * PACKED + u
            dest = target[b]
            slot = fill[dest]
            fill[dest] = slot + 1
            ready.append((dest, twins[dest], slot, rows[b]))
        for dest, twin, slot, row in ready:
            notes[dest, 0, slot] = row
            notes[twin, 0, LANES + slot] = row
        return 0

    lax.fori_loop(0, rows.shape[0] // PACKED, put, 0)

    def close(i, _):
        notes[i, 0, LANES - 1] = fill[i]
        notes[twins[i], 0, 2 * LANES - 1] = fill[i]
        return 0

    lax.fori_loop(0, n, close, 0, unroll=min(n, 4))


def note(n, target, rows, lens):
    smem = pl.BlockSpec(memory_space=pltpu.SMEM)
    return pl.pallas_call(
        functools.partial(note_kernel, n),
        out_shape=jax.ShapeDtypeStruct((n, 1, 3 * LANES), jnp.int32),
        in_specs=[smem] * 3,
        out_specs=smem,
        scratch_shapes=[pltpu.SMEM((n,), jnp.int32), pltpu.SMEM((n,), jnp.int32)],
        name="note",
    )(target, rows, lens)


def index_kernel(n, cap, rows, notes, stages, place, row_of, rank_of, used, tally):
    f32 = jnp.float32

    def iotas(shape):
        return [lax.broadcasted_iota(jnp.int32, shape, d) for d in (0, 1)]

    a, b = iotas((cap, cap))
    before = (a < b).astype(f32)
    a, b = iotas((n, n))
    sooner = (b < a).astype(f32)
    lines = [jnp.broadcast_to(stages[i : i + 1, :n], (n, n)) for i in (2, 3)]
    posts = [
        jnp.sum(jnp.where(a == b, line, 0), axis=1, keepdims=True) for line in lines
    ]
    mates = [jnp.where(line == post, sooner, 0.0) for line, post in zip(lines, posts)]
    kernel, lane = iotas((8, LANES))
    counts = jnp.zeros((8, LANES), f32)
    locals_ = []
    for side in range(2):
        there = notes[:, 0, side * LANES : (side + 1) * LANES]
        valid = lax.broadcasted_iota(jnp.int32, (n, cap), 1) < there[:, LANES - 1 :]
        rows_here = jnp.where(valid, there[:, :cap], -1)
        rank = jnp.zeros((n, cap), f32)
        local = jnp.zeros((n, cap), f32)
        for r in range(rows):
            hit = (rows_here == r).astype(f32)
            inside = jnp.dot(hit, before, preferred_element_type=f32)
            ahead = jnp.dot(sooner, hit, preferred_element_type=f32)
            near = jnp.dot(mates[side], hit, preferred_element_type=f32)
            rank += hit * (inside + jnp.sum(ahead, axis=1, keepdims=True))
            local += hit * (inside + jnp.sum(near, axis=1, keepdims=True))
            per_source = jnp.sum(hit, axis=1, keepdims=True)
            for stage in range(3):
                if (stage == 0) == (side == 1):
                    number = jnp.sum(
                        jnp.where(posts[side] == stage, per_source, 0.0), axis=0, keepdims=True
                    )
                    counts += jnp.where((kernel == stage) & (lane == r), number, 0.0)
        span = slice(side * n, side * n + n)
        locals_.append((span, valid, rows_here, local))
        row_of[span, :] = jnp.maximum(rows_here, 0)
        rank_of[span, :] = rank.astype(jnp.int32)
        filled = jnp.sum(valid.astype(f32), axis=1, keepdims=True)
        used[span, :] = jnp.broadcast_to(filled, (n, cap)).astype(jnp.int32)
    a, b = iotas((LANES, LANES))
    begin = jnp.dot(counts, (a < b).astype(f32), preferred_element_type=f32)
    in_plane = n // PLANES
    messages = {0: 2 * in_plane, 1: 3 * in_plane, 2: in_plane}
    for side, (span, valid, rows_here, local) in enumerate(locals_):
        unfilled = jnp.zeros((n, 1), f32)
        for stage in range(3):
            if (stage == 0) != (side == 1):
                continue
            mine = posts[side] == stage
            unfilled += jnp.where(mine, float(messages[stage] * cap + SPAN // BLK), 0.0)
            for r in range(rows):
                here = jnp.where(mine, begin[stage : stage + 1, r : r + 1], 0.0)
                local += jnp.where(rows_here == r, here, 0.0)
        place[span, :] = (jnp.where(valid, local, unfilled) * BLK).astype(jnp.int32)
    twin = twin_index(in_plane, lax.axis_index("seq"))
    source = lax.broadcasted_iota(jnp.int32, (n, LANES), 0)
    lens = jnp.sum(
        jnp.where(source == twin, notes[:, 0, 2 * LANES :], 0), axis=0, keepdims=True
    )
    tally[0:8, :] = jnp.where(kernel == 3, lens, begin.astype(jnp.int32))
    tally[8:16, :] = (counts * BLK).astype(jnp.int32)


def index(n, cap, rows, notes, stages):
    vmem = pl.BlockSpec(memory_space=pltpu.VMEM)
    slots = jax.ShapeDtypeStruct((2 * n, cap), jnp.int32)
    return pl.pallas_call(
        functools.partial(index_kernel, n, cap, rows),
        out_shape=(slots,) * 4 + (jax.ShapeDtypeStruct((16, LANES), jnp.int32),),
        in_specs=[vmem] * 2,
        out_specs=(vmem,) * 5,
        compiler_params=pltpu.CompilerParams(vmem_limit_bytes=GRANT),
        name="index",
    )(notes, stages)


def as_wide(line, width):
    if width % HD == 0:
        return jnp.concatenate([line] * (width // HD), axis=1)
    return line[:, :width]


def blend(queries, pieces, old, guard=False):
    scale = HD ** (-0.5)
    heads = range(KVH)
    scores = [
        [
            jnp.where(
                piece[2],
                lax.dot_general(
                    queries[head],
                    piece[0][head],
                    (((1,), (1,)), ((), ())),
                    preferred_element_type=jnp.float32,
                )
                * scale,
                NEG,
            )
            for piece in pieces
        ]
        for head in heads
    ]
    new = []
    for head in heads:
        peak = functools.reduce(
            jnp.maximum, [jnp.max(one, axis=-1, keepdims=True) for one in scores[head]]
        )
        if old is None:
            new_top = jnp.broadcast_to(peak, (peak.shape[0], HD))
        else:
            old_acc, old_top, old_total = old[head]
            new_top = jnp.maximum(old_top, peak)
        raw = [jnp.exp(one - as_wide(new_top, one.shape[1])) for one in scores[head]]
        if guard:
            raw = [jnp.where(piece[2], one, 0.0) for piece, one in zip(pieces, raw)]
        added = sum(jnp.sum(one, axis=-1, keepdims=True) for one in raw)
        mixed = sum(
            jnp.dot(one.astype(jnp.bfloat16), piece[1][head], preferred_element_type=jnp.float32)
            for one, piece in zip(raw, pieces)
        )
        if old is None:
            new.append((mixed, new_top, jnp.broadcast_to(added, new_top.shape)))
        else:
            factor = jnp.exp(old_top - new_top)
            new.append((old_acc * factor + mixed, new_top, old_total * factor + added))
    return new


def held(row, state):
    return [tuple(one[row, head] for one in state) for head in range(KVH)]


def hold(row, state, new):
    for head in range(KVH):
        for one, value in zip(state, new[head]):
            one[row, head] = value


def row_queries(row, q_ref):
    return [q_ref[row, head] for head in range(KVH)]


def resident_kernel(
    lens, q_ref, step_k, step_v, keys, values, acc, top, total, kbuf, vbuf, sems
):
    rows, slot_count = kbuf.shape[0], kbuf.shape[1]
    piece = min(CHUNK, slot_count)
    pieces = slot_count // piece
    steps = step_k.shape[1]
    width = q_ref.shape[2]

    def copies(r, i):
        part = pl.ds(i * piece, piece)
        return (
            pltpu.make_async_copy(keys.at[r, part], kbuf.at[r, part], sems.at[0, r, i]),
            pltpu.make_async_copy(values.at[r, part], vbuf.at[r, part], sems.at[1, r, i]),
        )

    def fetch(r, _):
        for i in range(pieces):

            @pl.when((i == 0) | (i * piece < lens[r]))
            def _():
                for copy in copies(r, i):
                    copy.start()

        return 0

    lax.fori_loop(0, rows, fetch, 0)
    lane = lax.broadcasted_iota(jnp.int32, (width, piece), 1)
    causal = (
        lax.broadcasted_iota(jnp.int32, (width, steps), 1)
        <= lax.rem(lax.broadcasted_iota(jnp.int32, (width, steps), 0), steps)
    )

    def one_row(r, _):
        def part(i):
            span = pl.ds(i * piece, piece)
            return (
                [kbuf[r, span, head * HD : (head + 1) * HD] for head in range(KVH)],
                [vbuf[r, span, head * HD : (head + 1) * HD] for head in range(KVH)],
                lane + i * piece < lens[r],
            )

        own = (
            [step_k[r, :, head * HD : (head + 1) * HD] for head in range(KVH)],
            [step_v[r, :, head * HD : (head + 1) * HD] for head in range(KVH)],
            causal,
        )
        state = (acc, top, total)
        for copy in copies(r, 0):
            copy.wait()
        hold(r, state, blend(row_queries(r, q_ref), [own, part(0)], None))
        for i in range(1, pieces):

            @pl.when(i * piece < lens[r])
            def _():
                for copy in copies(r, i):
                    copy.wait()
                hold(r, state, blend(row_queries(r, q_ref), [part(i)], held(r, state)))

        return 0

    lax.fori_loop(0, rows, one_row, 0)


def state_shapes(rows, width):
    shape = jax.ShapeDtypeStruct((rows, KVH, width, HD), jnp.float32)
    return (shape,) * 3


def resident(lens, grouped, step_k, step_v, keys, values):
    rows, slot_count, feature = keys.shape
    pieces = slot_count // min(CHUNK, slot_count)
    vmem = pl.BlockSpec(memory_space=pltpu.VMEM)
    hbm = pl.BlockSpec(memory_space=pltpu.HBM)
    return pl.pallas_call(
        resident_kernel,
        out_shape=state_shapes(rows, grouped.shape[2]),
        in_specs=[pl.BlockSpec(memory_space=pltpu.SMEM), vmem, vmem, vmem, hbm, hbm],
        out_specs=(vmem,) * 3,
        scratch_shapes=[
            pltpu.VMEM((rows, slot_count, feature), jnp.bfloat16),
            pltpu.VMEM((rows, slot_count, feature), jnp.bfloat16),
            pltpu.SemaphoreType.DMA((2, rows, pieces)),
        ],
        compiler_params=pltpu.CompilerParams(vmem_limit_bytes=WIDE),
        cost_estimate=pl.CostEstimate(
            flops=2 * 10**9, bytes_accessed=16 * 2**20, transcendentals=10**6
        ),
        name="resident",
    )(lens, grouped, step_k, step_v, keys, values)


def span_kernel(
    kind, kernel, first, count, cap, mine, place_of, row_of, rank_of, used, tally, lens,
    q_ref, ca, sa, cb, sb, *refs,
):
    messages = refs[:count]
    refs = refs[count:]
    before = refs[:3]
    if kind == "partial":
        out, stats, acc, top, total, kbuf, vbuf = refs
    elif kind == "state":
        acc, top, total, kbuf, vbuf = refs[3:]
    else:
        part, stats, out_all, acc, top, total, _, out, sems, kbuf, vbuf = refs[3:]
    state = (acc, top, total)
    rows = q_ref.shape[0]
    width = q_ref.shape[2]
    feature = kbuf.shape[1]
    last = tally[kernel, rows - 1] * BLK + tally[8 + kernel, rows - 1]
    tail = pl.ds(pl.multiple_of(last, BLK), SPAN)
    vbuf[tail, :] = jnp.zeros((SPAN, feature), jnp.float32)
    unroll = min(UNROLL, cap)
    for j in range(count):

        @pl.when(mine[1, first + j] == kernel)
        def _():
            source = mine[0, first + j]
            message = messages[j]

            def place(step, _):
                ready = []
                for u in range(unroll):
                    k = step * unroll + u
                    r = row_of[source, k]
                    rank = rank_of[source, k]
                    length = tally[3, r] if kind == "partial" else lens[r]
                    fine = pl.ds(length & (BLK - 1), BLK)
                    coarse = pl.ds(lax.shift_right_logical(length, BLK.bit_length() - 1) + rank, 1)
                    c_a, s_a = ca[fine, :], sa[fine, :]
                    c_b, s_b = cb[coarse, :], sb[coarse, :]
                    cosine = c_a * c_b - s_a * s_b
                    sine = s_a * c_b + c_a * s_b
                    where = pl.ds(pl.multiple_of(place_of[source, k], BLK), BLK)
                    value = message[1, k].astype(jnp.float32)
                    key = message[0, k].astype(jnp.float32)
                    turned = []
                    for head in range(KVH):
                        piece = key[:, head * HD : (head + 1) * HD]
                        turned.append(piece * cosine + pltpu.roll(piece, HD // 2, 1) * sine)
                    ready.append((where, turned, value))
                for where, turned, value in ready:
                    vbuf[where, :] = value
                    for head in range(KVH):
                        kbuf[where, head * HD : (head + 1) * HD] = turned[head]
                return 0

            lax.fori_loop(0, (used[source, 0] + unroll - 1) // unroll, place, 0)

    lane = lax.broadcasted_iota(jnp.int32, (width, SPAN), 1)
    eye = lax.broadcasted_iota(jnp.int32, (width, width), 0) == lax.broadcasted_iota(
        jnp.int32, (width, width), 1
    )

    def block(r, i):
        where = pl.ds(pl.multiple_of(tally[kernel, r] * BLK + i * SPAN, BLK), SPAN)
        return (
            [kbuf[where, h * HD : (h + 1) * HD].astype(jnp.bfloat16) for h in range(KVH)],
            [vbuf[where, h * HD : (h + 1) * HD].astype(jnp.bfloat16) for h in range(KVH)],
            lane + i * SPAN < tally[8 + kernel, r],
        )

    def beyond(r):
        def piece(i, _):
            hold(r, state, blend(row_queries(r, q_ref), [block(r, i)], held(r, state)))
            return 0

        lax.fori_loop(1, (tally[8 + kernel, r] + SPAN - 1) // SPAN, piece, 0)

    def partial_rows(pair):
        new = [blend(row_queries(r, q_ref), [block(r, 0)], None, guard=True) for r in pair]
        for r, one in zip(pair, new):
            hold(r, state, one)
        for r in pair:
            beyond(r)
        done = []
        for r in pair:
            for head in range(KVH):
                amount = total[r, head]
                safe = jnp.where(amount > 0.0, amount, 1.0)
                lines = [
                    jnp.sum(jnp.where(eye, one[:, :width], 0.0), axis=0, keepdims=True)
                    for one in (top[r, head], amount)
                ]
                done.append((r, head, (acc[r, head] / safe).astype(jnp.bfloat16), lines))
        for r, head, value, lines in done:
            out[r, head] = value
            for i in range(2):
                stats[r, head, pl.ds(i, 1), :] = lines[i]

    def with_part(r, new):
        merged = []
        for head in range(KVH):
            lines = []
            for i in range(2):
                line = jnp.broadcast_to(stats[r, head, pl.ds(i, 1), :], (width, width))
                lines.append(jnp.sum(jnp.where(eye, line, 0.0), axis=1, keepdims=True))
            other_top, other_total = lines
            other_top = jnp.where(other_total > 0.0, other_top, NEG)
            value, old_top, amount = new[head]
            new_top = jnp.maximum(old_top, other_top)
            mine = jnp.exp(old_top - new_top)
            theirs = jnp.exp(other_top - new_top) * other_total
            merged.append(
                (
                    value * mine + part[r, head].astype(jnp.float32) * theirs,
                    new_top,
                    amount * mine + theirs,
                )
            )
        return merged

    def state_rows(pair):
        new = [blend(row_queries(r, q_ref), [block(r, 0)], held(r, before)) for r in pair]
        for r, one in zip(pair, new):
            hold(r, state, one)
        for r in pair:
            beyond(r)

    def put_out(pair, new):
        steps = out.shape[1]
        group = width // steps
        for r, one in zip(pair, new):
            for head, (value, _, amount) in enumerate(one):
                done = value / amount
                for g in range(group):
                    column = (head * group + g) * HD
                    out[r, :, column : column + HD] = done[
                        g * steps : (g + 1) * steps, :
                    ].astype(jnp.bfloat16)

    def final_rows(pair):
        new = [blend(row_queries(r, q_ref), [block(r, 0)], held(r, before)) for r in pair]
        new = [with_part(r, one) for r, one in zip(pair, new)]
        put_out(pair, new)
        longest = functools.reduce(jnp.maximum, [tally[8 + kernel, r] for r in pair])

        @pl.when(longest > SPAN)
        def _():
            for r, one in zip(pair, new):
                hold(r, state, one)
            for r in pair:
                beyond(r)
            put_out(pair, [held(r, state) for r in pair])

        for r in pair:
            write(r).start()

    def write(r):
        return pltpu.make_async_copy(out.at[r], out_all.at[r], sems.at[r])

    run = {"partial": partial_rows, "state": state_rows, "final": final_rows}[kind]
    together = 2 if rows % 2 == 0 else 1

    def some_rows(i, _):
        run([i * together + u for u in range(together)])
        return 0

    lax.fori_loop(0, rows // together, some_rows, 0)
    if kind == "final":
        for r in range(rows):
            write(r).wait()


def span(kind, kernel, first, cap, scalars, grouped, tables, messages, state, extra, steps):
    rows, _, width, _ = grouped.shape
    feature = messages[0].shape[-1]
    count = len(messages)
    room = (count * cap + 1) * BLK + SPAN
    smem = pl.BlockSpec(memory_space=pltpu.SMEM)
    vmem = pl.BlockSpec(memory_space=pltpu.VMEM)
    running = [pltpu.VMEM((rows, KVH, width, HD), jnp.float32)] * 3
    scratch = []
    if kind == "partial":
        out_shape = (
            jax.ShapeDtypeStruct((rows, KVH, width, HD), jnp.bfloat16),
            jax.ShapeDtypeStruct((rows, KVH, 2, width), jnp.float32),
        )
        scratch += running
    elif kind == "state":
        out_shape = state_shapes(rows, width)
    else:
        out_shape = jax.ShapeDtypeStruct((rows, steps, QH * HD), jnp.bfloat16)
        scratch += running + [
            pltpu.VMEM((2 * KVH, width, HD), jnp.float32),
            pltpu.VMEM((rows, steps, QH * HD), jnp.bfloat16),
            pltpu.SemaphoreType.DMA((rows,)),
        ]
    scratch += [pltpu.VMEM((room, feature), jnp.float32)] * 2
    return pl.pallas_call(
        functools.partial(span_kernel, kind, kernel, first, count, cap),
        out_shape=out_shape,
        in_specs=[smem] * 7 + [vmem] * (5 + count + len(state) + len(extra)),
        out_specs=pl.BlockSpec(memory_space=pltpu.HBM)
        if kind == "final"
        else jax.tree.map(lambda _: vmem, out_shape),
        scratch_shapes=scratch,
        compiler_params=pltpu.CompilerParams(vmem_limit_bytes=GRANT),
        cost_estimate=pl.CostEstimate(
            flops=10**9, bytes_accessed=12 * 2**20, transcendentals=10**6
        ),
    )(*scalars, grouped, *tables, *messages, *state, *extra)


PHASES = {"d": (2, 2, 2, 2), "f": (0, 3, 3, 0), "g": (3, 0, 0, 3), "b": (1, 1, 1, 1)}


def site_plane(plane, flip):
    dest = plane ^ flip
    half = PLANES // 2
    if (plane < half) != (dest < half) and dest in (half - 1, half):
        return PLANES - 1 - dest
    return dest


def came_from(phase, plane):
    flips = PHASES[phase]
    return next(s for s in range(PLANES) if site_plane(s, flips[s]) == plane)


def for_mirror(phase, plane):
    source = came_from(phase, plane)
    return int(source ^ PHASES[phase][source] != plane)


def route(n, phase, offset):
    in_plane = n // PLANES
    return [
        (
            plane * in_plane + place,
            site_plane(plane, flip) * in_plane + (place + offset) % in_plane,
        )
        for plane, flip in enumerate(PHASES[phase])
        for place in range(in_plane)
    ]


STAGE = {"d": 1, "f": 1, "g": 1, "b": 2}


def device_tables(n):
    in_plane = n // PLANES
    lines = []
    for me in range(n):
        plane, place = me // in_plane, me % in_plane
        entry, stage = [], []
        post = [[-1] * n, [-1] * n]
        for phase in PHASES:
            mirror = for_mirror(phase, plane)
            for offset in range(in_plane):
                source = came_from(phase, plane) * in_plane + (place - offset) % in_plane
                entry.append(mirror * n + source)
                stage.append(0 if mirror else STAGE[phase])
                post[mirror][source] = stage[-1]
        lines.append((entry, stage, post[0], post[1]))
    return np.array(lines, np.int32)


def body(
    span_keys,
    span_values,
    block_device,
    block_row,
    cache_len,
    cache_keys,
    cache_values,
    queries,
    step_keys,
    step_values,
):
    n = lax.axis_size("seq")
    in_plane = n // PLANES
    me = lax.axis_index("seq").astype(jnp.int32)
    rows = cache_len.shape[0]
    feature = span_keys.shape[1]
    blocks = span_keys.shape[0] // BLK
    cap = max(2, (2 * blocks + n - 1) // n)
    steps = queries.shape[1]
    group = QH // KVH
    names = list(PHASES)

    phase_table = jnp.array(
        [
            [next(i for i, p in enumerate(names) if PHASES[p][z] == z ^ d) for d in range(PLANES)]
            for z in range(PLANES)
        ],
        jnp.int32,
    )
    half = PLANES // 2
    swap = [
        (a * in_plane + i, b * in_plane + i)
        for a, b in ((half - 1, half), (half, half - 1))
        for i in range(in_plane)
    ]
    mirrored = lax.ppermute(queries, "seq", swap)
    messages = pack(
        n,
        cap,
        phase_table,
        block_device[:, 0],
        span_keys.reshape(blocks, BLK, feature),
        span_values.reshape(blocks, BLK, feature),
    )
    packed = {p: messages[i * in_plane : (i + 1) * in_plane] for i, p in enumerate(names)}

    def send(phase):
        out = []
        for offset in range(in_plane):
            value = packed[phase][offset]
            pairs = route(n, phase, offset)
            if any(a != b for a, b in pairs):
                value = lax.ppermute(value, "seq", pairs)
            out.append(value)
        return out

    got = {phase: send(phase) for phase in names}

    def regroup(value):
        value = value.reshape(rows, steps, KVH, group, HD).transpose(0, 2, 3, 1, 4)
        return value.reshape(rows, KVH, steps * group, HD)

    queries, mirrored = lax.optimization_barrier((queries, mirrored))
    grouped, mirrored = regroup(queries), regroup(mirrored)
    state = resident(cache_len, grouped, step_keys, step_values, cache_keys, cache_values)

    notes = note(n, block_device[:, 0], block_row, cache_len)
    notes = lax.all_to_all(notes, "seq", split_axis=0, concat_axis=0, tiled=True)
    mine = lax.dynamic_index_in_dim(jnp.array(device_tables(n)), me, 0, keepdims=False)
    *slots, tally = index(n, cap, rows, notes, mine)
    reach = cache_keys.shape[1] // BLK + n * cap + 1
    tables = turn_tables(np.arange(2 * BLK)) + turn_tables(np.arange(reach) * BLK)
    scalars = (mine, *slots, tally, cache_len)

    partial, stats = span(
        "partial", 0, 0, cap, scalars, mirrored, tables,
        got["d"] + got["f"], (), (), steps,
    )
    partial = lax.ppermute(partial, "seq", swap)
    stats = lax.ppermute(stats, "seq", swap)
    state = span(
        "state", 1, 0, cap, scalars, grouped, tables,
        got["d"] + got["f"] + got["g"], tuple(state), (), steps,
    )
    return span(
        "final", 2, 3 * in_plane, cap, scalars, grouped, tables,
        got["b"], tuple(state), (partial, stats), steps,
    )


def solution(mesh):
    placed = (
        P(("groups", "seq"), None),
        P(("groups", "seq"), None),
        P(("groups", "seq"), None),
        P(("groups", "seq")),
        P(("groups", "seq")),
        P(("groups", "seq"), None, None),
        P(("groups", "seq"), None, None),
        P(("groups", "seq"), None, None),
        P(("groups", "seq"), None, None),
        P(("groups", "seq"), None, None),
    )

    return jax.shard_map(
        body,
        mesh=mesh,
        in_specs=placed,
        out_specs=P(("groups", "seq"), None, None),
        check_vma=False,
    )
```
